32 devices in a mesh: groups: 2 (over x), seq: 16 (over z, y, core).
Axes of the slice: x: 2, y: 2, z: 4, core: 2. Of those that a mesh axis runs over, the one named last changes fastest.
Arguments:
- queries: bfloat16 [16384, 2048], P(('groups', 'seq')), parts along dimension 0, may hold values from -8 to 8
- keys: bfloat16 [16384, 512], P(('groups', 'seq')), parts along dimension 0, may hold values from -8 to 8
- values: bfloat16 [16384, 512], P(('groups', 'seq')), parts along dimension 0, may hold values from -6 to 6
- block_table: int32 [128, 8], P(('groups', 'seq')), parts along dimension 0, may hold values from 0 to 63, as said below
- out_weight: bfloat16 [2048, 4096], P('seq'), may hold values from -0.125 to 0.125
Outputs:
- projected: bfloat16 [16384, 4096], P(('groups', 'seq')), parts along dimension 0
The draws below stay inside these ranges and needn't reach their ends.
There are 2 independent parts, one for each index of `groups`. The reference program is written for one: setup_inputs(seed, part) draws one part's arguments, and reference() takes and returns one part's arrays. A program takes and returns all parts, laid end to end along the dimension named above; an argument that names none is the same for every part. Nothing has to cross between parts.
Inputs may be any that keep to these rules, and one draw needn't show every extreme that they name: `block_table`: entry j of the row of query block b names a key block held by index (b // 4 + j * 2 - ((b mod 4) mod 2)) mod 16 of seq, that is a block number s * 4 + r with that index s and 0 <= r < 4.
All inputs are finite; a program needn't handle non-finite values.
Results may differ from the reference program's by a relative error of at most 0.013.
Values may be sent and summed in bfloat16 or wider, within the bound.
No kernel may reach another device: no remote copies, remote signals or barrier semaphores. Data moves between devices by JAX's collectives and lax.ppermute only.
A program may use at most 320 MiB of HBM per device.

```python
import jax
import jax.numpy as jnp
from jax import lax

D = 4096
H = 16
KVH = 4
HD = 128
QB = 128
ENTRIES = 8
TOKENS = 8192
NQB = 64
BPS = 4
STRIDE = 2


def draw_queries(key, part):
    shape = (TOKENS, KVH, H // KVH, HD)
    base = jnp.clip(jax.random.normal(jax.random.fold_in(key, 11), shape, jnp.float32), -6.0, 6.0)
    return base.reshape(TOKENS, H * HD).astype(jnp.bfloat16)


def draw_keys(key, part):
    shape = (TOKENS, KVH, HD)
    base = jnp.clip(jax.random.normal(jax.random.fold_in(key, 13), shape, jnp.float32), -6.0, 6.0)
    return base.reshape(TOKENS, KVH * HD).astype(jnp.bfloat16)


def draw_block_table(key, part):
    shards = NQB // BPS
    rows = jnp.arange(NQB, dtype=jnp.int32)
    entry = jnp.arange(ENTRIES, dtype=jnp.int32)
    lag = rows % BPS % 2
    target = (rows[:, None] // BPS + entry[None, :] * STRIDE - lag[:, None] + shards) % shards
    within = jax.random.randint(jax.random.fold_in(key, 17), (NQB, ENTRIES), 0, BPS, jnp.int32)
    within = within.at[0, 0].set(0).at[NQB - BPS, 0].set(BPS - 1)
    return (target * BPS + within).astype(jnp.int32)


def shard_levels(rng, extent, cuts, smallest, high):
    level, own = 1.0, jax.random.fold_in(rng, 6)
    for dim, blocks in cuts:
        steps = jnp.exp(jax.random.uniform(jax.random.fold_in(own, dim), (blocks,), jnp.float32, smallest / len(cuts), high / len(cuts)))
        level = level * jnp.repeat(steps, extent[dim] // blocks).reshape([-1 if axis == dim else 1 for axis in range(len(extent))])
    return level


def normal_values(rng, extent, width, limit, pieces=(), kind=jnp.bfloat16):
    values = jax.random.normal(rng, extent, jnp.float32) * width
    if len(pieces) > 0:
        values = shard_levels(rng, extent, pieces, -0.22, 0.18) * values
    return jnp.clip(values, min=-limit, max=limit).astype(kind)


def setup_inputs(seed: int = 0, part: int = 0) -> dict:
    key_list = jax.random.split(jax.random.key(seed), 6)
    part_splits = jax.random.split(jax.random.fold_in(key_list[5], part), 6)
    return {
        "queries": draw_queries(jax.random.fold_in(jax.random.fold_in(key_list[5], part), 71), part),
        "keys": draw_keys(jax.random.fold_in(jax.random.fold_in(key_list[5], part), 71), part),
        "values": normal_values(part_splits[2], (TOKENS, KVH * HD), 1.0, 6.0, ((0, 16),)),
        "block_table": draw_block_table(jax.random.fold_in(jax.random.fold_in(key_list[5], part), 71), part),
        "out_weight": normal_values(key_list[4], (H * HD, D), (H * HD) ** -0.5, 0.125, ((0, 16),)),
    }


def reference(queries, keys, values, block_table, out_weight):
    groups = H // KVH
    key_blocks = keys.reshape(NQB, QB, KVH, HD)
    value_blocks = values.reshape(NQB, QB, KVH, HD)
    query_blocks = queries.reshape(NQB, QB, KVH, groups, HD)
    scale = HD ** -0.5

    def one_block(packed):
        query, picks = packed
        key_set = key_blocks[picks].reshape(ENTRIES * QB, KVH, HD).astype(jnp.float32)
        value_set = value_blocks[picks].reshape(ENTRIES * QB, KVH, HD).astype(jnp.float32)
        scores = jnp.einsum("qkgd,skd->kgqs", query.astype(jnp.float32), key_set) * scale
        highest = jnp.max(scores, axis=-1, keepdims=True)
        weights = jnp.exp(scores - highest)
        total = jnp.sum(weights, axis=-1)
        rounded = lax.optimization_barrier(weights.astype(jnp.bfloat16)).astype(jnp.float32)
        mixed = jnp.einsum("kgqs,skd->qkgd", rounded, value_set)
        mixed = mixed / jnp.moveaxis(total, 2, 0)[..., None]
        return mixed.reshape(QB, H * HD).astype(jnp.bfloat16)

    attended = lax.map(one_block, (query_blocks, block_table)).reshape(TOKENS, H * HD)
    return jnp.dot(attended, out_weight, preferred_element_type=jnp.float32).astype(jnp.bfloat16)
```

```python
import functools

import jax
import jax.numpy as jnp
from jax import lax
from jax.experimental import pallas as pl
from jax.experimental.pallas import tpu as pltpu
from jax.sharding import PartitionSpec as P

H = 16
KVH = 4
HD = 128
QB = 128
ENTRIES = 8
GROUP = H // KVH
SCALE_LOG2 = HD ** (-0.5) * 1.4426950408889634


def attention_kernel(
    n_chip, hops, odd, where_ref, table_ref, q_ref, *refs
):
    count = len(hops)
    key_refs = refs[:count]
    value_refs = refs[count : 2 * count]
    o_ref, kbuf, vbuf, sems = refs[2 * count :]
    step = pl.program_id(0)
    head = pl.program_id(1)
    n_outer = n_chip // 2
    per_entry = n_chip // ENTRIES
    outer, side, core = where_ref[0], where_ref[1], where_ref[2]
    chip = outer * 2 + side

    @pl.when((step == 0) & (head == 0))
    def _():
        for at, (shift, flip) in enumerate(hops):
            source_outer = outer + shift
            source = source_outer * 2 + (1 - side if flip else side)
            ahead = source - chip + (core if odd else 0)
            ahead = lax.rem(ahead + 2 * n_chip, n_chip)
            usable = (source_outer >= 0) & (source_outer < n_outer)
            if per_entry > 1:
                usable = usable & (lax.rem(ahead, per_entry) == 0)
            entry = ahead // per_entry

            @pl.when(usable)
            def _():
                for block in range(2):
                    row = table_ref[2 * block + (1 if odd else 0), entry] & 3
                    rows = pl.ds(pl.multiple_of(row * QB, QB), QB)
                    slot = pl.ds(pl.multiple_of(entry * QB, QB), QB)
                    pltpu.make_async_copy(
                        key_refs[at].at[rows, :], kbuf.at[block, slot, :], sems.at[block, 0]
                    ).start()
                    pltpu.make_async_copy(
                        value_refs[at].at[rows, :], vbuf.at[block, slot, :], sems.at[block, 1]
                    ).start()

    @pl.when(head == 0)
    def _():
        pltpu.make_async_copy(kbuf.at[step], kbuf.at[step], sems.at[step, 0]).wait()
        pltpu.make_async_copy(vbuf.at[step], vbuf.at[step], sems.at[step, 1]).wait()

    columns = pl.ds(pl.multiple_of(head * HD, HD), HD)
    keys = kbuf[step, :, columns]
    values = vbuf[step, :, columns]
    for g in range(GROUP):
        query = q_ref[0, :, g * HD : (g + 1) * HD]
        scores = lax.dot_general(
            query, keys, (((1,), (1,)), ((), ())), preferred_element_type=jnp.float32
        )
        highest = jnp.max(scores, axis=-1, keepdims=True)
        weights = jnp.exp2((scores - highest) * SCALE_LOG2)
        total = jnp.sum(weights, axis=-1, keepdims=True)
        mixed = jnp.dot(
            weights.astype(jnp.bfloat16), values, preferred_element_type=jnp.float32
        )
        o_ref[0, :, g * HD : (g + 1) * HD] = (mixed / total).astype(jnp.bfloat16)


def attention(queries, where, table, hops, key_list, value_list, n_chip, odd):
    spread = queries.shape[0] // 2
    width = GROUP * HD
    rows = ENTRIES * QB
    hbm = pl.BlockSpec(memory_space=pl.ANY)
    return pl.pallas_call(
        functools.partial(attention_kernel, n_chip, hops, odd),
        out_shape=jax.ShapeDtypeStruct((2, QB, H * HD), jnp.bfloat16),
        grid_spec=pltpu.PrefetchScalarGridSpec(
            num_scalar_prefetch=2,
            grid=(2, KVH),
            in_specs=[pl.BlockSpec((1, QB, width), lambda b, h, w, t: (b * spread, 0, h))]
            + [hbm] * (2 * len(hops)),
            out_specs=pl.BlockSpec((1, QB, width), lambda b, h, w, t: (b, 0, h)),
            scratch_shapes=[
                pltpu.VMEM((2, rows, KVH * HD), jnp.bfloat16),
                pltpu.VMEM((2, rows, KVH * HD), jnp.bfloat16),
                pltpu.SemaphoreType.DMA((2, 2)),
            ],
        ),
        compiler_params=pltpu.CompilerParams(vmem_limit_bytes=32 * 1024 * 1024),
        cost_estimate=pl.CostEstimate(
            flops=4 * 2 * QB * rows * H * HD,
            bytes_accessed=2 * rows * 2 * KVH * HD * 2 + 4 * QB * H * HD * 2,
            transcendentals=2 * QB * rows * H,
        ),
    )(where, table, queries, *key_list, *value_list)


def project_kernel(even_ref, odd_ref, w_ref, o_ref, rows):
    @pl.when((pl.program_id(0) == 0) & (pl.program_id(1) == 0))
    def _():
        for block in range(2):
            rows[2 * block * QB : (2 * block + 1) * QB, :] = even_ref[block]
            rows[(2 * block + 1) * QB : (2 * block + 2) * QB, :] = odd_ref[block]

    o_ref[...] = jnp.dot(
        rows[...], w_ref[0], preferred_element_type=jnp.float32
    ).astype(jnp.bfloat16)


def project(even, odd, weights, tile=512):
    parts, depth, columns = weights.shape
    tiles = columns // tile
    whole = pl.BlockSpec((2, QB, depth), lambda p, t: (0, 0, 0))
    return pl.pallas_call(
        project_kernel,
        out_shape=jax.ShapeDtypeStruct((4 * QB, parts * columns), jnp.bfloat16),
        grid_spec=pl.GridSpec(
            grid=(parts, tiles),
            in_specs=[whole, whole, pl.BlockSpec((1, depth, tile), lambda p, t: (p, 0, t))],
            out_specs=pl.BlockSpec((4 * QB, tile), lambda p, t: (0, p * tiles + t)),
            scratch_shapes=[pltpu.VMEM((4 * QB, depth), jnp.bfloat16)],
        ),
        compiler_params=pltpu.CompilerParams(vmem_limit_bytes=32 * 1024 * 1024),
        cost_estimate=pl.CostEstimate(
            flops=2 * 4 * QB * depth * parts * columns,
            bytes_accessed=2 * (depth * parts * columns + 4 * QB * (depth + parts * columns)),
            transcendentals=0,
        ),
    )(even, odd, weights)


def body(n_groups, n_seq, queries, keys, values, block_table, out_weight):
    n_chip = n_seq // 2
    n_outer = n_chip // 2

    def index(outer, side, core):
        return (outer * 2 + side) * 2 + core

    places = [(o, s, c) for o in range(n_outer) for s in range(2) for c in range(2)]
    me = lax.axis_index("seq")
    where = jnp.stack([me // 4, (me // 2) % 2, me % 2]).astype(jnp.int32)

    def swap_core(array):
        return lax.ppermute(
            array, "seq", [(index(o, s, c), index(o, s, 1 - c)) for o, s, c in places]
        )

    def swap_side(array, shift):
        return lax.ppermute(
            array,
            "seq",
            [
                (index(o, s, c), index(o, 1 - s, c))
                for o, s, c in places
                if 0 <= o + shift < n_outer
            ],
        )

    def move(array, shift, way):
        return lax.ppermute(
            array,
            "seq",
            [
                (index(o, s, c), index(o + way, s, c))
                for o, s, c in places
                if 0 <= o + way < n_outer and 0 <= o + way + shift < n_outer
            ],
        )

    query_blocks = queries.reshape(4, QB, H * HD)
    far_queries = swap_core(query_blocks.reshape(2, 2, QB, H * HD)[:, 1])
    far_table = swap_core(block_table)

    group = lax.axis_index("groups")
    part = out_weight.shape[1] // n_groups
    mine = lax.dynamic_slice_in_dim(out_weight, group * part, part, 1)
    gathered = lax.all_gather(mine, ("groups", "seq"), axis=0, tiled=True)
    gathered = gathered.reshape(n_groups, n_seq * out_weight.shape[0], part)

    held = {0: (keys, values)}
    hops = [(0, False)]
    pieces = {(0, False): (keys, values)}
    for step in range(n_outer):
        for shift in ([0] if step == 0 else [-step, step]):
            pieces[(shift, True)] = tuple(swap_side(a, shift) for a in pieces[(shift, False)])
            hops.append((shift, True))
        if step + 1 < n_outer:
            for way in (1, -1):
                shift = -way * (step + 1)
                before = pieces[(-way * step, False)]
                pieces[(shift, False)] = tuple(move(a, shift, way) for a in before)
                hops.append((shift, False))

    key_list = [pieces[hop][0] for hop in hops]
    value_list = [pieces[hop][1] for hop in hops]
    far = attention(far_queries, where, far_table, hops, key_list, value_list, n_chip, True)
    odd = swap_core(far)
    even = attention(query_blocks, where, block_table, hops, key_list, value_list, n_chip, False)
    return project(even, odd, gathered)


def solution(mesh):
    in_specs = (
        P(("groups", "seq"), None),
        P(("groups", "seq"), None),
        P(("groups", "seq"), None),
        P(("groups", "seq"), None),
        P("seq", None),
    )
    out_specs = P(("groups", "seq"), None)
    run = functools.partial(body, mesh.shape["groups"], mesh.shape["seq"])
    return jax.shard_map(run, mesh=mesh, in_specs=in_specs, out_specs=out_specs, check_vma=False)
```

```python
import functools

import jax
import jax.numpy as jnp
import numpy as np
from jax import lax
from jax.experimental import pallas as pl
from jax.experimental.pallas import tpu as pltpu
from jax.sharding import PartitionSpec as P

H = 16
KVH = 4
HD = 128
QB = 128
ENTRIES = 8
GROUP = H // KVH
SCALE_LOG2 = HD ** (-0.5) * 1.4426950408889634
NT = (((1,), (1,)), ((), ()))


def arrivals(n_outer):
    rows = []
    for place in range(n_outer):
        row = [0]
        for hop in range(1, n_outer):
            if place - hop >= 0:
                row.append(-hop)
            if place + hop < n_outer:
                row.append(hop)
        rows.append(row)
    return rows


def attention_kernel(n_chip, odd, where_ref, order_ref, table_ref, q_ref, *refs):
    n_outer = n_chip // 2
    pieces = refs[: 2 * n_outer]
    o_ref, kbuf, vbuf, sems = refs[2 * n_outer :]
    step = pl.program_id(0)
    head = pl.program_id(1)
    per_entry = n_chip // ENTRIES
    outer, side, core = where_ref[0], where_ref[1], where_ref[2]
    chip = outer * 2 + side

    @pl.when((step == 0) & (head == 0))
    def _():
        for at in range(2 * n_outer):
            source_side = side if at < n_outer else 1 - side
            source = order_ref[outer, at % n_outer] * 2 + source_side
            ahead = source - chip + (core if odd else 0)
            ahead = lax.rem(ahead + 2 * n_chip, n_chip)
            entry = ahead // per_entry

            def fetch():
                for block in range(2):
                    row = table_ref[2 * block + (1 if odd else 0), entry] & 3
                    slot = pl.ds(pl.multiple_of(entry * QB, QB), QB)
                    for half, buf in enumerate((kbuf, vbuf)):
                        rows = pl.ds(pl.multiple_of((half * 4 + row) * QB, QB), QB)
                        pltpu.make_async_copy(
                            pieces[at].at[rows, :], buf.at[block, slot, :], sems.at[block, half]
                        ).start()

            if per_entry > 1:
                pl.when(lax.rem(ahead, per_entry) == 0)(fetch)
            else:
                fetch()

    @pl.when(head == 0)
    def _():
        pltpu.make_async_copy(kbuf.at[step], kbuf.at[step], sems.at[step, 0]).wait()
        pltpu.make_async_copy(vbuf.at[step], vbuf.at[step], sems.at[step, 1]).wait()

    columns = pl.ds(pl.multiple_of(head * HD, HD), HD)
    keys = kbuf[step, :, columns]
    values = vbuf[step, :, columns]
    scores = [
        lax.dot_general(
            q_ref[0, :, g * HD : (g + 1) * HD], keys, NT, preferred_element_type=jnp.float32
        )
        for g in range(GROUP)
    ]
    rounded, totals = [], []
    for s in scores:
        weights = jnp.exp2((s - jnp.max(s, axis=-1, keepdims=True)) * SCALE_LOG2)
        totals.append(jnp.sum(weights, axis=-1, keepdims=True))
        rounded.append(weights.astype(jnp.bfloat16))
    for g in range(GROUP):
        mixed = jnp.dot(rounded[g], values, preferred_element_type=jnp.float32)
        o_ref[0, :, g * HD : (g + 1) * HD] = (mixed / totals[g]).astype(jnp.bfloat16)


def attention(queries, where, order, table, pieces, n_chip, odd):
    spread = queries.shape[0] // 2
    width = GROUP * HD
    rows = ENTRIES * QB
    hbm = pl.BlockSpec(memory_space=pltpu.HBM)
    return pl.pallas_call(
        functools.partial(attention_kernel, n_chip, odd),
        out_shape=jax.ShapeDtypeStruct((2, QB, H * HD), jnp.bfloat16),
        grid_spec=pltpu.PrefetchScalarGridSpec(
            num_scalar_prefetch=3,
            grid=(2, KVH),
            in_specs=[pl.BlockSpec((1, QB, width), lambda b, h, *_: (b * spread, 0, h))]
            + [hbm] * len(pieces),
            out_specs=pl.BlockSpec((1, QB, width), lambda b, h, *_: (b, 0, h)),
            scratch_shapes=[
                pltpu.VMEM((2, rows, KVH * HD), jnp.bfloat16),
                pltpu.VMEM((2, rows, KVH * HD), jnp.bfloat16),
                pltpu.SemaphoreType.DMA((2, 2)),
            ],
        ),
        compiler_params=pltpu.CompilerParams(vmem_limit_bytes=32 * 1024 * 1024),
        cost_estimate=pl.CostEstimate(
            flops=4 * 2 * QB * rows * H * HD,
            bytes_accessed=2 * rows * 2 * KVH * HD * 2 + 4 * QB * H * HD * 2,
            transcendentals=2 * QB * rows * H,
        ),
    )(where, order, table, queries, *pieces)


def project_kernel(n_outer, parts, depth, where_ref, order_ref, even_ref, odd_ref, *refs):
    sets = [refs[p * n_outer : (p + 1) * n_outer] for p in range(parts)]
    o_ref, rows, wbuf, sems = refs[-4:]
    part, half = pl.program_id(0), pl.program_id(1)
    step = part * 2 + half
    outer, side = where_ref[0], where_ref[1]

    def fetch(into, p, h):
        for at in range(n_outer):
            chip = order_ref[outer, at] * 2
            for source_side, first in ((side, (0, 1)[h]), (1 - side, (3, 2)[h])):
                to = pl.ds(pl.multiple_of((chip + source_side) * depth, depth), depth)
                pltpu.make_async_copy(
                    sets[p][at].at[first * depth : (first + 1) * depth, :],
                    wbuf.at[into, to, :],
                    sems.at[into],
                ).start()

    @pl.when(step == 0)
    def _():
        fetch(0, 0, 0)
        for block in range(2):
            rows[2 * block * QB : (2 * block + 1) * QB, :] = even_ref[block]
            rows[(2 * block + 1) * QB : (2 * block + 2) * QB, :] = odd_ref[block]

    for later in range(1, 2 * parts):

        @pl.when(step == later - 1)
        def _():
            fetch(later % 2, later // 2, later % 2)

    pltpu.make_async_copy(wbuf.at[half], wbuf.at[half], sems.at[half]).wait()
    o_ref[...] = jnp.dot(
        rows[...], wbuf[half], preferred_element_type=jnp.float32
    ).astype(jnp.bfloat16)


def project(even, odd, where, order, places, sets, columns, before=None):
    parts, n_outer = len(sets), len(sets[0])
    depth, half = sets[0][0].shape[0] // 4, sets[0][0].shape[1]
    total = H * HD
    whole = pl.BlockSpec((2, QB, total), lambda p, h, *_: (0, 0, 0))
    hbm = pl.BlockSpec(memory_space=pltpu.HBM)
    count = 3 + 2 + parts * n_outer
    kernel = functools.partial(project_kernel, n_outer, parts, depth)
    if before is not None:
        inner = kernel

        def kernel(where_ref, order_ref, places_ref, e, o, *refs):
            inner(where_ref, order_ref, e, o, *refs[: parts * n_outer], *refs[-4:])

    else:
        inner = kernel

        def kernel(where_ref, order_ref, places_ref, e, o, *refs):
            inner(where_ref, order_ref, e, o, *refs)

    return pl.pallas_call(
        kernel,
        out_shape=jax.ShapeDtypeStruct((4 * QB, columns), jnp.bfloat16),
        grid_spec=pltpu.PrefetchScalarGridSpec(
            num_scalar_prefetch=3,
            grid=(parts, 2),
            in_specs=[whole, whole]
            + [hbm] * (parts * n_outer)
            + ([] if before is None else [hbm]),
            out_specs=pl.BlockSpec((4 * QB, half), lambda p, h, w, r, q: (0, q[p] * 2 + h)),
            scratch_shapes=[
                pltpu.VMEM((4 * QB, total), jnp.bfloat16),
                pltpu.VMEM((2, total, half), jnp.bfloat16),
                pltpu.SemaphoreType.DMA((2,)),
            ],
        ),
        input_output_aliases={} if before is None else {count: 0},
        compiler_params=pltpu.CompilerParams(vmem_limit_bytes=32 * 1024 * 1024),
        cost_estimate=pl.CostEstimate(
            flops=2 * 4 * QB * total * parts * 2 * half,
            bytes_accessed=2 * (total * parts * 2 * half + 4 * QB * (total + parts * 2 * half)),
            transcendentals=0,
        ),
    )(
        where,
        order,
        places,
        even,
        odd,
        *[piece for pieces in sets for piece in pieces],
        *([] if before is None else [before]),
    )


def body(n_groups, n_seq, queries, keys, values, block_table, out_weight):
    n_chip = n_seq // 2
    n_outer = n_chip // 2
    order_rows = arrivals(n_outer)

    def index(outer, side, core):
        return (outer * 2 + side) * 2 + core

    spots = [(o, s, c) for o in range(n_outer) for s in range(2) for c in range(2)]
    me = lax.axis_index("seq")
    group = lax.axis_index("groups")
    outer, side, core = me // 4, (me // 2) % 2, me % 2
    where = jnp.stack([outer, side, core]).astype(jnp.int32)
    order = jnp.asarray(
        np.array([[p + d for d in row] for p, row in enumerate(order_rows)], np.int32)
    )

    def swap_core(array):
        return lax.ppermute(
            array, "seq", [(index(o, s, c), index(o, s, 1 - c)) for o, s, c in spots]
        )

    def swap_side(array):
        return lax.ppermute(
            array, "seq", [(index(o, s, c), index(o, 1 - s, c)) for o, s, c in spots]
        )

    def move(array, hop, way):
        return lax.ppermute(
            array,
            "seq",
            [
                (index(o, s, c), index(o + way, s, c))
                for o, s, c in spots
                if 0 <= o + way < n_outer and 0 <= o - (hop - 1) * way < n_outer
            ],
        )

    def line(array):
        got = {0: array}
        for hop in range(1, n_outer):
            for way in (1, -1):
                got[-way * hop] = move(got[-way * (hop - 1)], hop, way)
        return got

    def pick(got, k):
        wanted = [row[k] for row in order_rows]
        result = got[wanted[0]]
        for offset in sorted(set(wanted[1:])):
            mask = functools.reduce(
                jnp.logical_or, [outer == p for p in range(n_outer) if wanted[p] == offset]
            )
            if offset != wanted[0]:
                result = jnp.where(mask, got[offset], result)
        return result

    query_blocks = queries.reshape(4, QB, H * HD)
    far_queries = swap_core(query_blocks.reshape(2, 2, QB, H * HD)[:, 1])
    far_table = swap_core(block_table)

    got = line(jnp.concatenate([keys, values], 0))
    near = [got[0]] + [pick(got, k) for k in range(1, n_outer)]
    pieces = near + [swap_side(piece) for piece in near]

    quarter = out_weight.shape[1] // (2 * n_groups)
    half = quarter // 2
    mine = lax.dynamic_slice_in_dim(out_weight, (group * 2 + core) * quarter, quarter, 1)
    theirs = lax.dynamic_slice_in_dim(out_weight, (group * 2 + 1 - core) * quarter, quarter, 1)
    theirs = swap_core(theirs)
    first = jnp.where(core == 0, mine, theirs)
    second = jnp.where(core == 0, theirs, mine)
    early = jnp.concatenate([first[:, half:], second[:, half:]], 0)
    late = jnp.concatenate([first[:, :half], second[:, :half]], 0)
    depth = late.shape[0]
    wgot = line(jnp.concatenate([late, early, swap_side(early)], 0))
    wnear = [wgot[0]] + [pick(wgot, k) for k in range(1, n_outer)]
    own = [jnp.concatenate([w, swap_side(w[:depth])], 0) for w in wnear]

    far = attention(far_queries, where, order, far_table, pieces, n_chip, True)
    odd = swap_core(far)
    even = attention(query_blocks, where, order, block_table, pieces, n_chip, False)

    sets = [own]
    for shift in range(1, n_groups):
        turn = [(g, (g + shift) % n_groups) for g in range(n_groups)]
        sets.append([lax.ppermute(w, "groups", turn) for w in own])
    groups = [(group - shift + n_groups) % n_groups for shift in range(n_groups)]
    columns = out_weight.shape[1]
    near_places = jnp.stack([g * 2 + core for g in groups]).astype(jnp.int32)
    far_places = jnp.stack([g * 2 + 1 - core for g in groups]).astype(jnp.int32)
    out = project(even, odd, where, order, near_places, sets, columns)
    far_sets = [[swap_core(w) for w in pieces_of] for pieces_of in sets]
    return project(even, odd, where, order, far_places, far_sets, columns, out)


def solution(mesh):
    in_specs = (
        P(("groups", "seq"), None),
        P(("groups", "seq"), None),
        P(("groups", "seq"), None),
        P(("groups", "seq"), None),
        P("seq", None),
    )
    out_specs = P(("groups", "seq"), None)
    run = functools.partial(body, mesh.shape["groups"], mesh.shape["seq"])
    return jax.shard_map(run, mesh=mesh, in_specs=in_specs, out_specs=out_specs, check_vma=False)
```

```python
import functools

import jax
import jax.numpy as jnp
import numpy as np
from jax import lax
from jax.experimental import pallas as pl
from jax.experimental.pallas import tpu as pltpu
from jax.sharding import PartitionSpec as P

H = 16
KVH = 4
HD = 128
QB = 128
ENTRIES = 8
GROUP = H // KVH
SCALE_LOG2 = HD ** (-0.5) * 1.4426950408889634
NT = (((1,), (1,)), ((), ()))
VMEM_LIMIT = 40 * 1024 * 1024


def arrivals(n_outer):
    rows = []
    for place in range(n_outer):
        row = [0]
        for hop in range(1, n_outer):
            if place - hop >= 0:
                row.append(-hop)
            if place + hop < n_outer:
                row.append(hop)
        rows.append(row)
    return rows


def attention_kernel(n_chip, odd, where_ref, order_ref, table_ref, q_ref, *refs):
    n_outer = n_chip // 2
    pieces, o_ref = refs[:-1], refs[-1]
    step = pl.program_id(0)
    head = pl.program_id(1)
    per_entry = n_chip // ENTRIES
    outer, side, core = where_ref[0], where_ref[1], where_ref[2]
    chip = outer * 2 + side
    columns = pl.ds(pl.multiple_of(head * HD, HD), HD)

    keys, values, usable = [], [], []
    for at, piece in enumerate(pieces):
        source_side = side if at < n_outer else 1 - side
        source = order_ref[outer, at % n_outer] * 2 + source_side
        ahead = lax.rem(source - chip + (core if odd else 0) + 2 * n_chip, n_chip)
        row = table_ref[2 * step + (1 if odd else 0), ahead // per_entry] & 3
        keys.append(piece[pl.ds(pl.multiple_of(row * QB, QB), QB), columns])
        values.append(piece[pl.ds(pl.multiple_of((4 + row) * QB, QB), QB), columns])
        usable.append(lax.rem(ahead, per_entry) == 0)
    keys = jnp.concatenate(keys, 0)
    values = jnp.concatenate(values, 0)

    scores = []
    for g in range(GROUP):
        s = lax.dot_general(
            q_ref[0, :, g * HD : (g + 1) * HD], keys, NT, preferred_element_type=jnp.float32
        )
        if per_entry > 1:
            s = jnp.concatenate(
                [
                    jnp.where(ok, s[:, at * QB : (at + 1) * QB], -1e30)
                    for at, ok in enumerate(usable)
                ],
                1,
            )
        scores.append(s)
    rounded, totals = [], []
    for s in scores:
        weights = jnp.exp2((s - jnp.max(s, axis=-1, keepdims=True)) * SCALE_LOG2)
        totals.append(jnp.sum(weights, axis=-1, keepdims=True))
        rounded.append(weights.astype(jnp.bfloat16))
    for g in range(GROUP):
        mixed = jnp.dot(rounded[g], values, preferred_element_type=jnp.float32)
        o_ref[0, :, g * HD : (g + 1) * HD] = (mixed / totals[g]).astype(jnp.bfloat16)


def attention(queries, where, order, table, pieces, n_chip, odd):
    spread = queries.shape[0] // 2
    width = GROUP * HD
    rows = ENTRIES * QB
    whole = pl.BlockSpec(memory_space=pltpu.VMEM)
    return pl.pallas_call(
        functools.partial(attention_kernel, n_chip, odd),
        out_shape=jax.ShapeDtypeStruct((2, QB, H * HD), jnp.bfloat16),
        grid_spec=pltpu.PrefetchScalarGridSpec(
            num_scalar_prefetch=3,
            grid=(2, KVH),
            in_specs=[pl.BlockSpec((1, QB, width), lambda b, h, *_: (b * spread, 0, h))]
            + [whole] * len(pieces),
            out_specs=pl.BlockSpec((1, QB, width), lambda b, h, *_: (b, 0, h)),
        ),
        compiler_params=pltpu.CompilerParams(vmem_limit_bytes=VMEM_LIMIT),
        cost_estimate=pl.CostEstimate(
            flops=4 * 2 * QB * rows * H * HD,
            bytes_accessed=2 * rows * 2 * KVH * HD * 2 + 4 * QB * H * HD * 2,
            transcendentals=2 * QB * rows * H,
        ),
    )(where, order, table, queries, *pieces)


def project_kernel(n_outer, parts, depth, where_ref, order_ref, even_ref, odd_ref, *refs):
    sets = [refs[p * n_outer : (p + 1) * n_outer] for p in range(parts)]
    o_ref, rows, wbuf, sems = refs[-4:]
    part, half = pl.program_id(0), pl.program_id(1)
    step = part * 2 + half
    outer, side = where_ref[0], where_ref[1]

    def fetch(into, p, h):
        for at in range(n_outer):
            chip = order_ref[outer, at] * 2
            for source_side, first in ((side, (0, 1)[h]), (1 - side, (3, 2)[h])):
                to = pl.ds(pl.multiple_of((chip + source_side) * depth, depth), depth)
                pltpu.make_async_copy(
                    sets[p][at].at[first * depth : (first + 1) * depth, :],
                    wbuf.at[into, to, :],
                    sems.at[into],
                ).start()

    @pl.when(step == 0)
    def _():
        fetch(0, 0, 0)
        for block in range(2):
            rows[2 * block * QB : (2 * block + 1) * QB, :] = even_ref[block]
            rows[(2 * block + 1) * QB : (2 * block + 2) * QB, :] = odd_ref[block]

    for later in range(1, 2 * parts):

        @pl.when(step == later - 1)
        def _():
            fetch(later % 2, later // 2, later % 2)

    pltpu.make_async_copy(wbuf.at[half], wbuf.at[half], sems.at[half]).wait()
    o_ref[...] = jnp.dot(
        rows[...], wbuf[half], preferred_element_type=jnp.float32
    ).astype(jnp.bfloat16)


def project(even, odd, where, order, places, sets, columns, before=None):
    parts, n_outer = len(sets), len(sets[0])
    depth, half = sets[0][0].shape[0] // 4, sets[0][0].shape[1]
    total = H * HD
    whole = pl.BlockSpec((2, QB, total), lambda p, h, *_: (0, 0, 0))
    inside = pl.BlockSpec(memory_space=pltpu.VMEM)
    hbm = pl.BlockSpec(memory_space=pltpu.HBM)
    count = 3 + 2 + parts * n_outer
    kernel = functools.partial(project_kernel, n_outer, parts, depth)
    if before is not None:
        inner = kernel

        def kernel(where_ref, order_ref, places_ref, e, o, *refs):
            inner(where_ref, order_ref, e, o, *refs[: parts * n_outer], *refs[-4:])

    else:
        inner = kernel

        def kernel(where_ref, order_ref, places_ref, e, o, *refs):
            inner(where_ref, order_ref, e, o, *refs)

    return pl.pallas_call(
        kernel,
        out_shape=jax.ShapeDtypeStruct((4 * QB, columns), jnp.bfloat16),
        grid_spec=pltpu.PrefetchScalarGridSpec(
            num_scalar_prefetch=3,
            grid=(parts, 2),
            in_specs=[whole, whole]
            + [inside] * (parts * n_outer)
            + ([] if before is None else [hbm]),
            out_specs=pl.BlockSpec((4 * QB, half), lambda p, h, w, r, q: (0, q[p] * 2 + h)),
            scratch_shapes=[
                pltpu.VMEM((4 * QB, total), jnp.bfloat16),
                pltpu.VMEM((2, total, half), jnp.bfloat16),
                pltpu.SemaphoreType.DMA((2,)),
            ],
        ),
        input_output_aliases={} if before is None else {count: 0},
        compiler_params=pltpu.CompilerParams(vmem_limit_bytes=VMEM_LIMIT),
        cost_estimate=pl.CostEstimate(
            flops=2 * 4 * QB * total * parts * 2 * half,
            bytes_accessed=2 * (total * parts * 2 * half + 4 * QB * (total + parts * 2 * half)),
            transcendentals=0,
        ),
    )(
        where,
        order,
        places,
        even,
        odd,
        *[piece for pieces in sets for piece in pieces],
        *([] if before is None else [before]),
    )


def body(n_groups, n_seq, queries, keys, values, block_table, out_weight):
    n_chip = n_seq // 2
    n_outer = n_chip // 2
    order_rows = arrivals(n_outer)

    def index(outer, side, core):
        return (outer * 2 + side) * 2 + core

    spots = [(o, s, c) for o in range(n_outer) for s in range(2) for c in range(2)]
    me = lax.axis_index("seq")
    group = lax.axis_index("groups")
    outer, side, core = me // 4, (me // 2) % 2, me % 2
    where = jnp.stack([outer, side, core]).astype(jnp.int32)
    order = jnp.asarray(
        np.array([[p + d for d in row] for p, row in enumerate(order_rows)], np.int32)
    )

    def swap_core(array):
        return lax.ppermute(
            array, "seq", [(index(o, s, c), index(o, s, 1 - c)) for o, s, c in spots]
        )

    def swap_side(array):
        return lax.ppermute(
            array, "seq", [(index(o, s, c), index(o, 1 - s, c)) for o, s, c in spots]
        )

    def move(array, hop, way):
        return lax.ppermute(
            array,
            "seq",
            [
                (index(o, s, c), index(o + way, s, c))
                for o, s, c in spots
                if 0 <= o + way < n_outer and 0 <= o - (hop - 1) * way < n_outer
            ],
        )

    def line(array):
        got = {0: array}
        for hop in range(1, n_outer):
            for way in (1, -1):
                got[-way * hop] = move(got[-way * (hop - 1)], hop, way)
        return got

    def pick(got, k):
        wanted = [row[k] for row in order_rows]
        result = got[wanted[0]]
        for offset in sorted(set(wanted[1:])):
            mask = functools.reduce(
                jnp.logical_or, [outer == p for p in range(n_outer) if wanted[p] == offset]
            )
            if offset != wanted[0]:
                result = jnp.where(mask, got[offset], result)
        return result

    def after(array, *others):
        return lax.optimization_barrier((array, *others))[0]

    got = line(jnp.concatenate([keys, values], 0))
    near, across = [got[0]], [swap_side(got[0])]
    for k in range(1, n_outer):
        tied = {
            d: after(got[d], near[-1])
            for d in sorted({row[k] for row in order_rows})
        }
        near.append(pick(tied, k))
        across.append(swap_side(after(near[-1], across[-1])))
    pieces = near + across

    query_blocks = queries.reshape(4, QB, H * HD)
    far_table = swap_core(block_table)

    quarter = out_weight.shape[1] // (2 * n_groups)
    half = quarter // 2
    mine = lax.dynamic_slice_in_dim(out_weight, (group * 2 + core) * quarter, quarter, 1)
    theirs = lax.dynamic_slice_in_dim(out_weight, (group * 2 + 1 - core) * quarter, quarter, 1)
    theirs = swap_core(theirs)
    far_queries = swap_core(
        after(query_blocks.reshape(2, 2, QB, H * HD)[:, 1], theirs)
    )
    first = jnp.where(core == 0, mine, theirs)
    second = jnp.where(core == 0, theirs, mine)
    early = jnp.concatenate([first[:, half:], second[:, half:]], 0)
    late = jnp.concatenate([first[:, :half], second[:, :half]], 0)
    depth = late.shape[0]
    ends = [got[d] for d in (1 - n_outer, n_outer - 1)]
    wgot = line(after(jnp.concatenate([late, early, swap_side(early)], 0), *ends))
    own = []
    last = across[-1]
    for k in range(n_outer):
        if k == 0:
            w = wgot[0]
        else:
            w = pick(
                {d: after(wgot[d], own[-1]) for d in sorted({row[k] for row in order_rows})}, k
            )
        last = swap_side(after(w[:depth], last))
        own.append(jnp.concatenate([w, last], 0))

    far = attention(far_queries, where, order, far_table, pieces, n_chip, True)
    odd = swap_core(far)
    even = attention(query_blocks, where, order, block_table, pieces, n_chip, False)

    sets = [own]
    for shift in range(1, n_groups):
        turn = [(g, (g + shift) % n_groups) for g in range(n_groups)]
        sets.append([lax.ppermute(w, "groups", turn) for w in own])
    groups = [(group - shift + n_groups) % n_groups for shift in range(n_groups)]
    columns = out_weight.shape[1]
    near_places = jnp.stack([g * 2 + core for g in groups]).astype(jnp.int32)
    far_places = jnp.stack([g * 2 + 1 - core for g in groups]).astype(jnp.int32)
    out = project(even, odd, where, order, near_places, sets, columns)
    far_sets = [[swap_core(w) for w in pieces_of] for pieces_of in sets]
    return project(even, odd, where, order, far_places, far_sets, columns, out)


def solution(mesh):
    in_specs = (
        P(("groups", "seq"), None),
        P(("groups", "seq"), None),
        P(("groups", "seq"), None),
        P(("groups", "seq"), None),
        P("seq", None),
    )
    out_specs = P(("groups", "seq"), None)
    run = functools.partial(body, mesh.shape["groups"], mesh.shape["seq"])
    return jax.shard_map(run, mesh=mesh, in_specs=in_specs, out_specs=out_specs, check_vma=False)
```

```python
import functools

import jax
import jax.numpy as jnp
import numpy as np
from jax import lax
from jax.experimental import pallas as pl
from jax.experimental.pallas import tpu as pltpu
from jax.sharding import PartitionSpec as P

H = 16
KVH = 4
HD = 128
QB = 128
ENTRIES = 8
GROUP = H // KVH
SCALE_LOG2 = HD ** (-0.5) * 1.4426950408889634
NT = (((1,), (1,)), ((), ()))
VMEM_LIMIT = 40 * 1024 * 1024


def arrivals(n_outer):
    rows = []
    for place in range(n_outer):
        row = [0]
        for hop in range(1, n_outer):
            if place - hop >= 0:
                row.append(-hop)
            if place + hop < n_outer:
                row.append(hop)
        rows.append(row)
    return rows


def attention_kernel(
    n_chip, where_ref, order_ref, table_ref, far_table_ref, q_ref, far_q_ref, *refs
):
    n_outer = n_chip // 2
    pieces, o_ref, far_o_ref = refs[:-2], refs[-2], refs[-1]
    step = pl.program_id(0)
    head = pl.program_id(1)
    per_entry = n_chip // ENTRIES
    outer, side, core = where_ref[0], where_ref[1], where_ref[2]
    chip = outer * 2 + side
    odd = step < 2
    columns = pl.ds(pl.multiple_of(head * HD, HD), HD)

    keys, values, usable = [], [], []
    for at, piece in enumerate(pieces):
        source_side = side if at < n_outer else 1 - side
        source = order_ref[outer, at % n_outer] * 2 + source_side
        ahead = lax.rem(source - chip + jnp.where(odd, core, 0) + 2 * n_chip, n_chip)
        entry = ahead // per_entry
        row = (
            jnp.where(
                odd,
                far_table_ref[2 * lax.rem(step, 2) + 1, entry],
                table_ref[2 * lax.rem(step, 2), entry],
            )
            & 3
        )
        keys.append(piece[pl.ds(pl.multiple_of(row * QB, QB), QB), columns])
        values.append(piece[pl.ds(pl.multiple_of((4 + row) * QB, QB), QB), columns])
        usable.append(lax.rem(ahead, per_entry) == 0)
    keys = jnp.concatenate(keys, 0)
    values = jnp.concatenate(values, 0)
    queries = jnp.where(odd, far_q_ref[0], q_ref[0])

    scores = []
    for g in range(GROUP):
        s = lax.dot_general(
            queries[:, g * HD : (g + 1) * HD], keys, NT, preferred_element_type=jnp.float32
        )
        if per_entry > 1:
            s = jnp.concatenate(
                [
                    jnp.where(ok, s[:, at * QB : (at + 1) * QB], -1e30)
                    for at, ok in enumerate(usable)
                ],
                1,
            )
        scores.append(s)
    rounded, totals = [], []
    for s in scores:
        weights = jnp.exp2((s - jnp.max(s, axis=-1, keepdims=True)) * SCALE_LOG2)
        totals.append(jnp.sum(weights, axis=-1, keepdims=True))
        rounded.append(weights.astype(jnp.bfloat16))
    mixed = [
        (jnp.dot(rounded[g], values, preferred_element_type=jnp.float32) / totals[g]).astype(
            jnp.bfloat16
        )
        for g in range(GROUP)
    ]
    result = jnp.concatenate(mixed, 1)

    @pl.when(odd)
    def _():
        far_o_ref[0] = result

    @pl.when(jnp.logical_not(odd))
    def _():
        o_ref[0] = result


def attention(queries, far_queries, where, order, table, far_table, pieces, n_chip):
    width = GROUP * HD
    rows = ENTRIES * QB
    whole = pl.BlockSpec(memory_space=pltpu.VMEM)
    last = KVH - 1

    def near_at(spread):
        return lambda b, h, *_: (
            jnp.where(b < 2, 0, b - 2) * spread, 0, jnp.where(b < 2, 0, h)
        )

    def far_at(b, h, *_):
        return (jnp.where(b < 2, b, 1), 0, jnp.where(b < 2, h, last))

    block = (1, QB, width)
    shape = jax.ShapeDtypeStruct((2, QB, H * HD), jnp.bfloat16)
    return pl.pallas_call(
        functools.partial(attention_kernel, n_chip),
        out_shape=(shape, shape),
        grid_spec=pltpu.PrefetchScalarGridSpec(
            num_scalar_prefetch=4,
            grid=(4, KVH),
            in_specs=[pl.BlockSpec(block, near_at(2)), pl.BlockSpec(block, far_at)]
            + [whole] * len(pieces),
            out_specs=(pl.BlockSpec(block, near_at(1)), pl.BlockSpec(block, far_at)),
        ),
        compiler_params=pltpu.CompilerParams(vmem_limit_bytes=VMEM_LIMIT),
        cost_estimate=pl.CostEstimate(
            flops=4 * 4 * QB * rows * H * HD,
            bytes_accessed=4 * rows * 2 * KVH * HD * 2 + 8 * QB * H * HD * 2,
            transcendentals=4 * QB * rows * H,
        ),
    )(where, order, table, far_table, queries, far_queries, *pieces)


def project_kernel(even_ref, odd_ref, w_ref, o_ref, rows):
    @pl.when((pl.program_id(0) == 0) & (pl.program_id(1) == 0))
    def _():
        for block in range(2):
            rows[2 * block * QB : (2 * block + 1) * QB, :] = even_ref[block]
            rows[(2 * block + 1) * QB : (2 * block + 2) * QB, :] = odd_ref[block]

    o_ref[...] = jnp.dot(
        rows[...], w_ref[0], preferred_element_type=jnp.float32
    ).astype(jnp.bfloat16)


def project(even, odd, weights, tile=512):
    parts, depth, columns = weights.shape
    tiles = columns // tile
    whole = pl.BlockSpec((2, QB, depth), lambda p, t: (0, 0, 0))
    return pl.pallas_call(
        project_kernel,
        out_shape=jax.ShapeDtypeStruct((4 * QB, parts * columns), jnp.bfloat16),
        grid_spec=pl.GridSpec(
            grid=(parts, tiles),
            in_specs=[whole, whole, pl.BlockSpec((1, depth, tile), lambda p, t: (p, 0, t))],
            out_specs=pl.BlockSpec((4 * QB, tile), lambda p, t: (0, p * tiles + t)),
            scratch_shapes=[pltpu.VMEM((4 * QB, depth), jnp.bfloat16)],
        ),
        compiler_params=pltpu.CompilerParams(vmem_limit_bytes=VMEM_LIMIT),
        cost_estimate=pl.CostEstimate(
            flops=2 * 4 * QB * depth * parts * columns,
            bytes_accessed=2 * (depth * parts * columns + 4 * QB * (depth + parts * columns)),
            transcendentals=0,
        ),
    )(even, odd, weights)


def body(n_groups, n_seq, queries, keys, values, block_table, out_weight):
    n_chip = n_seq // 2
    n_outer = n_chip // 2
    order_rows = arrivals(n_outer)

    def index(outer, side, core):
        return (outer * 2 + side) * 2 + core

    spots = [(o, s, c) for o in range(n_outer) for s in range(2) for c in range(2)]
    me = lax.axis_index("seq")
    group = lax.axis_index("groups")
    outer, side, core = me // 4, (me // 2) % 2, me % 2
    where = jnp.stack([outer, side, core]).astype(jnp.int32)
    order = jnp.asarray(
        np.array([[p + d for d in row] for p, row in enumerate(order_rows)], np.int32)
    )

    def swap_core(array):
        return lax.ppermute(
            array, "seq", [(index(o, s, c), index(o, s, 1 - c)) for o, s, c in spots]
        )

    def swap_side(array):
        return lax.ppermute(
            array, "seq", [(index(o, s, c), index(o, 1 - s, c)) for o, s, c in spots]
        )

    def move(array, hop, way):
        return lax.ppermute(
            array,
            "seq",
            [
                (index(o, s, c), index(o + way, s, c))
                for o, s, c in spots
                if 0 <= o + way < n_outer and 0 <= o - (hop - 1) * way < n_outer
            ],
        )

    def line(array):
        got = {0: array}
        for hop in range(1, n_outer):
            for way in (1, -1):
                got[-way * hop] = move(got[-way * (hop - 1)], hop, way)
        return got

    def pick(got, k):
        wanted = [row[k] for row in order_rows]
        result = got[wanted[0]]
        for offset in sorted(set(wanted[1:])):
            mask = functools.reduce(
                jnp.logical_or, [outer == p for p in range(n_outer) if wanted[p] == offset]
            )
            if offset != wanted[0]:
                result = jnp.where(mask, got[offset], result)
        return result

    def after(array, *others):
        return lax.optimization_barrier((array, *others))[0]

    got = line(jnp.concatenate([keys, values], 0))
    near, across = [got[0]], [swap_side(got[0])]
    for k in range(1, n_outer):
        tied = {
            d: after(got[d], near[-1])
            for d in sorted({row[k] for row in order_rows})
        }
        near.append(pick(tied, k))
        across.append(swap_side(after(near[-1], across[-1])))
    pieces = near + across

    query_blocks = queries.reshape(4, QB, H * HD)
    far_table = swap_core(block_table)

    part = out_weight.shape[1] // n_groups
    mine = lax.dynamic_slice_in_dim(out_weight, group * part, part, 1)
    gathered = lax.all_gather(mine, ("groups", "seq"), axis=0, tiled=True)
    gathered = gathered.reshape(n_groups, n_seq * out_weight.shape[0], part)
    far_queries = swap_core(query_blocks.reshape(2, 2, QB, H * HD)[:, 1])

    even, far = attention(
        query_blocks, far_queries, where, order, block_table, far_table, pieces, n_chip
    )
    return project(even, swap_core(far), gathered)


def solution(mesh):
    in_specs = (
        P(("groups", "seq"), None),
        P(("groups", "seq"), None),
        P(("groups", "seq"), None),
        P(("groups", "seq"), None),
        P("seq", None),
    )
    out_specs = P(("groups", "seq"), None)
    run = functools.partial(body, mesh.shape["groups"], mesh.shape["seq"])
    return jax.shard_map(run, mesh=mesh, in_specs=in_specs, out_specs=out_specs, check_vma=False)
```

```python
import functools

import jax
import jax.numpy as jnp
import numpy as np
from jax import lax
from jax.experimental import pallas as pl
from jax.experimental.pallas import tpu as pltpu
from jax.sharding import PartitionSpec as P

H = 16
KVH = 4
HD = 128
QB = 128
ENTRIES = 8
GROUP = H // KVH
SCALE_LOG2 = HD ** (-0.5) * 1.4426950408889634
NT = (((1,), (1,)), ((), ()))
VMEM_LIMIT = 40 * 1024 * 1024


def arrivals(n_outer):
    rows = []
    for place in range(n_outer):
        row = [0]
        for hop in range(1, n_outer):
            if place - hop >= 0:
                row.append(-hop)
            if place + hop < n_outer:
                row.append(hop)
        rows.append(row)
    return rows


def attention_kernel(n_chip, where_ref, order_ref, table_ref, q_ref, *refs):
    n_outer = n_chip // 2
    pieces, o_ref = refs[:-1], refs[-1]
    step = pl.program_id(0)
    head = pl.program_id(1)
    per_entry = n_chip // ENTRIES
    outer, side, core, asking = where_ref[0], where_ref[1], where_ref[2], where_ref[3]
    chip = outer * 2 + asking
    turn = jnp.where(step < 2, 0, core) + 2 * n_chip - chip
    columns = pl.ds(pl.multiple_of(head * HD, HD), HD)

    keys, values, usable = [], [], []
    for at, piece in enumerate(pieces):
        source_side = side if at < n_outer else 1 - side
        source = order_ref[outer, at % n_outer] * 2 + source_side
        ahead = lax.rem(source + turn, n_chip)
        row = table_ref[step, ahead // per_entry] & 3
        keys.append(piece[pl.ds(pl.multiple_of(row * QB, QB), QB), columns])
        values.append(piece[pl.ds(pl.multiple_of((4 + row) * QB, QB), QB), columns])
        usable.append(lax.rem(ahead, per_entry) == 0)
    keys = jnp.concatenate(keys, 0)
    values = jnp.concatenate(values, 0)

    scores = []
    for g in range(GROUP):
        s = lax.dot_general(
            q_ref[0, :, g * HD : (g + 1) * HD], keys, NT, preferred_element_type=jnp.float32
        )
        if per_entry > 1:
            s = jnp.concatenate(
                [
                    jnp.where(ok, s[:, at * QB : (at + 1) * QB], -1e30)
                    for at, ok in enumerate(usable)
                ],
                1,
            )
        scores.append(s)
    rounded, totals = [], []
    for s in scores:
        weights = jnp.exp2((s - jnp.max(s, axis=-1, keepdims=True)) * SCALE_LOG2)
        totals.append(jnp.sum(weights, axis=-1, keepdims=True))
        rounded.append(weights.astype(jnp.bfloat16))
    for g in range(GROUP):
        mixed = jnp.dot(rounded[g], values, preferred_element_type=jnp.float32)
        o_ref[0, :, g * HD : (g + 1) * HD] = (mixed / totals[g]).astype(jnp.bfloat16)


def attention(queries, where, order, table, pieces, n_chip):
    width = GROUP * HD
    blocks, _, columns = queries.shape
    rows = len(pieces) * QB
    whole = pl.BlockSpec(memory_space=pltpu.VMEM)
    tile = pl.BlockSpec((1, QB, width), lambda b, h, *_: (b, 0, h))
    return pl.pallas_call(
        functools.partial(attention_kernel, n_chip),
        out_shape=jax.ShapeDtypeStruct(queries.shape, jnp.bfloat16),
        grid_spec=pltpu.PrefetchScalarGridSpec(
            num_scalar_prefetch=3,
            grid=(blocks, columns // width),
            in_specs=[tile] + [whole] * len(pieces),
            out_specs=tile,
        ),
        compiler_params=pltpu.CompilerParams(vmem_limit_bytes=VMEM_LIMIT),
        cost_estimate=pl.CostEstimate(
            flops=4 * blocks * QB * rows * columns,
            bytes_accessed=2 * blocks * (rows * columns // 2 + 2 * QB * columns),
            transcendentals=blocks * QB * rows * columns // HD,
        ),
    )(where, order, table, queries, *pieces)


def project_kernel(where_ref, near_ref, across_ref, far_ref, far_across_ref, w_ref, o_ref, rows):
    side = where_ref[1]

    @pl.when((pl.program_id(0) == 0) & (pl.program_id(1) == 0))
    def _():
        width = near_ref.shape[-1]
        here = pl.ds(pl.multiple_of(side * width, width), width)
        there = pl.ds(pl.multiple_of((1 - side) * width, width), width)
        for block in range(2):
            even = slice(2 * block * QB, (2 * block + 1) * QB)
            odd = slice((2 * block + 1) * QB, (2 * block + 2) * QB)
            rows[even, here] = near_ref[block]
            rows[even, there] = across_ref[block]
            rows[odd, here] = far_ref[block]
            rows[odd, there] = far_across_ref[block]

    o_ref[...] = jnp.dot(
        rows[...], w_ref[0], preferred_element_type=jnp.float32
    ).astype(jnp.bfloat16)


def project(where, near, across, far, far_across, weights, tile=512):
    parts, depth, columns = weights.shape
    tiles = columns // tile
    half = pl.BlockSpec((2, QB, depth // 2), lambda p, t, *_: (0, 0, 0))
    return pl.pallas_call(
        project_kernel,
        out_shape=jax.ShapeDtypeStruct((4 * QB, parts * columns), jnp.bfloat16),
        grid_spec=pltpu.PrefetchScalarGridSpec(
            num_scalar_prefetch=1,
            grid=(parts, tiles),
            in_specs=[half] * 4 + [pl.BlockSpec((1, depth, tile), lambda p, t, *_: (p, 0, t))],
            out_specs=pl.BlockSpec((4 * QB, tile), lambda p, t, *_: (0, p * tiles + t)),
            scratch_shapes=[pltpu.VMEM((4 * QB, depth), jnp.bfloat16)],
        ),
        compiler_params=pltpu.CompilerParams(vmem_limit_bytes=VMEM_LIMIT),
        cost_estimate=pl.CostEstimate(
            flops=2 * 4 * QB * depth * parts * columns,
            bytes_accessed=2 * (depth * parts * columns + 4 * QB * (depth + parts * columns)),
            transcendentals=0,
        ),
    )(where, near, across, far, far_across, weights)


def body(n_groups, n_seq, queries, keys, values, block_table, out_weight):
    n_chip = n_seq // 2
    n_outer = n_chip // 2
    order_rows = arrivals(n_outer)

    def index(outer, side, core):
        return (outer * 2 + side) * 2 + core

    spots = [(o, s, c) for o in range(n_outer) for s in range(2) for c in range(2)]
    me = lax.axis_index("seq")
    group = lax.axis_index("groups")
    outer, side, core = me // 4, (me // 2) % 2, me % 2
    where = jnp.stack([outer, side, core, side]).astype(jnp.int32)
    where_across = jnp.stack([outer, side, core, 1 - side]).astype(jnp.int32)
    order = jnp.asarray(
        np.array([[p + d for d in row] for p, row in enumerate(order_rows)], np.int32)
    )

    def swap_core(array):
        return lax.ppermute(
            array, "seq", [(index(o, s, c), index(o, s, 1 - c)) for o, s, c in spots]
        )

    def swap_side(array):
        return lax.ppermute(
            array, "seq", [(index(o, s, c), index(o, 1 - s, c)) for o, s, c in spots]
        )

    def move(array, hop, way):
        return lax.ppermute(
            array,
            "seq",
            [
                (index(o, s, c), index(o + way, s, c))
                for o, s, c in spots
                if 0 <= o + way < n_outer and 0 <= o - (hop - 1) * way < n_outer
            ],
        )

    def line(array):
        got = {0: array}
        for hop in range(1, n_outer):
            for way in (1, -1):
                got[-way * hop] = move(got[-way * (hop - 1)], hop, way)
        return got

    def pick(got, k):
        wanted = [row[k] for row in order_rows]
        result = got[wanted[0]]
        for offset in sorted(set(wanted[1:])):
            mask = functools.reduce(
                jnp.logical_or, [outer == p for p in range(n_outer) if wanted[p] == offset]
            )
            if offset != wanted[0]:
                result = jnp.where(mask, got[offset], result)
        return result

    def after(array, *others):
        return lax.optimization_barrier((array, *others))[0]

    def half_of(array, which):
        width = array.shape[-1] // 2
        return lax.dynamic_slice_in_dim(array, which * width, width, array.ndim - 1)

    mine = jnp.concatenate([half_of(keys, side), half_of(values, side)], 0)
    theirs = jnp.concatenate([half_of(keys, 1 - side), half_of(values, 1 - side)], 0)
    theirs = swap_side(theirs)
    pieces = []
    for chain in (mine, theirs):
        got = line(chain)
        near = [got[0]]
        for k in range(1, n_outer):
            tied = {d: after(got[d], near[-1]) for d in sorted({row[k] for row in order_rows})}
            near.append(pick(tied, k))
        pieces += near

    part = out_weight.shape[1] // n_groups
    columns = lax.dynamic_slice_in_dim(out_weight, group * part, part, 1)
    gathered = lax.all_gather(columns, ("groups", "seq"), axis=0, tiled=True)
    gathered = gathered.reshape(n_groups, n_seq * out_weight.shape[0], part)

    query_blocks = queries.reshape(2, 2, QB, H * HD)
    far_queries = swap_core(query_blocks[:, 1])
    far_table = swap_core(block_table)
    table = jnp.concatenate([block_table[0::2], far_table[1::2]], 0)
    near_queries = query_blocks[:, 0]

    def my_blocks(which):
        return jnp.concatenate([half_of(near_queries, which), half_of(far_queries, which)], 0)

    across_queries = swap_side(my_blocks(1 - side))
    across_table = swap_side(table)

    across = attention(across_queries, where_across, order, across_table, pieces, n_chip)
    across = swap_side(across)
    near = attention(my_blocks(side), where, order, table, pieces, n_chip)
    far = swap_core(near[2:])
    far_across = swap_core(across[2:])
    return project(where, near, across, far, far_across, gathered)


def solution(mesh):
    in_specs = (
        P(("groups", "seq"), None),
        P(("groups", "seq"), None),
        P(("groups", "seq"), None),
        P(("groups", "seq"), None),
        P("seq", None),
    )
    out_specs = P(("groups", "seq"), None)
    run = functools.partial(body, mesh.shape["groups"], mesh.shape["seq"])
    return jax.shard_map(run, mesh=mesh, in_specs=in_specs, out_specs=out_specs, check_vma=False)
```

```python
import functools

import jax
import jax.numpy as jnp
import numpy as np
from jax import lax
from jax.experimental import pallas as pl
from jax.experimental.pallas import tpu as pltpu
from jax.sharding import Mesh
from jax.sharding import PartitionSpec as P

H = 16
KVH = 4
HD = 128
QB = 128
ENTRIES = 8
GROUP = H // KVH
SCALE_LOG2 = HD ** (-0.5) * 1.4426950408889634
NT = (((1,), (1,)), ((), ()))
VMEM_LIMIT = 40 * 1024 * 1024


def arrivals(n_outer):
    rows = []
    for place in range(n_outer):
        row = [0]
        for hop in range(1, n_outer):
            if place - hop >= 0:
                row.append(-hop)
            if place + hop < n_outer:
                row.append(hop)
        rows.append(row)
    return rows


def attention_kernel(n_chip, where_ref, order_ref, table_ref, q_ref, *refs):
    n_outer = n_chip // 2
    pieces, o_ref = refs[:-1], refs[-1]
    step = pl.program_id(0)
    head = pl.program_id(1)
    per_entry = n_chip // ENTRIES
    outer, side, core, asking = where_ref[0], where_ref[1], where_ref[2], where_ref[3]
    chip = outer * 2 + asking
    turn = jnp.where(step < 2, 0, core) + 2 * n_chip - chip
    columns = pl.ds(pl.multiple_of(head * HD, HD), HD)

    keys, values, usable = [], [], []
    for at, piece in enumerate(pieces):
        source_side = side if at < n_outer else 1 - side
        source = order_ref[outer, at % n_outer] * 2 + source_side
        ahead = lax.rem(source + turn, n_chip)
        row = table_ref[step, ahead // per_entry] & 3
        keys.append(piece[pl.ds(pl.multiple_of(row * QB, QB), QB), columns])
        values.append(piece[pl.ds(pl.multiple_of((4 + row) * QB, QB), QB), columns])
        usable.append(lax.rem(ahead, per_entry) == 0)
    keys = jnp.concatenate(keys, 0)
    values = jnp.concatenate(values, 0)

    scores = []
    for g in range(GROUP):
        s = lax.dot_general(
            q_ref[0, :, g * HD : (g + 1) * HD], keys, NT, preferred_element_type=jnp.float32
        )
        if per_entry > 1:
            s = jnp.concatenate(
                [
                    jnp.where(ok, s[:, at * QB : (at + 1) * QB], -1e30)
                    for at, ok in enumerate(usable)
                ],
                1,
            )
        scores.append(s)
    rounded, totals = [], []
    for s in scores:
        weights = jnp.exp2((s - jnp.max(s, axis=-1, keepdims=True)) * SCALE_LOG2)
        totals.append(jnp.sum(weights, axis=-1, keepdims=True))
        rounded.append(weights.astype(jnp.bfloat16))
    for g in range(GROUP):
        mixed = jnp.dot(rounded[g], values, preferred_element_type=jnp.float32)
        o_ref[0, :, g * HD : (g + 1) * HD] = (mixed / totals[g]).astype(jnp.bfloat16)


def attention(queries, where, order, table, pieces, n_chip):
    width = GROUP * HD
    blocks, _, columns = queries.shape
    rows = len(pieces) * QB
    whole = pl.BlockSpec(memory_space=pltpu.VMEM)
    tile = pl.BlockSpec((1, QB, width), lambda b, h, *_: (b, 0, h))
    return pl.pallas_call(
        functools.partial(attention_kernel, n_chip),
        out_shape=jax.ShapeDtypeStruct(queries.shape, jnp.bfloat16),
        grid_spec=pltpu.PrefetchScalarGridSpec(
            num_scalar_prefetch=3,
            grid=(blocks, columns // width),
            in_specs=[tile] + [whole] * len(pieces),
            out_specs=tile,
        ),
        compiler_params=pltpu.CompilerParams(vmem_limit_bytes=VMEM_LIMIT),
        cost_estimate=pl.CostEstimate(
            flops=4 * blocks * QB * rows * columns,
            bytes_accessed=2 * blocks * (rows * columns // 2 + 2 * QB * columns),
            transcendentals=blocks * QB * rows * columns // HD,
        ),
    )(where, order, table, queries, *pieces)


def project_kernel(
    n_outer, where_ref, near_ref, across_ref, far_ref, far_across_ref, w_ref, o_ref, rows
):
    side = where_ref[1]

    @pl.when((pl.program_id(0) == 0) & (pl.program_id(1) == 0))
    def _():
        heads = H // 2
        for block in range(2):
            even = slice(2 * block * QB, (2 * block + 1) * QB)
            odd = slice((2 * block + 1) * QB, (2 * block + 2) * QB)
            for which, even_ref, odd_ref in (
                (side, near_ref, far_ref),
                (1 - side, across_ref, far_across_ref),
            ):
                for h in range(heads):
                    at = slice(h * HD, (h + 1) * HD)
                    if n_outer:
                        to = (h % 4) * n_outer + h // 4 + which * (heads // 4)
                    else:
                        to = h + which * heads
                    to = pl.ds(pl.multiple_of(to * HD, HD), HD)
                    rows[even, to] = even_ref[block, :, at]
                    rows[odd, to] = odd_ref[block, :, at]

    o_ref[...] = jnp.dot(
        rows[...], w_ref[0], preferred_element_type=jnp.float32
    ).astype(jnp.bfloat16)


def project(n_outer, where, near, across, far, far_across, weights, tile=512):
    parts, depth, columns = weights.shape
    tiles = columns // tile
    half = pl.BlockSpec((2, QB, depth // 2), lambda p, t, *_: (0, 0, 0))
    return pl.pallas_call(
        functools.partial(project_kernel, n_outer),
        out_shape=jax.ShapeDtypeStruct((4 * QB, parts * columns), jnp.bfloat16),
        grid_spec=pltpu.PrefetchScalarGridSpec(
            num_scalar_prefetch=1,
            grid=(parts, tiles),
            in_specs=[half] * 4 + [pl.BlockSpec((1, depth, tile), lambda p, t, *_: (p, 0, t))],
            out_specs=pl.BlockSpec((4 * QB, tile), lambda p, t, *_: (0, p * tiles + t)),
            scratch_shapes=[pltpu.VMEM((4 * QB, depth), jnp.bfloat16)],
        ),
        compiler_params=pltpu.CompilerParams(vmem_limit_bytes=VMEM_LIMIT),
        cost_estimate=pl.CostEstimate(
            flops=2 * 4 * QB * depth * parts * columns,
            bytes_accessed=2 * (depth * parts * columns + 4 * QB * (depth + parts * columns)),
            transcendentals=0,
        ),
    )(where, near, across, far, far_across, weights)


LINE = "outer"
PLANE = ("groups", "side", "core")
SEQ = ("outer", "side", "core")


def body(n_groups, n_outer, queries, keys, values, block_table, out_weight):
    n_chip = n_outer * 2
    order_rows = arrivals(n_outer)

    def index(outer, side, core):
        return (outer * 2 + side) * 2 + core

    spots = [(o, s, c) for o in range(n_outer) for s in range(2) for c in range(2)]
    group = lax.axis_index("groups")
    outer, side, core = (lax.axis_index(name) for name in SEQ)
    where = jnp.stack([outer, side, core, side]).astype(jnp.int32)
    where_across = jnp.stack([outer, side, core, 1 - side]).astype(jnp.int32)
    order = jnp.asarray(
        np.array([[p + d for d in row] for p, row in enumerate(order_rows)], np.int32)
    )

    def swap_core(array):
        return lax.ppermute(
            array, SEQ, [(index(o, s, c), index(o, s, 1 - c)) for o, s, c in spots]
        )

    def swap_side(array):
        return lax.ppermute(
            array, SEQ, [(index(o, s, c), index(o, 1 - s, c)) for o, s, c in spots]
        )

    def move(array, hop, way):
        return lax.ppermute(
            array,
            SEQ,
            [
                (index(o, s, c), index(o + way, s, c))
                for o, s, c in spots
                if 0 <= o + way < n_outer and 0 <= o - (hop - 1) * way < n_outer
            ],
        )

    def line(array):
        got = {0: array}
        for hop in range(1, n_outer):
            for way in (1, -1):
                got[-way * hop] = move(got[-way * (hop - 1)], hop, way)
        return got

    def pick(got, k):
        wanted = [row[k] for row in order_rows]
        result = got[wanted[0]]
        for offset in sorted(set(wanted[1:])):
            mask = functools.reduce(
                jnp.logical_or, [outer == p for p in range(n_outer) if wanted[p] == offset]
            )
            if offset != wanted[0]:
                result = jnp.where(mask, got[offset], result)
        return result

    def after(array, *others):
        return lax.optimization_barrier((array, *others))[0]

    def half_of(array, which):
        width = array.shape[-1] // 2
        return lax.dynamic_slice_in_dim(array, which * width, width, array.ndim - 1)

    part = out_weight.shape[1] // n_groups
    columns = lax.dynamic_slice_in_dim(out_weight, group * part, part, 1)
    gathered = lax.all_gather(columns, LINE, axis=0, tiled=True)

    mine = jnp.concatenate([half_of(keys, side), half_of(values, side)], 0)
    theirs = jnp.concatenate([half_of(keys, 1 - side), half_of(values, 1 - side)], 0)
    theirs = swap_side(theirs)

    query_blocks = queries.reshape(2, 2, QB, H * HD)
    far_queries = swap_core(query_blocks[:, 1])
    far_table = swap_core(block_table)
    table = jnp.concatenate([block_table[0::2], far_table[1::2]], 0)
    near_queries = query_blocks[:, 0]

    def my_blocks(which):
        return jnp.concatenate([half_of(near_queries, which), half_of(far_queries, which)], 0)

    across_queries = swap_side(my_blocks(1 - side))
    across_table = swap_side(table)

    gathered = after(gathered, theirs, across_queries, across_table)
    mine, theirs = after(mine, gathered), after(theirs, gathered)
    gathered = lax.all_gather(gathered, PLANE, axis=0, tiled=True)
    held = out_weight.shape[0]
    order_of_rows = n_outer
    if held != HD:
        gathered = gathered.reshape(n_groups, 2, 2, n_outer, held, part)
        gathered = jnp.transpose(gathered, (0, 3, 1, 2, 4, 5))
        order_of_rows = 0
    gathered = gathered.reshape(n_groups, H * HD, part)

    pieces = []
    for chain in (mine, theirs):
        got = line(chain)
        near = [got[0]]
        for k in range(1, n_outer):
            tied = {d: after(got[d], near[-1]) for d in sorted({row[k] for row in order_rows})}
            near.append(pick(tied, k))
        pieces += near

    across = attention(across_queries, where_across, order, across_table, pieces, n_chip)
    across = swap_side(across)
    near = attention(my_blocks(side), where, order, table, pieces, n_chip)
    far = swap_core(near[2:])
    far_across = swap_core(across[2:])
    return project(order_of_rows, where, near, across, far, far_across, gathered)


def solution(mesh):
    n_groups, n_seq = mesh.shape["groups"], mesh.shape["seq"]
    n_outer = n_seq // 4
    split = Mesh(mesh.devices.reshape(n_groups, n_outer, 2, 2), ("groups", *SEQ))
    rows = P(("groups", *SEQ), None)
    in_specs = (rows, rows, rows, rows, P(SEQ, None))
    run = functools.partial(body, n_groups, n_outer)
    return jax.shard_map(run, mesh=split, in_specs=in_specs, out_specs=rows, check_vma=False)
```

```python
import functools

import jax
import jax.numpy as jnp
import numpy as np
from jax import lax
from jax.experimental import pallas as pl
from jax.experimental.pallas import tpu as pltpu
from jax.sharding import Mesh
from jax.sharding import PartitionSpec as P

H = 16
KVH = 4
HD = 128
QB = 128
ENTRIES = 8
GROUP = H // KVH
SCALE_LOG2 = HD ** (-0.5) * 1.4426950408889634
NT = (((1,), (1,)), ((), ()))
VMEM_LIMIT = 40 * 1024 * 1024


def arrivals(n_outer):
    rows = []
    for place in range(n_outer):
        row = [0]
        for hop in range(1, n_outer):
            if place - hop >= 0:
                row.append(-hop)
            if place + hop < n_outer:
                row.append(hop)
        rows.append(row)
    return rows


def attention_kernel(n_chip, where_ref, order_ref, table_ref, q_ref, *refs):
    n_outer = n_chip // 2
    pieces, o_ref = refs[:-1], refs[-1]
    step = pl.program_id(0)
    head = pl.program_id(1)
    per_entry = n_chip // ENTRIES
    outer, side, core, asking = where_ref[0], where_ref[1], where_ref[2], where_ref[3]
    chip = outer * 2 + asking
    turn = jnp.where(step < 2, 0, core) + 2 * n_chip - chip
    columns = pl.ds(pl.multiple_of(head * HD, HD), HD)

    keys, values, usable = [], [], []
    for at, piece in enumerate(pieces):
        source_side = side if at < n_outer else 1 - side
        source = order_ref[outer, at % n_outer] * 2 + source_side
        ahead = lax.rem(source + turn, n_chip)
        row = table_ref[step, ahead // per_entry] & 3
        keys.append(piece[pl.ds(pl.multiple_of(row * QB, QB), QB), columns])
        values.append(piece[pl.ds(pl.multiple_of((4 + row) * QB, QB), QB), columns])
        usable.append(lax.rem(ahead, per_entry) == 0)
    keys = jnp.concatenate(keys, 0)
    values = jnp.concatenate(values, 0)

    scores = []
    for g in range(GROUP):
        s = lax.dot_general(
            q_ref[0, :, g * HD : (g + 1) * HD], keys, NT, preferred_element_type=jnp.float32
        )
        if per_entry > 1:
            s = jnp.concatenate(
                [
                    jnp.where(ok, s[:, at * QB : (at + 1) * QB], -1e30)
                    for at, ok in enumerate(usable)
                ],
                1,
            )
        scores.append(s)
    rounded, totals = [], []
    for s in scores:
        weights = jnp.exp2((s - jnp.max(s, axis=-1, keepdims=True)) * SCALE_LOG2)
        totals.append(jnp.sum(weights, axis=-1, keepdims=True))
        rounded.append(weights.astype(jnp.bfloat16))
    for g in range(GROUP):
        mixed = jnp.dot(rounded[g], values, preferred_element_type=jnp.float32)
        o_ref[0, :, g * HD : (g + 1) * HD] = (mixed / totals[g]).astype(jnp.bfloat16)


def attention(queries, where, order, table, pieces, n_chip):
    width = GROUP * HD
    blocks, _, columns = queries.shape
    rows = len(pieces) * QB
    whole = pl.BlockSpec(memory_space=pltpu.VMEM)
    tile = pl.BlockSpec((1, QB, width), lambda b, h, *_: (b, 0, h))
    return pl.pallas_call(
        functools.partial(attention_kernel, n_chip),
        out_shape=jax.ShapeDtypeStruct(queries.shape, jnp.bfloat16),
        grid_spec=pltpu.PrefetchScalarGridSpec(
            num_scalar_prefetch=3,
            grid=(blocks, columns // width),
            in_specs=[tile] + [whole] * len(pieces),
            out_specs=tile,
        ),
        compiler_params=pltpu.CompilerParams(vmem_limit_bytes=VMEM_LIMIT),
        cost_estimate=pl.CostEstimate(
            flops=4 * blocks * QB * rows * columns,
            bytes_accessed=2 * blocks * (rows * columns // 2 + 2 * QB * columns),
            transcendentals=blocks * QB * rows * columns // HD,
        ),
    )(where, order, table, queries, *pieces)


def project_kernel(
    n_outer, where_ref, near_ref, across_ref, far_ref, far_across_ref, w_ref, o_ref, rows
):
    side = where_ref[1]

    @pl.when((pl.program_id(0) == 0) & (pl.program_id(1) == 0))
    def _():
        heads = H // 2
        for block in range(2):
            even = slice(2 * block * QB, (2 * block + 1) * QB)
            odd = slice((2 * block + 1) * QB, (2 * block + 2) * QB)
            for which, even_ref, odd_ref in (
                (side, near_ref, far_ref),
                (1 - side, across_ref, far_across_ref),
            ):
                for h in range(heads):
                    at = slice(h * HD, (h + 1) * HD)
                    if n_outer:
                        to = (h % 4) * n_outer + h // 4 + which * (heads // 4)
                    else:
                        to = h + which * heads
                    to = pl.ds(pl.multiple_of(to * HD, HD), HD)
                    rows[even, to] = even_ref[block, :, at]
                    rows[odd, to] = odd_ref[block, :, at]

    o_ref[...] = jnp.dot(
        rows[...], w_ref[0], preferred_element_type=jnp.float32
    ).astype(jnp.bfloat16)


def project(n_outer, where, near, across, far, far_across, weights, tile=512):
    parts, depth, columns = weights.shape
    tiles = columns // tile
    half = pl.BlockSpec((2, QB, depth // 2), lambda p, t, *_: (0, 0, 0))
    return pl.pallas_call(
        functools.partial(project_kernel, n_outer),
        out_shape=jax.ShapeDtypeStruct((4 * QB, parts * columns), jnp.bfloat16),
        grid_spec=pltpu.PrefetchScalarGridSpec(
            num_scalar_prefetch=1,
            grid=(parts, tiles),
            in_specs=[half] * 4 + [pl.BlockSpec((1, depth, tile), lambda p, t, *_: (p, 0, t))],
            out_specs=pl.BlockSpec((4 * QB, tile), lambda p, t, *_: (0, p * tiles + t)),
            scratch_shapes=[pltpu.VMEM((4 * QB, depth), jnp.bfloat16)],
        ),
        compiler_params=pltpu.CompilerParams(vmem_limit_bytes=VMEM_LIMIT),
        cost_estimate=pl.CostEstimate(
            flops=2 * 4 * QB * depth * parts * columns,
            bytes_accessed=2 * (depth * parts * columns + 4 * QB * (depth + parts * columns)),
            transcendentals=0,
        ),
    )(where, near, across, far, far_across, weights)


LINE = "outer"
PLANE = ("groups", "side", "core")
SEQ = ("outer", "side", "core")


def body(n_groups, n_outer, queries, keys, values, block_table, out_weight):
    n_chip = n_outer * 2
    order_rows = arrivals(n_outer)

    def index(outer, side, core):
        return (outer * 2 + side) * 2 + core

    spots = [(o, s, c) for o in range(n_outer) for s in range(2) for c in range(2)]
    group = lax.axis_index("groups")
    outer, side, core = (lax.axis_index(name) for name in SEQ)
    where = jnp.stack([outer, side, core, side]).astype(jnp.int32)
    where_across = jnp.stack([outer, side, core, 1 - side]).astype(jnp.int32)
    order = jnp.asarray(
        np.array([[p + d for d in row] for p, row in enumerate(order_rows)], np.int32)
    )

    def swap_core(array):
        return lax.ppermute(
            array, SEQ, [(index(o, s, c), index(o, s, 1 - c)) for o, s, c in spots]
        )

    def swap_side(array):
        return lax.ppermute(
            array, SEQ, [(index(o, s, c), index(o, 1 - s, c)) for o, s, c in spots]
        )

    def move(array, hop, way):
        return lax.ppermute(
            array,
            SEQ,
            [
                (index(o, s, c), index(o + way, s, c))
                for o, s, c in spots
                if 0 <= o + way < n_outer and 0 <= o - (hop - 1) * way < n_outer
            ],
        )

    def after(array, *others):
        return lax.optimization_barrier((array, *others))[0]

    def line(array, gates={}):
        got = {0: array}
        for hop in range(1, n_outer):
            for way in (1, -1):
                sent = got[-way * (hop - 1)]
                if hop in gates:
                    sent = after(sent, *gates[hop])
                got[-way * hop] = move(sent, hop, way)
        return got

    def pick(got, k):
        wanted = [row[k] for row in order_rows]
        result = got[wanted[0]]
        for offset in sorted(set(wanted[1:])):
            mask = functools.reduce(
                jnp.logical_or, [outer == p for p in range(n_outer) if wanted[p] == offset]
            )
            if offset != wanted[0]:
                result = jnp.where(mask, got[offset], result)
        return result

    def half_of(array, which):
        width = array.shape[-1] // 2
        return lax.dynamic_slice_in_dim(array, which * width, width, array.ndim - 1)

    query_blocks = queries.reshape(2, 2, QB, H * HD)
    far_queries = swap_core(query_blocks[:, 1])
    far_table = swap_core(block_table)
    table = jnp.concatenate([block_table[0::2], far_table[1::2]], 0)
    near_queries = query_blocks[:, 0]

    def my_blocks(which):
        return jnp.concatenate([half_of(near_queries, which), half_of(far_queries, which)], 0)

    sent_queries = my_blocks(1 - side)

    mine = jnp.concatenate([half_of(keys, side), half_of(values, side)], 0)
    theirs = jnp.concatenate([half_of(keys, 1 - side), half_of(values, 1 - side)], 0)
    theirs = swap_side(theirs)

    part = out_weight.shape[1] // n_groups
    columns = lax.dynamic_slice_in_dim(out_weight, group * part, part, 1)
    held = out_weight.shape[0]
    strip = held // 2
    gates = {2: (far_queries, far_table), 3: (theirs, mine, sent_queries, table)}
    strips = [line(columns[:strip], gates), line(columns[strip:], gates)]

    across_queries = swap_side(after(sent_queries, theirs))
    across_table = swap_side(table)

    gathered = jnp.zeros((n_outer * held, part), columns.dtype)
    for k in range(n_outer):
        for at, got in enumerate(strips):
            rows = (order[outer, k] * 2 + at) * strip
            piece = pick({d: after(got[d], gathered) for d in {row[k] for row in order_rows}}, k)
            gathered = lax.dynamic_update_slice_in_dim(gathered, piece, rows, 0)

    ends = (1 - n_outer, n_outer - 1)
    mine = after(mine, *[strips[0][d] for d in ends])
    theirs = after(theirs, *[strips[1][d] for d in ends])
    gathered = lax.all_gather(gathered, PLANE, axis=0, tiled=True)
    order_of_rows = n_outer
    if held != HD:
        gathered = gathered.reshape(n_groups, 2, 2, n_outer, held, part)
        gathered = jnp.transpose(gathered, (0, 3, 1, 2, 4, 5))
        order_of_rows = 0
    gathered = gathered.reshape(n_groups, H * HD, part)

    pieces = []
    for chain in (mine, theirs):
        got = line(chain, {2: (across_queries, across_table)})
        near = [got[0]]
        for k in range(1, n_outer):
            tied = {d: after(got[d], near[-1]) for d in sorted({row[k] for row in order_rows})}
            near.append(pick(tied, k))
        pieces += near

    across = attention(across_queries, where_across, order, across_table, pieces, n_chip)
    across = swap_side(across)
    near = attention(my_blocks(side), where, order, table, pieces, n_chip)
    far = swap_core(near[2:])
    far_across = swap_core(across[2:])
    return project(order_of_rows, where, near, across, far, far_across, gathered)


def solution(mesh):
    n_groups, n_seq = mesh.shape["groups"], mesh.shape["seq"]
    n_outer = n_seq // 4
    split = Mesh(mesh.devices.reshape(n_groups, n_outer, 2, 2), ("groups", *SEQ))
    rows = P(("groups", *SEQ), None)
    in_specs = (rows, rows, rows, rows, P(SEQ, None))
    run = functools.partial(body, n_groups, n_outer)
    return jax.shard_map(run, mesh=split, in_specs=in_specs, out_specs=rows, check_vma=False)
```

```python
import functools

import jax
import jax.numpy as jnp
import numpy as np
from jax import lax
from jax.experimental import pallas as pl
from jax.experimental.pallas import tpu as pltpu
from jax.sharding import Mesh
from jax.sharding import PartitionSpec as P

H = 16
KVH = 4
HD = 128
QB = 128
ENTRIES = 8
GROUP = H // KVH
SCALE_LOG2 = HD ** (-0.5) * 1.4426950408889634
NT = (((1,), (1,)), ((), ()))
VMEM_LIMIT = 40 * 1024 * 1024
PROJECT_TILE = 512


def arrivals(n_outer):
    rows = []
    for place in range(n_outer):
        row = [0]
        for hop in range(1, n_outer):
            if place - hop >= 0:
                row.append(-hop)
            if place + hop < n_outer:
                row.append(hop)
        rows.append(row)
    return rows


def attention_kernel(n_chip, slots, first, last, where_ref, order_ref, table_ref, q_ref, *refs):
    count = 2 * len(slots)
    pieces = refs[:count]
    before, after = ((), refs[count:]) if first else (refs[count : count + 2], refs[count + 2 :])
    step = pl.program_id(0)
    head = pl.program_id(1)
    per_entry = n_chip // ENTRIES
    outer, side, core, asking = where_ref[0], where_ref[1], where_ref[2], where_ref[3]
    turn = jnp.where(step < 2, 0, core) + 2 * n_chip - (outer * 2 + asking)
    columns = pl.ds(pl.multiple_of(head * HD, HD), HD)

    keys, values, usable = [], [], []
    for at, piece in enumerate(pieces):
        source_side = side if at < len(slots) else 1 - side
        source = order_ref[outer, slots[at % len(slots)]] * 2 + source_side
        ahead = lax.rem(source + turn, n_chip)
        row = table_ref[step, ahead // per_entry] & 3
        keys.append(piece[pl.ds(pl.multiple_of(row * QB, QB), QB), columns])
        values.append(piece[pl.ds(pl.multiple_of((4 + row) * QB, QB), QB), columns])
        usable.append(lax.rem(ahead, per_entry) == 0)
    keys = jnp.concatenate(keys, 0)
    values = jnp.concatenate(values, 0)

    scores = []
    for g in range(GROUP):
        s = lax.dot_general(
            q_ref[0, :, g * HD : (g + 1) * HD], keys, NT, preferred_element_type=jnp.float32
        )
        if per_entry > 1:
            s = jnp.concatenate(
                [
                    jnp.where(ok, s[:, at * QB : (at + 1) * QB], -1e30)
                    for at, ok in enumerate(usable)
                ],
                1,
            )
        scores.append(s)
    rounded, totals, highs, factors = [], [], [], []
    for g, s in enumerate(scores):
        high = jnp.max(s, axis=-1, keepdims=True)
        if not first:
            known = before[1][0, :, g * HD : g * HD + 1]
            high = jnp.maximum(high, known)
            factors.append(jnp.exp2((known - high) * SCALE_LOG2))
        weights = jnp.exp2((s - high) * SCALE_LOG2)
        total = jnp.sum(weights, axis=-1, keepdims=True)
        if not first:
            total += before[1][0, :, g * HD + HD // 2 : g * HD + HD // 2 + 1] * factors[g]
        highs.append(high)
        totals.append(total)
        rounded.append(weights.astype(jnp.bfloat16))
    left = lax.broadcasted_iota(jnp.int32, (QB, HD), 1) < HD // 2
    for g in range(GROUP):
        at = slice(g * HD, (g + 1) * HD)
        mixed = jnp.dot(rounded[g], values, preferred_element_type=jnp.float32)
        if not first:
            mixed += before[0][0, :, at] * factors[g]
        if last:
            after[0][0, :, at] = (mixed / totals[g]).astype(jnp.bfloat16)
        else:
            after[0][0, :, at] = mixed
            after[1][0, :, at] = jnp.where(left, highs[g], totals[g])


def attention(queries, where, order, table, pieces, slots, n_chip, state=None, last=True):
    width = GROUP * HD
    blocks, _, columns = queries.shape
    rows = len(pieces) * QB
    whole = pl.BlockSpec(memory_space=pltpu.VMEM)
    tile = pl.BlockSpec((1, QB, width), lambda b, h, *_: (b, 0, h))
    state_shape = jax.ShapeDtypeStruct(queries.shape, jnp.float32)
    done_shape = jax.ShapeDtypeStruct(queries.shape, jnp.bfloat16)
    return pl.pallas_call(
        functools.partial(attention_kernel, n_chip, slots, state is None, last),
        out_shape=done_shape if last else (state_shape, state_shape),
        grid_spec=pltpu.PrefetchScalarGridSpec(
            num_scalar_prefetch=3,
            grid=(blocks, columns // width),
            in_specs=[tile] + [whole] * len(pieces) + [tile] * (0 if state is None else 2),
            out_specs=tile if last else (tile, tile),
        ),
        compiler_params=pltpu.CompilerParams(vmem_limit_bytes=VMEM_LIMIT),
        cost_estimate=pl.CostEstimate(
            flops=4 * blocks * QB * rows * columns,
            bytes_accessed=2 * blocks * (rows * columns // 2 + 6 * QB * columns),
            transcendentals=blocks * QB * rows * columns // HD,
        ),
    )(where, order, table, queries, *pieces, *(state or ()))


def lay_out_kernel(n_outer, where_ref, near_ref, across_ref, far_ref, far_across_ref, rows):
    side = where_ref[1]
    heads = H // 2
    for block in range(2):
        even = slice(2 * block * QB, (2 * block + 1) * QB)
        odd = slice((2 * block + 1) * QB, (2 * block + 2) * QB)
        for which, even_ref, odd_ref in (
            (side, near_ref, far_ref),
            (1 - side, across_ref, far_across_ref),
        ):
            for h in range(heads):
                at = slice(h * HD, (h + 1) * HD)
                if n_outer:
                    to = (h % 4) * n_outer + h // 4 + which * (heads // 4)
                else:
                    to = h + which * heads
                to = pl.ds(pl.multiple_of(to * HD, HD), HD)
                rows[even, to] = even_ref[block, :, at]
                rows[odd, to] = odd_ref[block, :, at]


def lay_out(n_outer, where, near, across, far, far_across):
    half = pl.BlockSpec((2, QB, near.shape[-1]), lambda i, *_: (0, 0, 0))
    return pl.pallas_call(
        functools.partial(lay_out_kernel, n_outer),
        out_shape=jax.ShapeDtypeStruct((4 * QB, H * HD), jnp.bfloat16),
        grid_spec=pltpu.PrefetchScalarGridSpec(
            num_scalar_prefetch=1,
            grid=(1,),
            in_specs=[half] * 4,
            out_specs=pl.BlockSpec((4 * QB, H * HD), lambda i, *_: (0, 0)),
        ),
        compiler_params=pltpu.CompilerParams(vmem_limit_bytes=VMEM_LIMIT),
    )(where, near, across, far, far_across)


def project_kernel(rows_ref, w_ref, o_ref):
    o_ref[...] = jnp.dot(
        rows_ref[...], w_ref[0], preferred_element_type=jnp.float32
    ).astype(jnp.bfloat16)


def project(rows, weights, tile=PROJECT_TILE):
    parts, depth, columns = weights.shape
    tiles = columns // tile
    return pl.pallas_call(
        project_kernel,
        out_shape=jax.ShapeDtypeStruct((rows.shape[0], parts * columns), jnp.bfloat16),
        grid_spec=pl.GridSpec(
            grid=(parts, tiles),
            in_specs=[
                pl.BlockSpec(rows.shape, lambda p, t: (0, 0)),
                pl.BlockSpec((1, depth, tile), lambda p, t: (p, 0, t)),
            ],
            out_specs=pl.BlockSpec((rows.shape[0], tile), lambda p, t: (0, p * tiles + t)),
        ),
        compiler_params=pltpu.CompilerParams(vmem_limit_bytes=VMEM_LIMIT),
        cost_estimate=pl.CostEstimate(
            flops=2 * rows.shape[0] * depth * parts * columns,
            bytes_accessed=2 * (depth * parts * columns + rows.shape[0] * (depth + parts * columns)),
            transcendentals=0,
        ),
    )(rows, weights)


LINE = "outer"
PLANE = ("groups", "side", "core")
SEQ = ("outer", "side", "core")


def body(n_groups, n_outer, queries, keys, values, block_table, out_weight):
    n_chip = n_outer * 2
    order_rows = arrivals(n_outer)

    def index(outer, side, core):
        return (outer * 2 + side) * 2 + core

    spots = [(o, s, c) for o in range(n_outer) for s in range(2) for c in range(2)]
    group = lax.axis_index("groups")
    outer, side, core = (lax.axis_index(name) for name in SEQ)
    where = jnp.stack([outer, side, core, side]).astype(jnp.int32)
    where_across = jnp.stack([outer, side, core, 1 - side]).astype(jnp.int32)
    order = jnp.asarray(
        np.array([[p + d for d in row] for p, row in enumerate(order_rows)], np.int32)
    )

    def swap_core(array):
        return lax.ppermute(
            array, SEQ, [(index(o, s, c), index(o, s, 1 - c)) for o, s, c in spots]
        )

    def swap_side(array):
        return lax.ppermute(
            array, SEQ, [(index(o, s, c), index(o, 1 - s, c)) for o, s, c in spots]
        )

    def move(array, hop, way):
        return lax.ppermute(
            array,
            SEQ,
            [
                (index(o, s, c), index(o + way, s, c))
                for o, s, c in spots
                if 0 <= o + way < n_outer and 0 <= o - (hop - 1) * way < n_outer
            ],
        )

    def after(array, *others):
        return lax.optimization_barrier((array, *others))[0]

    def line(array, gates={}):
        got = {0: array}
        for hop in range(1, n_outer):
            for way in (1, -1):
                sent = got[-way * (hop - 1)]
                if hop in gates:
                    sent = after(sent, *gates[hop])
                got[-way * hop] = move(sent, hop, way)
        return got

    def pick(got, k):
        wanted = [row[k] for row in order_rows]
        result = got[wanted[0]]
        for offset in sorted(set(wanted[1:])):
            mask = functools.reduce(
                jnp.logical_or, [outer == p for p in range(n_outer) if wanted[p] == offset]
            )
            if offset != wanted[0]:
                result = jnp.where(mask, got[offset], result)
        return result

    def half_of(array, which):
        width = array.shape[-1] // 2
        return lax.dynamic_slice_in_dim(array, which * width, width, array.ndim - 1)

    part = out_weight.shape[1] // n_groups
    columns = lax.dynamic_slice_in_dim(out_weight, group * part, part, 1)
    gathered = lax.all_gather(columns, LINE, axis=0, tiled=True)

    mine = jnp.concatenate([half_of(keys, side), half_of(values, side)], 0)
    theirs = jnp.concatenate([half_of(keys, 1 - side), half_of(values, 1 - side)], 0)
    theirs = swap_side(theirs)

    query_blocks = queries.reshape(2, 2, QB, H * HD)
    far_queries = swap_core(query_blocks[:, 1])
    far_table = swap_core(block_table)
    table = jnp.concatenate([block_table[0::2], far_table[1::2]], 0)
    near_queries = query_blocks[:, 0]

    def my_blocks(which):
        return jnp.concatenate([half_of(near_queries, which), half_of(far_queries, which)], 0)

    across_queries = swap_side(my_blocks(1 - side))
    across_table = swap_side(table)

    gathered = after(gathered, theirs, across_queries, across_table)
    gates = ({2: (gathered,)}, {1: (gathered,)})
    gathered = lax.all_gather(gathered, PLANE, axis=0, tiled=True)
    held = out_weight.shape[0]
    order_of_rows = n_outer
    if held != HD:
        gathered = gathered.reshape(n_groups, 2, 2, n_outer, held, part)
        gathered = jnp.transpose(gathered, (0, 3, 1, 2, 4, 5))
        order_of_rows = 0
    gathered = gathered.reshape(n_groups, H * HD, part)

    early, late = [], []
    for chain, gate in zip((mine, theirs), gates):
        got = line(chain, gate)
        near = [got[0]]
        for k in range(1, n_outer):
            tied = {d: after(got[d], near[-1]) for d in sorted({row[k] for row in order_rows})}
            near.append(pick(tied, k))
        early += near[:-1]
        late += near[-1:]

    asks = (
        (across_queries, where_across, order, across_table),
        (my_blocks(side), where, order, table),
    )
    slots = tuple(range(n_outer))
    states = [attention(*ask, early, slots[:-1], n_chip, last=False) for ask in asks]
    across, near = (
        attention(*ask, late, slots[-1:], n_chip, state) for ask, state in zip(asks, states)
    )
    across = swap_side(across)
    far = swap_core(near[2:])
    far_across = swap_core(across[2:])
    rows = lay_out(order_of_rows, where, near, across, far, far_across)
    return project(rows, gathered)


def solution(mesh):
    n_groups, n_seq = mesh.shape["groups"], mesh.shape["seq"]
    n_outer = n_seq // 4
    split = Mesh(mesh.devices.reshape(n_groups, n_outer, 2, 2), ("groups", *SEQ))
    rows = P(("groups", *SEQ), None)
    in_specs = (rows, rows, rows, rows, P(SEQ, None))
    run = functools.partial(body, n_groups, n_outer)
    return jax.shard_map(run, mesh=split, in_specs=in_specs, out_specs=rows, check_vma=False)
```

```python
import functools

import jax
import jax.numpy as jnp
import numpy as np
from jax import lax
from jax.experimental import pallas as pl
from jax.experimental.pallas import tpu as pltpu
from jax.sharding import Mesh
from jax.sharding import PartitionSpec as P

H = 16
KVH = 4
HD = 128
QB = 128
ENTRIES = 8
GROUP = H // KVH
SCALE_LOG2 = HD ** (-0.5) * 1.4426950408889634
NT = (((1,), (1,)), ((), ()))
VMEM_LIMIT = 40 * 1024 * 1024
PROJECT_TILE = 1024


def arrivals(n_outer):
    rows = []
    for place in range(n_outer):
        row = [0]
        for hop in range(1, n_outer):
            if place - hop >= 0:
                row.append(-hop)
            if place + hop < n_outer:
                row.append(hop)
        rows.append(row)
    return rows


def attention_kernel(n_chip, slots, first, last, where_ref, order_ref, table_ref, q_ref, *refs):
    count = 2 * len(slots)
    pieces = refs[:count]
    before, after = ((), refs[count:]) if first else (refs[count : count + 3], refs[count + 3 :])
    step = pl.program_id(0)
    per_entry = n_chip // ENTRIES
    outer, side, core, asking = where_ref[0], where_ref[1], where_ref[2], where_ref[3]
    turn = jnp.where(step < 2, 0, core) + 2 * n_chip - (outer * 2 + asking)

    starts, usable = [], []
    for at in range(count):
        source_side = side if at < len(slots) else 1 - side
        source = order_ref[outer, slots[at % len(slots)]] * 2 + source_side
        ahead = lax.rem(source + turn, n_chip)
        row = table_ref[step, ahead // per_entry] & 3
        starts.append(pl.multiple_of(row * QB, QB))
        usable.append(lax.rem(ahead, per_entry) == 0)

    def gather(head, base):
        columns = slice(head * HD, (head + 1) * HD)
        return jnp.concatenate(
            [
                piece[pl.ds(start + base, QB), columns]
                for piece, start in zip(pieces, starts)
            ],
            0,
        )

    def spread(column):
        return jnp.broadcast_to(column, (QB, HD))

    heads = q_ref.shape[-1] // HD
    scores = []
    for h in range(heads):
        if h % GROUP == 0:
            keys = gather(h // GROUP, 0)
        s = lax.dot_general(
            q_ref[0, :, h * HD : (h + 1) * HD], keys, NT, preferred_element_type=jnp.float32
        )
        if per_entry > 1:
            s = jnp.concatenate(
                [
                    jnp.where(ok, s[:, at * QB : (at + 1) * QB], -1e30)
                    for at, ok in enumerate(usable)
                ],
                1,
            )
        scores.append(s)
    rounded, totals, factors = [], [], []
    for h, s in enumerate(scores):
        lanes = slice(h * HD, (h + 1) * HD)
        high = spread(jnp.max(s, axis=-1, keepdims=True))
        if not first:
            known = before[1][0, :, lanes]
            high = jnp.maximum(high, known)
            factors.append(jnp.exp2((known - high) * SCALE_LOG2))
        if not last:
            after[1][0, :, lanes] = high
        weights = jnp.exp2((s - jnp.concatenate([high] * count, 1)) * SCALE_LOG2)
        total = spread(jnp.sum(weights, axis=-1, keepdims=True))
        if not first:
            total += before[2][0, :, lanes] * factors[h]
        if not last:
            after[2][0, :, lanes] = total
        totals.append(total)
        rounded.append(weights.astype(jnp.bfloat16))
    for h in range(heads):
        lanes = slice(h * HD, (h + 1) * HD)
        if h % GROUP == 0:
            values = gather(h // GROUP, 4 * QB)
        mixed = jnp.dot(rounded[h], values, preferred_element_type=jnp.float32)
        if not first:
            mixed += before[0][0, :, lanes] * factors[h]
        if last:
            after[0][0, :, lanes] = (mixed / totals[h]).astype(jnp.bfloat16)
        else:
            after[0][0, :, lanes] = mixed


def attention(queries, where, order, table, pieces, slots, n_chip, state=(), last=True):
    blocks, _, columns = queries.shape
    rows = len(pieces) * QB
    whole = pl.BlockSpec(memory_space=pltpu.VMEM)
    tile = pl.BlockSpec((1, QB, columns), lambda b, *_: (b, 0, 0))
    state_shape = jax.ShapeDtypeStruct(queries.shape, jnp.float32)
    done_shape = jax.ShapeDtypeStruct(queries.shape, jnp.bfloat16)
    return pl.pallas_call(
        functools.partial(attention_kernel, n_chip, slots, not state, last),
        out_shape=done_shape if last else (state_shape,) * 3,
        grid_spec=pltpu.PrefetchScalarGridSpec(
            num_scalar_prefetch=3,
            grid=(blocks,),
            in_specs=[tile] + [whole] * len(pieces) + [tile] * len(state),
            out_specs=tile if last else (tile,) * 3,
        ),
        compiler_params=pltpu.CompilerParams(vmem_limit_bytes=VMEM_LIMIT),
        cost_estimate=pl.CostEstimate(
            flops=4 * blocks * QB * rows * columns,
            bytes_accessed=2 * blocks * (rows * columns // 2 + 6 * QB * columns),
            transcendentals=blocks * QB * rows * columns // HD,
        ),
    )(where, order, table, queries, *pieces, *state)


def lay_out_kernel(n_outer, where_ref, near_ref, across_ref, far_ref, far_across_ref, rows):
    side = where_ref[1]
    heads = H // 2
    for block in range(2):
        even = slice(2 * block * QB, (2 * block + 1) * QB)
        odd = slice((2 * block + 1) * QB, (2 * block + 2) * QB)
        for which, even_ref, odd_ref in (
            (side, near_ref, far_ref),
            (1 - side, across_ref, far_across_ref),
        ):
            for h in range(heads):
                at = slice(h * HD, (h + 1) * HD)
                if n_outer:
                    to = (h % 4) * n_outer + h // 4 + which * (heads // 4)
                else:
                    to = h + which * heads
                to = pl.ds(pl.multiple_of(to * HD, HD), HD)
                rows[even, to] = even_ref[block, :, at]
                rows[odd, to] = odd_ref[block, :, at]


def lay_out(n_outer, where, near, across, far, far_across):
    half = pl.BlockSpec((2, QB, near.shape[-1]), lambda i, *_: (0, 0, 0))
    return pl.pallas_call(
        functools.partial(lay_out_kernel, n_outer),
        out_shape=jax.ShapeDtypeStruct((4 * QB, H * HD), jnp.bfloat16),
        grid_spec=pltpu.PrefetchScalarGridSpec(
            num_scalar_prefetch=1,
            grid=(1,),
            in_specs=[half] * 4,
            out_specs=pl.BlockSpec((4 * QB, H * HD), lambda i, *_: (0, 0)),
        ),
        compiler_params=pltpu.CompilerParams(vmem_limit_bytes=VMEM_LIMIT),
    )(where, near, across, far, far_across)


def project_kernel(rows_ref, w_ref, o_ref):
    o_ref[...] = jnp.dot(
        rows_ref[...], w_ref[0], preferred_element_type=jnp.float32
    ).astype(jnp.bfloat16)


def project(rows, weights, tile=PROJECT_TILE):
    parts, depth, columns = weights.shape
    tiles = columns // tile
    return pl.pallas_call(
        project_kernel,
        out_shape=jax.ShapeDtypeStruct((rows.shape[0], parts * columns), jnp.bfloat16),
        grid_spec=pl.GridSpec(
            grid=(parts, tiles),
            in_specs=[
                pl.BlockSpec(rows.shape, lambda p, t: (0, 0)),
                pl.BlockSpec((1, depth, tile), lambda p, t: (p, 0, t)),
            ],
            out_specs=pl.BlockSpec((rows.shape[0], tile), lambda p, t: (0, p * tiles + t)),
        ),
        compiler_params=pltpu.CompilerParams(vmem_limit_bytes=VMEM_LIMIT),
        cost_estimate=pl.CostEstimate(
            flops=2 * rows.shape[0] * depth * parts * columns,
            bytes_accessed=2 * (depth * parts * columns + rows.shape[0] * (depth + parts * columns)),
            transcendentals=0,
        ),
    )(rows, weights)


LINE = "outer"
PLANE = ("groups", "side", "core")
SEQ = ("outer", "side", "core")


def body(n_groups, n_outer, queries, keys, values, block_table, out_weight):
    n_chip = n_outer * 2
    order_rows = arrivals(n_outer)

    def index(outer, side, core):
        return (outer * 2 + side) * 2 + core

    spots = [(o, s, c) for o in range(n_outer) for s in range(2) for c in range(2)]
    group = lax.axis_index("groups")
    outer, side, core = (lax.axis_index(name) for name in SEQ)
    where = jnp.stack([outer, side, core, side]).astype(jnp.int32)
    where_across = jnp.stack([outer, side, core, 1 - side]).astype(jnp.int32)
    order = jnp.asarray(
        np.array([[p + d for d in row] for p, row in enumerate(order_rows)], np.int32)
    )

    def swap_core(array):
        return lax.ppermute(
            array, SEQ, [(index(o, s, c), index(o, s, 1 - c)) for o, s, c in spots]
        )

    def swap_side(array):
        return lax.ppermute(
            array, SEQ, [(index(o, s, c), index(o, 1 - s, c)) for o, s, c in spots]
        )

    def move(array, hop, way):
        return lax.ppermute(
            array,
            SEQ,
            [
                (index(o, s, c), index(o + way, s, c))
                for o, s, c in spots
                if 0 <= o + way < n_outer and 0 <= o - (hop - 1) * way < n_outer
            ],
        )

    def after(array, *others):
        return lax.optimization_barrier((array, *others))[0]

    def line(array, gates={}, got={}):
        got = {0: array, **got}
        for hop in range(1, n_outer):
            for way in (1, -1):
                if -way * hop in got:
                    continue
                sent = got[-way * (hop - 1)]
                if hop in gates:
                    sent = after(sent, *gates[hop])
                got[-way * hop] = move(sent, hop, way)
        return got

    def pick(got, k):
        wanted = [row[k] for row in order_rows]
        result = got[wanted[0]]
        for offset in sorted(set(wanted[1:])):
            mask = functools.reduce(
                jnp.logical_or, [outer == p for p in range(n_outer) if wanted[p] == offset]
            )
            if offset != wanted[0]:
                result = jnp.where(mask, got[offset], result)
        return result

    def half_of(array, which):
        width = array.shape[-1] // 2
        return lax.dynamic_slice_in_dim(array, which * width, width, array.ndim - 1)

    part = out_weight.shape[1] // n_groups
    columns = lax.dynamic_slice_in_dim(out_weight, group * part, part, 1)
    gathered = lax.all_gather(columns, LINE, axis=0, tiled=True)

    mine = jnp.concatenate([half_of(keys, side), half_of(values, side)], 0)
    theirs = jnp.concatenate([half_of(keys, 1 - side), half_of(values, 1 - side)], 0)
    theirs = swap_side(theirs)

    query_blocks = queries.reshape(2, 2, QB, H * HD)
    far_queries = swap_core(query_blocks[:, 1])
    far_table = swap_core(block_table)
    table = jnp.concatenate([block_table[0::2], far_table[1::2]], 0)
    near_queries = query_blocks[:, 0]

    def my_blocks(which):
        return jnp.concatenate([half_of(near_queries, which), half_of(far_queries, which)], 0)

    across_queries = swap_side(my_blocks(1 - side))
    across_table = swap_side(table)

    hops = {-way: move(mine, 1, way) for way in (1, -1)}
    gathered = after(gathered, theirs, across_queries, across_table, *hops.values())
    gates = ({2: (gathered,)}, {1: (gathered,)})
    gathered = lax.all_gather(gathered, PLANE, axis=0, tiled=True)
    held = out_weight.shape[0]
    order_of_rows = n_outer
    if held != HD:
        gathered = gathered.reshape(n_groups, 2, 2, n_outer, held, part)
        gathered = jnp.transpose(gathered, (0, 3, 1, 2, 4, 5))
        order_of_rows = 0
    gathered = gathered.reshape(n_groups, H * HD, part)

    chains = [line(chain, gate, first) for chain, gate, first in zip((mine, theirs), gates, (hops, {}))]
    early, last = [], n_outer - 1
    for got in chains:
        near = [got[0]]
        for k in range(1, last):
            tied = {d: after(got[d], near[-1]) for d in sorted({row[k] for row in order_rows})}
            near.append(pick(tied, k))
        early += near

    asks = (
        (across_queries, where_across, order, across_table),
        (my_blocks(side), where, order, table),
    )
    states = [attention(*ask, early, tuple(range(last)), n_chip, last=False) for ask in asks]
    tie = [state[2] for state in states]
    late = [
        pick({d: after(got[d], *tie) for d in sorted({row[last] for row in order_rows})}, last)
        for got in chains
    ]
    across, near = (
        attention(*ask, late, (last,), n_chip, state) for ask, state in zip(asks, states)
    )
    across = swap_side(across)
    far = swap_core(near[2:])
    far_across = swap_core(across[2:])
    rows = lay_out(order_of_rows, where, near, across, far, far_across)
    return project(rows, gathered)


def solution(mesh):
    n_groups, n_seq = mesh.shape["groups"], mesh.shape["seq"]
    n_outer = n_seq // 4
    split = Mesh(mesh.devices.reshape(n_groups, n_outer, 2, 2), ("groups", *SEQ))
    rows = P(("groups", *SEQ), None)
    in_specs = (rows, rows, rows, rows, P(SEQ, None))
    run = functools.partial(body, n_groups, n_outer)
    return jax.shard_map(run, mesh=split, in_specs=in_specs, out_specs=rows, check_vma=False)
```

```python
import functools

import jax
import jax.numpy as jnp
import numpy as np
from jax import lax
from jax.experimental import pallas as pl
from jax.experimental.pallas import tpu as pltpu
from jax.sharding import Mesh
from jax.sharding import PartitionSpec as P

H = 16
KVH = 4
HD = 128
QB = 128
ENTRIES = 8
GROUP = H // KVH
SCALE_LOG2 = HD ** (-0.5) * 1.4426950408889634
NT = (((1,), (1,)), ((), ()))
VMEM_LIMIT = 40 * 1024 * 1024
PROJECT_TILE = 1024


def arrivals(n_outer):
    rows = []
    for place in range(n_outer):
        row = [0]
        for hop in range(1, n_outer):
            if place - hop >= 0:
                row.append(-hop)
            if place + hop < n_outer:
                row.append(hop)
        rows.append(row)
    return rows


def attention_kernel(n_chip, slots, first, last, where_ref, order_ref, table_ref, q_ref, *refs):
    pieces, refs = refs[: len(slots)], refs[len(slots) :]
    before, after = ((), refs) if first else (refs[:3], refs[3:])
    count = 2 * len(slots)
    step = pl.program_id(0)
    per_entry = n_chip // ENTRIES
    outer, side, core, asking = where_ref[0], where_ref[1], where_ref[2], where_ref[3]
    turn = jnp.where(step < 2, 0, core) + 2 * n_chip - (outer * 2 + asking)

    starts, usable = [], []
    for at in range(count):
        source_side = side if at < len(slots) else 1 - side
        source = order_ref[outer, slots[at % len(slots)]] * 2 + source_side
        ahead = lax.rem(source + turn, n_chip)
        row = table_ref[step, ahead // per_entry] & 3
        base = 0 if at < len(slots) else 8
        starts.append(pl.multiple_of((base + row) * QB, QB))
        usable.append(lax.rem(ahead, per_entry) == 0)

    def gather(base):
        return jnp.concatenate(
            [pieces[at % len(slots)][pl.ds(start + base, QB), :] for at, start in enumerate(starts)],
            0,
        )

    keys, values = gather(0), gather(4 * QB)

    def spread(column):
        return jnp.broadcast_to(column, (QB, HD))

    scores = []
    for h in range(GROUP):
        s = lax.dot_general(
            q_ref[0, :, h * HD : (h + 1) * HD], keys, NT, preferred_element_type=jnp.float32
        )
        if per_entry > 1:
            s = jnp.concatenate(
                [
                    jnp.where(ok, s[:, at * QB : (at + 1) * QB], -1e30)
                    for at, ok in enumerate(usable)
                ],
                1,
            )
        scores.append(s)
    rounded, totals, factors = [], [], []
    for h, s in enumerate(scores):
        lanes = slice(h * HD, (h + 1) * HD)
        high = spread(jnp.max(s, axis=-1, keepdims=True))
        if not first:
            known = before[1][0, :, lanes]
            high = jnp.maximum(high, known)
            factors.append(jnp.exp2((known - high) * SCALE_LOG2))
        if not last:
            after[1][0, :, lanes] = high
        weights = jnp.exp2((s - jnp.concatenate([high] * count, 1)) * SCALE_LOG2)
        total = spread(jnp.sum(weights, axis=-1, keepdims=True))
        if not first:
            total += before[2][0, :, lanes] * factors[h]
        if not last:
            after[2][0, :, lanes] = total
        totals.append(total)
        rounded.append(weights.astype(jnp.bfloat16))
    for h in range(GROUP):
        lanes = slice(h * HD, (h + 1) * HD)
        mixed = jnp.dot(rounded[h], values, preferred_element_type=jnp.float32)
        if not first:
            mixed += before[0][0, :, lanes] * factors[h]
        if last:
            after[0][0, :, lanes] = (mixed / totals[h]).astype(jnp.bfloat16)
        else:
            after[0][0, :, lanes] = mixed


def attention(queries, where, order, table, head, pieces, slots, n_chip, state=(), last=True):
    blocks, _, columns = queries.shape
    width = GROUP * HD
    rows = 2 * len(pieces) * QB
    whole = pl.BlockSpec(memory_space=pltpu.VMEM)
    tile = pl.BlockSpec((1, QB, width), lambda b, *_: (b, 0, 0))
    shape = (blocks, QB, width)
    state_shape = jax.ShapeDtypeStruct(shape, jnp.float32)
    done_shape = jax.ShapeDtypeStruct(shape, jnp.bfloat16)
    return pl.pallas_call(
        functools.partial(attention_kernel, n_chip, slots, not state, last),
        out_shape=done_shape if last else (state_shape,) * 3,
        grid_spec=pltpu.PrefetchScalarGridSpec(
            num_scalar_prefetch=3,
            grid=(blocks,),
            in_specs=[pl.BlockSpec((1, QB, width), lambda b, *_: (b, 0, head))]
            + [whole] * len(pieces)
            + [tile] * len(state),
            out_specs=tile if last else (tile,) * 3,
        ),
        compiler_params=pltpu.CompilerParams(vmem_limit_bytes=VMEM_LIMIT),
        cost_estimate=pl.CostEstimate(flops=1, bytes_accessed=1, transcendentals=0),
    )(where, order, table, queries, *pieces, *state)


def lay_out_kernel(n_outer, where_ref, *refs):
    rows = refs[-1]
    side = where_ref[1]
    for kv, group in enumerate(refs[i : i + 4] for i in range(0, len(refs) - 1, 4)):
        for at, ref in enumerate(group):
            which = 1 - side if at % 2 else side
            for g in range(GROUP):
                h = kv * GROUP + g
                if n_outer:
                    to = g * n_outer + kv + which * (KVH // 2)
                else:
                    to = h + which * (H // 2)
                to = pl.ds(pl.multiple_of(to * HD, HD), HD)
                for block in range(2):
                    first = (2 * block + at // 2) * QB
                    rows[first : first + QB, to] = ref[block, :, g * HD : (g + 1) * HD]


def lay_out(n_outer, where, parts):
    half = pl.BlockSpec((2, QB, GROUP * HD), lambda i, *_: (0, 0, 0))
    return pl.pallas_call(
        functools.partial(lay_out_kernel, n_outer),
        out_shape=jax.ShapeDtypeStruct((4 * QB, H * HD), jnp.bfloat16),
        grid_spec=pltpu.PrefetchScalarGridSpec(
            num_scalar_prefetch=1,
            grid=(1,),
            in_specs=[half] * len(parts),
            out_specs=pl.BlockSpec((4 * QB, H * HD), lambda i, *_: (0, 0)),
        ),
        compiler_params=pltpu.CompilerParams(vmem_limit_bytes=VMEM_LIMIT),
    )(where, *parts)


def project_kernel(rows_ref, w_ref, o_ref):
    o_ref[...] = jnp.dot(
        rows_ref[...], w_ref[0], preferred_element_type=jnp.float32
    ).astype(jnp.bfloat16)


def project(rows, weights, tile=PROJECT_TILE):
    parts, depth, columns = weights.shape
    tiles = columns // tile
    return pl.pallas_call(
        project_kernel,
        out_shape=jax.ShapeDtypeStruct((rows.shape[0], parts * columns), jnp.bfloat16),
        grid_spec=pl.GridSpec(
            grid=(parts, tiles),
            in_specs=[
                pl.BlockSpec(rows.shape, lambda p, t: (0, 0)),
                pl.BlockSpec((1, depth, tile), lambda p, t: (p, 0, t)),
            ],
            out_specs=pl.BlockSpec((rows.shape[0], tile), lambda p, t: (0, p * tiles + t)),
        ),
        compiler_params=pltpu.CompilerParams(vmem_limit_bytes=VMEM_LIMIT),
        cost_estimate=pl.CostEstimate(
            flops=2 * rows.shape[0] * depth * parts * columns,
            bytes_accessed=2 * (depth * parts * columns + rows.shape[0] * (depth + parts * columns)),
            transcendentals=0,
        ),
    )(rows, weights)


LINE = "outer"
PLANE = ("groups", "side", "core")
SEQ = ("outer", "side", "core")


def body(n_groups, n_outer, queries, keys, values, block_table, out_weight):
    n_chip = n_outer * 2
    order_rows = arrivals(n_outer)

    def index(outer, side, core):
        return (outer * 2 + side) * 2 + core

    spots = [(o, s, c) for o in range(n_outer) for s in range(2) for c in range(2)]
    group = lax.axis_index("groups")
    outer, side, core = (lax.axis_index(name) for name in SEQ)
    where = jnp.stack([outer, side, core, side]).astype(jnp.int32)
    where_across = jnp.stack([outer, side, core, 1 - side]).astype(jnp.int32)
    order = jnp.asarray(
        np.array([[p + d for d in row] for p, row in enumerate(order_rows)], np.int32)
    )

    def swap_core(array):
        return lax.ppermute(
            array, SEQ, [(index(o, s, c), index(o, s, 1 - c)) for o, s, c in spots]
        )

    def swap_side(array):
        return lax.ppermute(
            array, SEQ, [(index(o, s, c), index(o, 1 - s, c)) for o, s, c in spots]
        )

    def move(array, hop, way):
        return lax.ppermute(
            array,
            SEQ,
            [
                (index(o, s, c), index(o + way, s, c))
                for o, s, c in spots
                if 0 <= o + way < n_outer and 0 <= o - (hop - 1) * way < n_outer
            ],
        )

    def after(array, *others):
        return lax.optimization_barrier((array, *others))[0]

    def line(array, gates={}, got={}):
        got = {0: array, **got}
        for hop in range(1, n_outer):
            for way in (1, -1):
                if -way * hop in got:
                    continue
                sent = got[-way * (hop - 1)]
                if hop in gates:
                    sent = after(sent, *gates[hop])
                got[-way * hop] = move(sent, hop, way)
        return got

    def pick(got, k):
        wanted = [row[k] for row in order_rows]
        result = got[wanted[0]]
        for offset in sorted(set(wanted[1:])):
            mask = functools.reduce(
                jnp.logical_or, [outer == p for p in range(n_outer) if wanted[p] == offset]
            )
            if offset != wanted[0]:
                result = jnp.where(mask, got[offset], result)
        return result

    def half_of(array, which):
        width = array.shape[-1] // 2
        return lax.dynamic_slice_in_dim(array, which * width, width, array.ndim - 1)

    part = out_weight.shape[1] // n_groups
    columns = lax.dynamic_slice_in_dim(out_weight, group * part, part, 1)
    gathered = lax.all_gather(columns, LINE, axis=0, tiled=True)

    mine = jnp.concatenate([half_of(keys, side), half_of(values, side)], 0)
    theirs = jnp.concatenate([half_of(keys, 1 - side), half_of(values, 1 - side)], 0)
    theirs = swap_side(theirs)

    query_blocks = queries.reshape(2, 2, QB, H * HD)
    far_queries = swap_core(query_blocks[:, 1])
    far_table = swap_core(block_table)
    table = jnp.concatenate([block_table[0::2], far_table[1::2]], 0)
    near_queries = query_blocks[:, 0]

    def my_blocks(which):
        return jnp.concatenate([half_of(near_queries, which), half_of(far_queries, which)], 0)

    across_queries = swap_side(my_blocks(1 - side))
    across_table = swap_side(table)

    chains = [
        jnp.concatenate([half[:, h * HD : (h + 1) * HD] for half in (mine, theirs)], 0)
        for h in range(KVH // 2)
    ]
    gathered = after(gathered, across_queries, across_table, *chains)
    chains = [after(chain, gathered) for chain in chains]
    gathered = lax.all_gather(gathered, PLANE, axis=0, tiled=True)
    held = out_weight.shape[0]
    order_of_rows = n_outer
    if held != HD:
        gathered = gathered.reshape(n_groups, 2, 2, n_outer, held, part)
        gathered = jnp.transpose(gathered, (0, 3, 1, 2, 4, 5))
        order_of_rows = 0
    gathered = gathered.reshape(n_groups, H * HD, part)

    asks = (
        (across_queries, where_across, order, across_table),
        (my_blocks(side), where, order, table),
    )
    last = n_outer - 1
    lines = [line(chain) for chain in chains]
    states = []
    for head, got in enumerate(lines):
        near = [got[0]]
        for k in range(1, last):
            tied = {d: after(got[d], near[-1]) for d in sorted({row[k] for row in order_rows})}
            near.append(pick(tied, k))
        states.append(
            [attention(*ask, head, near, tuple(range(last)), n_chip, last=False) for ask in asks]
        )
    tie = [state[2] for pair in states for state in pair]
    late, across = [], []
    for head, got in enumerate(lines):
        piece = pick({d: after(got[d], *tie) for d in sorted({row[last] for row in order_rows})}, last)
        late.append([piece])
        out = attention(*asks[0], head, late[head], (last,), n_chip, states[head][0])
        tie = [out]
        across.append(swap_side(out))
    parts = []
    for head in range(KVH // 2):
        state = [after(array, *tie) for array in states[head][1]]
        near = attention(*asks[1], head, late[head], (last,), n_chip, state)
        tie = [across[head]]
        parts += [near, across[head], swap_core(near[2:]), swap_core(across[head][2:])]
    rows = lay_out(order_of_rows, where, parts)
    return project(rows, gathered)


def solution(mesh):
    n_groups, n_seq = mesh.shape["groups"], mesh.shape["seq"]
    n_outer = n_seq // 4
    split = Mesh(mesh.devices.reshape(n_groups, n_outer, 2, 2), ("groups", *SEQ))
    rows = P(("groups", *SEQ), None)
    in_specs = (rows, rows, rows, rows, P(SEQ, None))
    run = functools.partial(body, n_groups, n_outer)
    return jax.shard_map(run, mesh=split, in_specs=in_specs, out_specs=rows, check_vma=False)
```

```python
import functools

import jax
import jax.numpy as jnp
import numpy as np
from jax import lax
from jax.experimental import pallas as pl
from jax.experimental.pallas import tpu as pltpu
from jax.sharding import Mesh
from jax.sharding import PartitionSpec as P

H = 16
KVH = 4
HD = 128
QB = 128
ENTRIES = 8
GROUP = H // KVH
SCALE_LOG2 = HD ** (-0.5) * 1.4426950408889634
NT = (((1,), (1,)), ((), ()))
VMEM_LIMIT = 40 * 1024 * 1024
PROJECT_TILE = 1024


def arrivals(n_outer):
    rows = []
    for place in range(n_outer):
        row = [0]
        for hop in range(1, n_outer):
            if place - hop >= 0:
                row.append(-hop)
            if place + hop < n_outer:
                row.append(hop)
        rows.append(row)
    return rows


def attention_kernel(n_chip, slots, first, last, where_ref, order_ref, table_ref, q_ref, *refs):
    count = 2 * len(slots)
    pieces = refs[:count]
    before, after = ((), refs[count:]) if first else (refs[count : count + 3], refs[count + 3 :])
    step = pl.program_id(0)
    per_entry = n_chip // ENTRIES
    outer, side, core, asking = where_ref[0], where_ref[1], where_ref[2], where_ref[3]
    turn = jnp.where(step < 2, 0, core) + 2 * n_chip - (outer * 2 + asking)

    starts, usable = [], []
    for at in range(count):
        source_side = side if at < len(slots) else 1 - side
        source = order_ref[outer, slots[at % len(slots)]] * 2 + source_side
        ahead = lax.rem(source + turn, n_chip)
        row = table_ref[step, ahead // per_entry] & 3
        starts.append(pl.multiple_of(row * QB, QB))
        usable.append(lax.rem(ahead, per_entry) == 0)

    def gather(head, base):
        columns = slice(head * HD, (head + 1) * HD)
        return jnp.concatenate(
            [
                piece[pl.ds(start + base, QB), columns]
                for piece, start in zip(pieces, starts)
            ],
            0,
        )

    def spread(column):
        return jnp.broadcast_to(column, (QB, HD))

    heads = q_ref.shape[-1] // HD
    scores = []
    for h in range(heads):
        if h % GROUP == 0:
            keys = gather(h // GROUP, 0)
        s = lax.dot_general(
            q_ref[0, :, h * HD : (h + 1) * HD], keys, NT, preferred_element_type=jnp.float32
        )
        if per_entry > 1:
            s = jnp.concatenate(
                [
                    jnp.where(ok, s[:, at * QB : (at + 1) * QB], -1e30)
                    for at, ok in enumerate(usable)
                ],
                1,
            )
        scores.append(s)
    rounded, totals, factors = [], [], []
    for h, s in enumerate(scores):
        lanes = slice(h * HD, (h + 1) * HD)
        high = spread(jnp.max(s, axis=-1, keepdims=True))
        if not first:
            known = before[1][0, :, lanes]
            high = jnp.maximum(high, known)
            factors.append(jnp.exp2((known - high) * SCALE_LOG2))
        if not last:
            after[1][0, :, lanes] = high
        weights = jnp.exp2((s - jnp.concatenate([high] * count, 1)) * SCALE_LOG2)
        total = spread(jnp.sum(weights, axis=-1, keepdims=True))
        if not first:
            total += before[2][0, :, lanes] * factors[h]
        if not last:
            after[2][0, :, lanes] = total
        totals.append(total)
        rounded.append(weights.astype(jnp.bfloat16))
    for h in range(heads):
        lanes = slice(h * HD, (h + 1) * HD)
        if h % GROUP == 0:
            values = gather(h // GROUP, 4 * QB)
        mixed = jnp.dot(rounded[h], values, preferred_element_type=jnp.float32)
        if not first:
            mixed += before[0][0, :, lanes] * factors[h]
        if last:
            after[0][0, :, lanes] = (mixed / totals[h]).astype(jnp.bfloat16)
        else:
            after[0][0, :, lanes] = mixed


def attention(queries, where, order, table, pieces, slots, n_chip, state=(), last=True):
    blocks, _, columns = queries.shape
    rows = len(pieces) * QB
    whole = pl.BlockSpec(memory_space=pltpu.VMEM)
    tile = pl.BlockSpec((1, QB, columns), lambda b, *_: (b, 0, 0))
    state_shape = jax.ShapeDtypeStruct(queries.shape, jnp.float32)
    done_shape = jax.ShapeDtypeStruct(queries.shape, jnp.bfloat16)
    return pl.pallas_call(
        functools.partial(attention_kernel, n_chip, slots, not state, last),
        out_shape=done_shape if last else (state_shape,) * 3,
        grid_spec=pltpu.PrefetchScalarGridSpec(
            num_scalar_prefetch=3,
            grid=(blocks,),
            in_specs=[tile] + [whole] * len(pieces) + [tile] * len(state),
            out_specs=tile if last else (tile,) * 3,
        ),
        compiler_params=pltpu.CompilerParams(vmem_limit_bytes=VMEM_LIMIT),
        cost_estimate=pl.CostEstimate(flops=1, bytes_accessed=1, transcendentals=0),
    )(where, order, table, queries, *pieces, *state)


def lay_out_kernel(n_outer, where_ref, near_ref, across_ref, far_ref, far_across_ref, rows):
    side = where_ref[1]
    heads = H // 2
    for block in range(2):
        even = slice(2 * block * QB, (2 * block + 1) * QB)
        odd = slice((2 * block + 1) * QB, (2 * block + 2) * QB)
        for which, even_ref, odd_ref in (
            (side, near_ref, far_ref),
            (1 - side, across_ref, far_across_ref),
        ):
            for h in range(heads):
                at = slice(h * HD, (h + 1) * HD)
                if n_outer:
                    to = (h % 4) * n_outer + h // 4 + which * (heads // 4)
                else:
                    to = h + which * heads
                to = pl.ds(pl.multiple_of(to * HD, HD), HD)
                rows[even, to] = even_ref[block, :, at]
                rows[odd, to] = odd_ref[block, :, at]


def lay_out(n_outer, where, near, across, far, far_across):
    half = pl.BlockSpec((2, QB, near.shape[-1]), lambda i, *_: (0, 0, 0))
    return pl.pallas_call(
        functools.partial(lay_out_kernel, n_outer),
        out_shape=jax.ShapeDtypeStruct((4 * QB, H * HD), jnp.bfloat16),
        grid_spec=pltpu.PrefetchScalarGridSpec(
            num_scalar_prefetch=1,
            grid=(1,),
            in_specs=[half] * 4,
            out_specs=pl.BlockSpec((4 * QB, H * HD), lambda i, *_: (0, 0)),
        ),
        compiler_params=pltpu.CompilerParams(vmem_limit_bytes=VMEM_LIMIT),
    )(where, near, across, far, far_across)


def project_kernel(rows_ref, w_ref, o_ref):
    o_ref[...] = jnp.dot(
        rows_ref[...], w_ref[0], preferred_element_type=jnp.float32
    ).astype(jnp.bfloat16)


def project(rows, weights, tile=PROJECT_TILE):
    parts, depth, columns = weights.shape
    tiles = columns // tile
    return pl.pallas_call(
        project_kernel,
        out_shape=jax.ShapeDtypeStruct((rows.shape[0], parts * columns), jnp.bfloat16),
        grid_spec=pl.GridSpec(
            grid=(parts, tiles),
            in_specs=[
                pl.BlockSpec(rows.shape, lambda p, t: (0, 0)),
                pl.BlockSpec((1, depth, tile), lambda p, t: (p, 0, t)),
            ],
            out_specs=pl.BlockSpec((rows.shape[0], tile), lambda p, t: (0, p * tiles + t)),
        ),
        compiler_params=pltpu.CompilerParams(vmem_limit_bytes=VMEM_LIMIT),
        cost_estimate=pl.CostEstimate(
            flops=2 * rows.shape[0] * depth * parts * columns,
            bytes_accessed=2 * (depth * parts * columns + rows.shape[0] * (depth + parts * columns)),
            transcendentals=0,
        ),
    )(rows, weights)


LINE = "outer"
PLANE = ("groups", "side", "core")
SEQ = ("outer", "side", "core")


def body(n_groups, n_outer, queries, keys, values, block_table, out_weight):
    n_chip = n_outer * 2
    order_rows = arrivals(n_outer)

    def index(outer, side, core):
        return (outer * 2 + side) * 2 + core

    spots = [(o, s, c) for o in range(n_outer) for s in range(2) for c in range(2)]
    group = lax.axis_index("groups")
    outer, side, core = (lax.axis_index(name) for name in SEQ)
    where = jnp.stack([outer, side, core, side]).astype(jnp.int32)
    where_across = jnp.stack([outer, side, core, 1 - side]).astype(jnp.int32)
    order = jnp.asarray(
        np.array([[p + d for d in row] for p, row in enumerate(order_rows)], np.int32)
    )

    def swap_core(array):
        return lax.ppermute(
            array, SEQ, [(index(o, s, c), index(o, s, 1 - c)) for o, s, c in spots]
        )

    def swap_side(array):
        return lax.ppermute(
            array, SEQ, [(index(o, s, c), index(o, 1 - s, c)) for o, s, c in spots]
        )

    def move(array, hop, way):
        return lax.ppermute(
            array,
            SEQ,
            [
                (index(o, s, c), index(o + way, s, c))
                for o, s, c in spots
                if 0 <= o + way < n_outer and 0 <= o - (hop - 1) * way < n_outer
            ],
        )

    def after(array, *others):
        return lax.optimization_barrier((array, *others))[0]

    def line(array, gates={}, got={}):
        got = {0: array, **got}
        for hop in range(1, n_outer):
            for way in (1, -1):
                if -way * hop in got:
                    continue
                sent = got[-way * (hop - 1)]
                if hop in gates:
                    sent = after(sent, *gates[hop])
                got[-way * hop] = move(sent, hop, way)
        return got

    def pick(got, k):
        wanted = [row[k] for row in order_rows]
        result = got[wanted[0]]
        for offset in sorted(set(wanted[1:])):
            mask = functools.reduce(
                jnp.logical_or, [outer == p for p in range(n_outer) if wanted[p] == offset]
            )
            if offset != wanted[0]:
                result = jnp.where(mask, got[offset], result)
        return result

    def half_of(array, which):
        width = array.shape[-1] // 2
        return lax.dynamic_slice_in_dim(array, which * width, width, array.ndim - 1)

    part = out_weight.shape[1] // n_groups
    columns = lax.dynamic_slice_in_dim(out_weight, group * part, part, 1)
    gathered = lax.all_gather(columns, LINE, axis=0, tiled=True)

    mine = jnp.concatenate([half_of(keys, side), half_of(values, side)], 0)
    hops = {-way: move(mine, 1, way) for way in (1, -1)}
    theirs = jnp.concatenate(
        [half_of(after(array, mine), 1 - side) for array in (keys, values)], 0
    )
    theirs = swap_side(theirs)

    query_blocks = after(queries, mine).reshape(2, 2, QB, H * HD)
    far_queries = swap_core(query_blocks[:, 1])
    far_table = swap_core(block_table)
    table = jnp.concatenate([block_table[0::2], far_table[1::2]], 0)
    near_queries = query_blocks[:, 0]

    def my_blocks(which):
        return jnp.concatenate([half_of(near_queries, which), half_of(far_queries, which)], 0)

    across_queries = swap_side(after(my_blocks(1 - side), theirs, *hops.values()))
    across_table = swap_side(table)

    gathered = after(gathered, theirs, across_queries, across_table, *hops.values())
    gates = ({2: (gathered,)}, {1: (gathered,)})
    gathered = lax.all_gather(gathered, PLANE, axis=0, tiled=True)
    held = out_weight.shape[0]
    order_of_rows = n_outer
    if held != HD:
        gathered = gathered.reshape(n_groups, 2, 2, n_outer, held, part)
        gathered = jnp.transpose(gathered, (0, 3, 1, 2, 4, 5))
        order_of_rows = 0
    gathered = gathered.reshape(n_groups, H * HD, part)

    chains = [line(chain, gate, first) for chain, gate, first in zip((mine, theirs), gates, (hops, {}))]
    early, last = [], n_outer - 1
    for got in chains:
        near = [got[0]]
        for k in range(1, last):
            tied = {d: after(got[d], near[-1]) for d in sorted({row[k] for row in order_rows})}
            near.append(pick(tied, k))
        early += near

    asks = (
        (across_queries, where_across, order, across_table),
        (my_blocks(side), where, order, table),
    )
    states = [attention(*ask, early, tuple(range(last)), n_chip, last=False) for ask in asks]
    tie = [state[2] for state in states]
    late = [
        pick({d: after(got[d], *tie) for d in sorted({row[last] for row in order_rows})}, last)
        for got in chains
    ]
    across, near = (
        attention(*ask, late, (last,), n_chip, state) for ask, state in zip(asks, states)
    )
    across = swap_side(across)
    far = swap_core(near[2:])
    far_across = swap_core(across[2:])
    rows = lay_out(order_of_rows, where, near, across, far, far_across)
    return project(rows, gathered)


def solution(mesh):
    n_groups, n_seq = mesh.shape["groups"], mesh.shape["seq"]
    n_outer = n_seq // 4
    split = Mesh(mesh.devices.reshape(n_groups, n_outer, 2, 2), ("groups", *SEQ))
    rows = P(("groups", *SEQ), None)
    in_specs = (rows, rows, rows, rows, P(SEQ, None))
    run = functools.partial(body, n_groups, n_outer)
    return jax.shard_map(run, mesh=split, in_specs=in_specs, out_specs=rows, check_vma=False)
```

```python
import functools

import jax
import jax.numpy as jnp
import numpy as np
from jax import lax
from jax.experimental import pallas as pl
from jax.experimental.pallas import tpu as pltpu
from jax.sharding import Mesh
from jax.sharding import PartitionSpec as P

H = 16
KVH = 4
HD = 128
QB = 128
ENTRIES = 8
GROUP = H // KVH
SCALE_LOG2 = HD ** (-0.5) * 1.4426950408889634
NT = (((1,), (1,)), ((), ()))
VMEM_LIMIT = 40 * 1024 * 1024
PROJECT_TILE = 1024


def arrivals(n_outer):
    rows = []
    for place in range(n_outer):
        row = [0]
        for hop in range(1, n_outer):
            if place - hop >= 0:
                row.append(-hop)
            if place + hop < n_outer:
                row.append(hop)
        rows.append(row)
    return rows


def attention_kernel(n_chip, slots, first, last, where_ref, order_ref, table_ref, q_ref, *refs):
    pieces, refs = refs[: len(slots)], refs[len(slots) :]
    before, after = ((), refs) if first else (refs[:3], refs[3:])
    count = 2 * len(slots)
    step = pl.program_id(0)
    per_entry = n_chip // ENTRIES
    outer, side, core, asking = where_ref[0], where_ref[1], where_ref[2], where_ref[3]
    turn = jnp.where(step < 2, 0, core) + 2 * n_chip - (outer * 2 + asking)

    starts, usable = [], []
    for at in range(count):
        source_side = side if at < len(slots) else 1 - side
        source = order_ref[outer, slots[at % len(slots)]] * 2 + source_side
        ahead = lax.rem(source + turn, n_chip)
        row = table_ref[step, ahead // per_entry] & 3
        base = 0 if at < len(slots) else 8
        starts.append(pl.multiple_of((base + row) * QB, QB))
        usable.append(lax.rem(ahead, per_entry) == 0)

    def gather(base):
        return jnp.concatenate(
            [pieces[at % len(slots)][pl.ds(start + base, QB), :] for at, start in enumerate(starts)],
            0,
        )

    keys, values = gather(0), gather(4 * QB)

    def spread(column):
        return jnp.broadcast_to(column, (QB, HD))

    scores = []
    for h in range(GROUP):
        s = lax.dot_general(
            q_ref[0, :, h * HD : (h + 1) * HD], keys, NT, preferred_element_type=jnp.float32
        )
        if per_entry > 1:
            s = jnp.concatenate(
                [
                    jnp.where(ok, s[:, at * QB : (at + 1) * QB], -1e30)
                    for at, ok in enumerate(usable)
                ],
                1,
            )
        scores.append(s)
    rounded, totals, factors = [], [], []
    for h, s in enumerate(scores):
        lanes = slice(h * HD, (h + 1) * HD)
        high = spread(jnp.max(s, axis=-1, keepdims=True))
        if not first:
            known = before[1][0, :, lanes]
            high = jnp.maximum(high, known)
            factors.append(jnp.exp2((known - high) * SCALE_LOG2))
        if not last:
            after[1][0, :, lanes] = high
        weights = jnp.exp2((s - jnp.concatenate([high] * count, 1)) * SCALE_LOG2)
        total = spread(jnp.sum(weights, axis=-1, keepdims=True))
        if not first:
            total += before[2][0, :, lanes] * factors[h]
        if not last:
            after[2][0, :, lanes] = total
        totals.append(total)
        rounded.append(weights.astype(jnp.bfloat16))
    for h in range(GROUP):
        lanes = slice(h * HD, (h + 1) * HD)
        mixed = jnp.dot(rounded[h], values, preferred_element_type=jnp.float32)
        if not first:
            mixed += before[0][0, :, lanes] * factors[h]
        if last:
            after[0][0, :, lanes] = (mixed / totals[h]).astype(jnp.bfloat16)
        else:
            after[0][0, :, lanes] = mixed


def attention(queries, where, order, table, head, pieces, slots, n_chip, state=(), last=True):
    blocks, _, columns = queries.shape
    width = GROUP * HD
    rows = 2 * len(pieces) * QB
    whole = pl.BlockSpec(memory_space=pltpu.VMEM)
    tile = pl.BlockSpec((1, QB, width), lambda b, *_: (b, 0, 0))
    shape = (blocks, QB, width)
    state_shape = jax.ShapeDtypeStruct(shape, jnp.float32)
    done_shape = jax.ShapeDtypeStruct(shape, jnp.bfloat16)
    return pl.pallas_call(
        functools.partial(attention_kernel, n_chip, slots, not state, last),
        out_shape=done_shape if last else (state_shape,) * 3,
        grid_spec=pltpu.PrefetchScalarGridSpec(
            num_scalar_prefetch=3,
            grid=(blocks,),
            in_specs=[pl.BlockSpec((1, QB, width), lambda b, *_: (b, 0, head))]
            + [whole] * len(pieces)
            + [tile] * len(state),
            out_specs=tile if last else (tile,) * 3,
        ),
        compiler_params=pltpu.CompilerParams(vmem_limit_bytes=VMEM_LIMIT),
        cost_estimate=pl.CostEstimate(flops=1, bytes_accessed=1, transcendentals=0),
    )(where, order, table, queries, *pieces, *state)


def row_block(n_outer, which, kv, g):
    if n_outer:
        return g * n_outer + kv + which * (KVH // 2)
    return which * (H // 2) + kv * GROUP + g


def lay_out_kernel(*refs):
    rows = refs[-1]
    width = GROUP * HD
    for at, ref in enumerate(refs[:-1]):
        columns = slice(at // 2 * width, (at // 2 + 1) * width)
        for block in range(2):
            first = (2 * block + at % 2) * QB
            rows[first : first + QB, columns] = ref[block]


def lay_out(parts):
    half = pl.BlockSpec((2, QB, GROUP * HD), lambda i: (0, 0, 0))
    shape = (4 * QB, len(parts) // 2 * GROUP * HD)
    return pl.pallas_call(
        lay_out_kernel,
        out_shape=jax.ShapeDtypeStruct(shape, jnp.bfloat16),
        grid=(1,),
        in_specs=[half] * len(parts),
        out_specs=pl.BlockSpec(shape, lambda i: (0, 0)),
        compiler_params=pltpu.CompilerParams(vmem_limit_bytes=VMEM_LIMIT),
    )(*parts)


def project_kernel(n_outer, groups, steps, where_ref, rows_ref, w_ref, *refs):
    o_ref, wbuf, sems = refs[-3:]
    side = where_ref[1]
    step = pl.program_id(0)
    tile = wbuf.shape[-1]
    tiles = w_ref.shape[-1] // tile

    def fetch(later):
        columns = slice(later % tiles * tile, (later % tiles + 1) * tile)
        for at, (other, kv) in enumerate(groups):
            for g in range(GROUP):
                block = row_block(n_outer, 1 - side if other else side, kv, g)
                to = (at * GROUP + g) * HD
                pltpu.make_async_copy(
                    w_ref.at[later // tiles, pl.ds(pl.multiple_of(block * HD, HD), HD), columns],
                    wbuf.at[later % 2, to : to + HD, :],
                    sems.at[later % 2],
                ).start()

    @pl.when(step == 0)
    def _():
        fetch(0)

    for later in range(1, steps):

        @pl.when(step == later - 1)
        def _():
            fetch(later)

    slot = lax.rem(step, 2)
    pltpu.make_async_copy(wbuf.at[slot], wbuf.at[slot], sems.at[slot]).wait()
    total = jnp.dot(rows_ref[...], wbuf[slot], preferred_element_type=jnp.float32)
    if len(refs) > 3:
        total += refs[0][...]
    o_ref[...] = total.astype(o_ref.dtype)


def project(n_outer, where, rows, groups, weights, before=None, tile=PROJECT_TILE):
    parts, _, columns = weights.shape
    steps = parts * columns // tile
    length, depth = rows.shape
    block = pl.BlockSpec((length, tile), lambda s, *_: (0, s))
    dtype = jnp.float32 if before is None else jnp.bfloat16
    return pl.pallas_call(
        functools.partial(project_kernel, n_outer, groups, steps),
        out_shape=jax.ShapeDtypeStruct((length, parts * columns), dtype),
        grid_spec=pltpu.PrefetchScalarGridSpec(
            num_scalar_prefetch=1,
            grid=(steps,),
            in_specs=[
                pl.BlockSpec((length, depth), lambda s, *_: (0, 0)),
                pl.BlockSpec(memory_space=pltpu.HBM),
            ]
            + [block] * (before is not None),
            out_specs=block,
            scratch_shapes=[
                pltpu.VMEM((2, depth, tile), jnp.bfloat16),
                pltpu.SemaphoreType.DMA((2,)),
            ],
        ),
        compiler_params=pltpu.CompilerParams(vmem_limit_bytes=VMEM_LIMIT),
        cost_estimate=pl.CostEstimate(flops=1, bytes_accessed=1, transcendentals=0),
    )(where, rows, weights, *([] if before is None else [before]))


LINE = "outer"
PLANE = ("groups", "side", "core")
SEQ = ("outer", "side", "core")


def body(n_groups, n_outer, queries, keys, values, block_table, out_weight):
    n_chip = n_outer * 2
    order_rows = arrivals(n_outer)

    def index(outer, side, core):
        return (outer * 2 + side) * 2 + core

    spots = [(o, s, c) for o in range(n_outer) for s in range(2) for c in range(2)]
    group = lax.axis_index("groups")
    outer, side, core = (lax.axis_index(name) for name in SEQ)
    where = jnp.stack([outer, side, core, side]).astype(jnp.int32)
    where_across = jnp.stack([outer, side, core, 1 - side]).astype(jnp.int32)
    order = jnp.asarray(
        np.array([[p + d for d in row] for p, row in enumerate(order_rows)], np.int32)
    )

    def swap_core(array):
        return lax.ppermute(
            array, SEQ, [(index(o, s, c), index(o, s, 1 - c)) for o, s, c in spots]
        )

    def swap_side(array):
        return lax.ppermute(
            array, SEQ, [(index(o, s, c), index(o, 1 - s, c)) for o, s, c in spots]
        )

    def move(array, hop, way):
        return lax.ppermute(
            array,
            SEQ,
            [
                (index(o, s, c), index(o + way, s, c))
                for o, s, c in spots
                if 0 <= o + way < n_outer and 0 <= o - (hop - 1) * way < n_outer
            ],
        )

    def after(array, *others):
        return lax.optimization_barrier((array, *others))[0]

    def line(array, gates={}, got={}):
        got = {0: array, **got}
        for hop in range(1, n_outer):
            for way in (1, -1):
                if -way * hop in got:
                    continue
                sent = got[-way * (hop - 1)]
                if hop in gates:
                    sent = after(sent, *gates[hop])
                got[-way * hop] = move(sent, hop, way)
        return got

    def pick(got, k):
        wanted = [row[k] for row in order_rows]
        result = got[wanted[0]]
        for offset in sorted(set(wanted[1:])):
            mask = functools.reduce(
                jnp.logical_or, [outer == p for p in range(n_outer) if wanted[p] == offset]
            )
            if offset != wanted[0]:
                result = jnp.where(mask, got[offset], result)
        return result

    def half_of(array, which):
        width = array.shape[-1] // 2
        return lax.dynamic_slice_in_dim(array, which * width, width, array.ndim - 1)

    part = out_weight.shape[1] // n_groups
    columns = lax.dynamic_slice_in_dim(out_weight, group * part, part, 1)
    gathered = lax.all_gather(columns, LINE, axis=0, tiled=True)

    mine = jnp.concatenate([half_of(keys, side), half_of(values, side)], 0)
    theirs = jnp.concatenate([half_of(keys, 1 - side), half_of(values, 1 - side)], 0)
    theirs = swap_side(theirs)

    query_blocks = queries.reshape(2, 2, QB, H * HD)
    far_queries = swap_core(query_blocks[:, 1])
    far_table = swap_core(block_table)
    table = jnp.concatenate([block_table[0::2], far_table[1::2]], 0)
    near_queries = query_blocks[:, 0]

    def my_blocks(which):
        return jnp.concatenate([half_of(near_queries, which), half_of(far_queries, which)], 0)

    across_queries = swap_side(my_blocks(1 - side))
    across_table = swap_side(table)

    chains = [
        jnp.concatenate([half[:, h * HD : (h + 1) * HD] for half in (mine, theirs)], 0)
        for h in range(KVH // 2)
    ]
    gathered = after(gathered, across_queries, across_table, *chains)
    chains = [after(chain, gathered) for chain in chains]
    gathered = lax.all_gather(gathered, PLANE, axis=0, tiled=True)
    held = out_weight.shape[0]
    order_of_rows = n_outer
    if held != HD:
        gathered = gathered.reshape(n_groups, 2, 2, n_outer, held, part)
        gathered = jnp.transpose(gathered, (0, 3, 1, 2, 4, 5))
        order_of_rows = 0
    gathered = gathered.reshape(n_groups, H * HD, part)

    asks = (
        (across_queries, where_across, order, across_table),
        (my_blocks(side), where, order, table),
    )
    last = n_outer - 1
    lines = [line(chain) for chain in chains]
    states = []
    for head, got in enumerate(lines):
        near = [got[0]]
        for k in range(1, last):
            tied = {d: after(got[d], near[-1]) for d in sorted({row[k] for row in order_rows})}
            near.append(pick(tied, k))
        states.append(
            [attention(*ask, head, near, tuple(range(last)), n_chip, last=False) for ask in asks]
        )
    tie = [state[2] for pair in states for state in pair]
    late, across = [], []
    for head, got in enumerate(lines):
        piece = pick({d: after(got[d], *tie) for d in sorted({row[last] for row in order_rows})}, last)
        late.append([piece])
        out = attention(*asks[0], head, late[head], (last,), n_chip, states[head][0])
        tie = [out]
        across.append(swap_side(out))
    def even_and_odd(array):
        return [array, swap_core(array[2:])]

    parts = []
    for head in range(KVH // 2):
        state = [after(array, *tie) for array in states[head][1]]
        near = attention(*asks[1], head, late[head], (last,), n_chip, state)
        parts += [near, swap_core(near[2:])]
    for array in across[:-1]:
        parts += even_and_odd(array)
    groups = [(other, kv) for other in (0, 1) for kv in range(KVH // 2)]
    sums = project(order_of_rows, where, lay_out(parts), groups[:-1], gathered)
    rows = lay_out(even_and_odd(after(across[-1], sums)))
    return project(order_of_rows, where, rows, groups[-1:], gathered, sums)


def solution(mesh):
    n_groups, n_seq = mesh.shape["groups"], mesh.shape["seq"]
    n_outer = n_seq // 4
    split = Mesh(mesh.devices.reshape(n_groups, n_outer, 2, 2), ("groups", *SEQ))
    rows = P(("groups", *SEQ), None)
    in_specs = (rows, rows, rows, rows, P(SEQ, None))
    run = functools.partial(body, n_groups, n_outer)
    return jax.shard_map(run, mesh=split, in_specs=in_specs, out_specs=rows, check_vma=False)
```

```python
import functools

import jax
import jax.numpy as jnp
import numpy as np
from jax import lax
from jax.experimental import pallas as pl
from jax.experimental.pallas import tpu as pltpu
from jax.sharding import Mesh
from jax.sharding import PartitionSpec as P

H = 16
KVH = 4
HD = 128
QB = 128
ENTRIES = 8
GROUP = H // KVH
SCALE_LOG2 = HD ** (-0.5) * 1.4426950408889634
NT = (((1,), (1,)), ((), ()))
VMEM_LIMIT = 40 * 1024 * 1024
PROJECT_TILE = 1024


def arrivals(n_outer):
    rows = []
    for place in range(n_outer):
        row = [0]
        for hop in range(1, n_outer):
            if place - hop >= 0:
                row.append(-hop)
            if place + hop < n_outer:
                row.append(hop)
        rows.append(row)
    return rows


def attention_kernel(n_chip, slots, first, last, where_ref, order_ref, table_ref, q_ref, *refs):
    pieces, refs = refs[: len(slots)], refs[len(slots) :]
    before, after = ((), refs) if first else (refs[:3], refs[3:])
    count = 2 * len(slots)
    step = pl.program_id(0)
    per_entry = n_chip // ENTRIES
    outer, side, core, asking = where_ref[0], where_ref[1], where_ref[2], where_ref[3]
    turn = jnp.where(step < 2, 0, core) + 2 * n_chip - (outer * 2 + asking)

    starts, usable = [], []
    for at in range(count):
        source_side = side if at < len(slots) else 1 - side
        source = order_ref[outer, slots[at % len(slots)]] * 2 + source_side
        ahead = lax.rem(source + turn, n_chip)
        row = table_ref[step, ahead // per_entry] & 3
        base = 0 if at < len(slots) else 8
        starts.append(pl.multiple_of((base + row) * QB, QB))
        usable.append(lax.rem(ahead, per_entry) == 0)

    def gather(base):
        return jnp.concatenate(
            [pieces[at % len(slots)][pl.ds(start + base, QB), :] for at, start in enumerate(starts)],
            0,
        )

    keys, values = gather(0), gather(4 * QB)

    def spread(column):
        return jnp.broadcast_to(column, (QB, HD))

    scores = []
    for h in range(GROUP):
        s = lax.dot_general(
            q_ref[0, :, h * HD : (h + 1) * HD], keys, NT, preferred_element_type=jnp.float32
        )
        if per_entry > 1:
            s = jnp.concatenate(
                [
                    jnp.where(ok, s[:, at * QB : (at + 1) * QB], -1e30)
                    for at, ok in enumerate(usable)
                ],
                1,
            )
        scores.append(s)
    rounded, totals, factors = [], [], []
    for h, s in enumerate(scores):
        lanes = slice(h * HD, (h + 1) * HD)
        high = spread(jnp.max(s, axis=-1, keepdims=True))
        if not first:
            known = before[1][0, :, lanes]
            high = jnp.maximum(high, known)
            factors.append(jnp.exp2((known - high) * SCALE_LOG2))
        if not last:
            after[1][0, :, lanes] = high
        weights = jnp.exp2((s - jnp.concatenate([high] * count, 1)) * SCALE_LOG2)
        total = spread(jnp.sum(weights, axis=-1, keepdims=True))
        if not first:
            total += before[2][0, :, lanes] * factors[h]
        if not last:
            after[2][0, :, lanes] = total
        totals.append(total)
        rounded.append(weights.astype(jnp.bfloat16))
    for h in range(GROUP):
        lanes = slice(h * HD, (h + 1) * HD)
        mixed = jnp.dot(rounded[h], values, preferred_element_type=jnp.float32)
        if not first:
            mixed += before[0][0, :, lanes] * factors[h]
        if last:
            after[0][0, :, lanes] = (mixed / totals[h]).astype(jnp.bfloat16)
        else:
            after[0][0, :, lanes] = mixed


def attention(queries, where, order, table, head, pieces, slots, n_chip, state=(), last=True):
    blocks, _, columns = queries.shape
    width = GROUP * HD
    rows = 2 * len(pieces) * QB
    whole = pl.BlockSpec(memory_space=pltpu.VMEM)
    tile = pl.BlockSpec((1, QB, width), lambda b, *_: (b, 0, 0))
    shape = (blocks, QB, width)
    state_shape = jax.ShapeDtypeStruct(shape, jnp.float32)
    done_shape = jax.ShapeDtypeStruct(shape, jnp.bfloat16)
    return pl.pallas_call(
        functools.partial(attention_kernel, n_chip, slots, not state, last),
        out_shape=done_shape if last else (state_shape,) * 3,
        grid_spec=pltpu.PrefetchScalarGridSpec(
            num_scalar_prefetch=3,
            grid=(blocks,),
            in_specs=[pl.BlockSpec((1, QB, width), lambda b, *_: (b, 0, head))]
            + [whole] * len(pieces)
            + [tile] * len(state),
            out_specs=tile if last else (tile,) * 3,
        ),
        compiler_params=pltpu.CompilerParams(vmem_limit_bytes=VMEM_LIMIT),
        cost_estimate=pl.CostEstimate(flops=1, bytes_accessed=1, transcendentals=0),
    )(where, order, table, queries, *pieces, *state)


def row_block(n_outer, which, kv, g):
    if n_outer:
        return g * n_outer + kv + which * (KVH // 2)
    return which * (H // 2) + kv * GROUP + g


def lay_out_kernel(*refs):
    rows = refs[-1]
    width = GROUP * HD
    for at, ref in enumerate(refs[:-1]):
        columns = slice(at // 2 * width, (at // 2 + 1) * width)
        for block in range(2):
            first = (2 * block + at % 2) * QB
            rows[first : first + QB, columns] = ref[block]


def lay_out(parts):
    half = pl.BlockSpec((2, QB, GROUP * HD), lambda i: (0, 0, 0))
    shape = (4 * QB, len(parts) // 2 * GROUP * HD)
    return pl.pallas_call(
        lay_out_kernel,
        out_shape=jax.ShapeDtypeStruct(shape, jnp.bfloat16),
        grid=(1,),
        in_specs=[half] * len(parts),
        out_specs=pl.BlockSpec(shape, lambda i: (0, 0)),
        compiler_params=pltpu.CompilerParams(vmem_limit_bytes=VMEM_LIMIT),
    )(*parts)


def project_kernel(n_outer, groups, steps, where_ref, rows_ref, w_ref, *refs):
    o_ref, wbuf, sems = refs[-3:]
    side = where_ref[1]
    step = pl.program_id(0)
    tile = wbuf.shape[-1]
    tiles = w_ref.shape[-1] // tile

    def fetch(later):
        columns = slice(later % tiles * tile, (later % tiles + 1) * tile)
        for at, (other, kv) in enumerate(groups):
            for g in range(GROUP):
                block = row_block(n_outer, 1 - side if other else side, kv, g)
                to = (at * GROUP + g) * HD
                pltpu.make_async_copy(
                    w_ref.at[later // tiles, pl.ds(pl.multiple_of(block * HD, HD), HD), columns],
                    wbuf.at[later % 2, to : to + HD, :],
                    sems.at[later % 2],
                ).start()

    @pl.when(step == 0)
    def _():
        fetch(0)

    for later in range(1, steps):

        @pl.when(step == later - 1)
        def _():
            fetch(later)

    slot = lax.rem(step, 2)
    pltpu.make_async_copy(wbuf.at[slot], wbuf.at[slot], sems.at[slot]).wait()
    total = jnp.dot(rows_ref[...], wbuf[slot], preferred_element_type=jnp.float32)
    if len(refs) > 3:
        total += refs[0][:, pl.ds(pl.multiple_of(step * tile, tile), tile)]
    o_ref[...] = total.astype(o_ref.dtype)


def project(n_outer, where, rows, groups, weights, before=None, tile=PROJECT_TILE):
    parts, _, columns = weights.shape
    steps = parts * columns // tile
    length, depth = rows.shape
    block = pl.BlockSpec((length, tile), lambda s, *_: (0, s))
    dtype = jnp.float32 if before is None else jnp.bfloat16
    return pl.pallas_call(
        functools.partial(project_kernel, n_outer, groups, steps),
        out_shape=jax.ShapeDtypeStruct((length, parts * columns), dtype),
        grid_spec=pltpu.PrefetchScalarGridSpec(
            num_scalar_prefetch=1,
            grid=(steps,),
            in_specs=[
                pl.BlockSpec((length, depth), lambda s, *_: (0, 0)),
                pl.BlockSpec(memory_space=pltpu.HBM),
            ]
            + [pl.BlockSpec(memory_space=pltpu.VMEM)] * (before is not None),
            out_specs=block,
            scratch_shapes=[
                pltpu.VMEM((2, depth, tile), jnp.bfloat16),
                pltpu.SemaphoreType.DMA((2,)),
            ],
        ),
        compiler_params=pltpu.CompilerParams(vmem_limit_bytes=VMEM_LIMIT),
        cost_estimate=pl.CostEstimate(flops=1, bytes_accessed=1, transcendentals=0),
    )(where, rows, weights, *([] if before is None else [before]))


LINE = "outer"
PLANE = ("groups", "side", "core")
SEQ = ("outer", "side", "core")


def body(n_groups, n_outer, queries, keys, values, block_table, out_weight):
    n_chip = n_outer * 2
    order_rows = arrivals(n_outer)

    def index(outer, side, core):
        return (outer * 2 + side) * 2 + core

    spots = [(o, s, c) for o in range(n_outer) for s in range(2) for c in range(2)]
    group = lax.axis_index("groups")
    outer, side, core = (lax.axis_index(name) for name in SEQ)
    where = jnp.stack([outer, side, core, side]).astype(jnp.int32)
    where_across = jnp.stack([outer, side, core, 1 - side]).astype(jnp.int32)
    order = jnp.asarray(
        np.array([[p + d for d in row] for p, row in enumerate(order_rows)], np.int32)
    )

    def swap_core(array):
        return lax.ppermute(
            array, SEQ, [(index(o, s, c), index(o, s, 1 - c)) for o, s, c in spots]
        )

    def swap_side(array):
        return lax.ppermute(
            array, SEQ, [(index(o, s, c), index(o, 1 - s, c)) for o, s, c in spots]
        )

    def move(array, hop, way):
        return lax.ppermute(
            array,
            SEQ,
            [
                (index(o, s, c), index(o + way, s, c))
                for o, s, c in spots
                if 0 <= o + way < n_outer and 0 <= o - (hop - 1) * way < n_outer
            ],
        )

    def after(array, *others):
        return lax.optimization_barrier((array, *others))[0]

    def line(array, gates={}, got={}):
        got = {0: array, **got}
        for hop in range(1, n_outer):
            for way in (1, -1):
                if -way * hop in got:
                    continue
                sent = got[-way * (hop - 1)]
                if hop in gates:
                    sent = after(sent, *gates[hop])
                got[-way * hop] = move(sent, hop, way)
        return got

    def pick(got, k):
        wanted = [row[k] for row in order_rows]
        result = got[wanted[0]]
        for offset in sorted(set(wanted[1:])):
            mask = functools.reduce(
                jnp.logical_or, [outer == p for p in range(n_outer) if wanted[p] == offset]
            )
            if offset != wanted[0]:
                result = jnp.where(mask, got[offset], result)
        return result

    def half_of(array, which):
        width = array.shape[-1] // 2
        return lax.dynamic_slice_in_dim(array, which * width, width, array.ndim - 1)

    part = out_weight.shape[1] // n_groups
    columns = lax.dynamic_slice_in_dim(out_weight, group * part, part, 1)
    gathered = lax.all_gather(columns, LINE, axis=0, tiled=True)

    mine = jnp.concatenate([half_of(keys, side), half_of(values, side)], 0)
    theirs = jnp.concatenate([half_of(keys, 1 - side), half_of(values, 1 - side)], 0)
    theirs = swap_side(theirs)

    query_blocks = queries.reshape(2, 2, QB, H * HD)
    far_queries = swap_core(query_blocks[:, 1])
    far_table = swap_core(block_table)
    table = jnp.concatenate([block_table[0::2], far_table[1::2]], 0)
    near_queries = query_blocks[:, 0]

    def my_blocks(which):
        return jnp.concatenate([half_of(near_queries, which), half_of(far_queries, which)], 0)

    across_queries = swap_side(my_blocks(1 - side))
    across_table = swap_side(table)

    chains = [
        jnp.concatenate([half[:, h * HD : (h + 1) * HD] for half in (mine, theirs)], 0)
        for h in range(KVH // 2)
    ]
    gathered = after(gathered, across_queries, across_table, *chains)
    chains = [after(chain, gathered) for chain in chains]
    gathered = lax.all_gather(gathered, PLANE, axis=0, tiled=True)
    held = out_weight.shape[0]
    order_of_rows = n_outer
    if held != HD:
        gathered = gathered.reshape(n_groups, 2, 2, n_outer, held, part)
        gathered = jnp.transpose(gathered, (0, 3, 1, 2, 4, 5))
        order_of_rows = 0
    gathered = gathered.reshape(n_groups, H * HD, part)

    asks = (
        (across_queries, where_across, order, across_table),
        (my_blocks(side), where, order, table),
    )
    last = n_outer - 1
    lines = [line(chain) for chain in chains]
    states = []
    for head, got in enumerate(lines):
        near = [got[0]]
        for k in range(1, last):
            tied = {d: after(got[d], near[-1]) for d in sorted({row[k] for row in order_rows})}
            near.append(pick(tied, k))
        states.append(
            [attention(*ask, head, near, tuple(range(last)), n_chip, last=False) for ask in asks]
        )
    tie = [state[2] for pair in states for state in pair]
    late, across = [], []
    for head, got in enumerate(lines):
        piece = pick({d: after(got[d], *tie) for d in sorted({row[last] for row in order_rows})}, last)
        late.append([piece])
        out = attention(*asks[0], head, late[head], (last,), n_chip, states[head][0])
        tie = [out]
        if head + 1 == KVH // 2:
            out = jnp.concatenate([out[:2], swap_core(out[2:])], 0)
        across.append(swap_side(out))
    def even_and_odd(array):
        return [array, swap_core(array[2:])]

    parts = []
    for head in range(KVH // 2):
        state = [after(array, *tie) for array in states[head][1]]
        near = attention(*asks[1], head, late[head], (last,), n_chip, state)
        parts += [near, swap_core(near[2:])]
    for array in across[:-1]:
        parts += even_and_odd(array)
    groups = [(other, kv) for other in (0, 1) for kv in range(KVH // 2)]
    sums = project(order_of_rows, where, lay_out(parts), groups[:-1], gathered)
    arrived = after(across[-1], sums)
    rows = lay_out([arrived[:2], arrived[2:]])
    return project(order_of_rows, where, rows, groups[-1:], gathered, sums)


def solution(mesh):
    n_groups, n_seq = mesh.shape["groups"], mesh.shape["seq"]
    n_outer = n_seq // 4
    split = Mesh(mesh.devices.reshape(n_groups, n_outer, 2, 2), ("groups", *SEQ))
    rows = P(("groups", *SEQ), None)
    in_specs = (rows, rows, rows, rows, P(SEQ, None))
    run = functools.partial(body, n_groups, n_outer)
    return jax.shard_map(run, mesh=split, in_specs=in_specs, out_specs=rows, check_vma=False)
```

```python
import functools

import jax
import jax.numpy as jnp
import numpy as np
from jax import lax
from jax.experimental import pallas as pl
from jax.experimental.pallas import tpu as pltpu
from jax.sharding import Mesh
from jax.sharding import PartitionSpec as P

H = 16
KVH = 4
HD = 128
QB = 128
ENTRIES = 8
GROUP = H // KVH
SCALE_LOG2 = HD ** (-0.5) * 1.4426950408889634
NT = (((1,), (1,)), ((), ()))
VMEM_LIMIT = 40 * 1024 * 1024
PROJECT_TILE = 1024


def arrivals(n_outer):
    rows = []
    for place in range(n_outer):
        row = [0]
        for hop in range(1, n_outer):
            if place - hop >= 0:
                row.append(-hop)
            if place + hop < n_outer:
                row.append(hop)
        rows.append(row)
    return rows


def attention_kernel(n_chip, slots, first, last, where_ref, order_ref, table_ref, q_ref, *refs):
    pieces, refs = refs[: len(slots)], refs[len(slots) :]
    before, after = ((), refs) if first else (refs[:3], refs[3:])
    count = 2 * len(slots)
    step = pl.program_id(0)
    per_entry = n_chip // ENTRIES
    outer, side, core, asking = where_ref[0], where_ref[1], where_ref[2], where_ref[3]
    turn = jnp.where(step < 2, 0, core) + 2 * n_chip - (outer * 2 + asking)

    starts, usable = [], []
    for at in range(count):
        source_side = side if at < len(slots) else 1 - side
        source = order_ref[outer, slots[at % len(slots)]] * 2 + source_side
        ahead = lax.rem(source + turn, n_chip)
        row = table_ref[step, ahead // per_entry] & 3
        base = 0 if at < len(slots) else 8
        starts.append(pl.multiple_of((base + row) * QB, QB))
        usable.append(lax.rem(ahead, per_entry) == 0)

    def gather(base):
        return jnp.concatenate(
            [pieces[at % len(slots)][pl.ds(start + base, QB), :] for at, start in enumerate(starts)],
            0,
        )

    keys, values = gather(0), gather(4 * QB)

    def spread(column):
        return jnp.broadcast_to(column, (QB, HD))

    scores = []
    for h in range(GROUP):
        s = lax.dot_general(
            q_ref[0, :, h * HD : (h + 1) * HD], keys, NT, preferred_element_type=jnp.float32
        )
        if per_entry > 1:
            s = jnp.concatenate(
                [
                    jnp.where(ok, s[:, at * QB : (at + 1) * QB], -1e30)
                    for at, ok in enumerate(usable)
                ],
                1,
            )
        scores.append(s)
    rounded, totals, factors = [], [], []
    for h, s in enumerate(scores):
        lanes = slice(h * HD, (h + 1) * HD)
        high = spread(jnp.max(s, axis=-1, keepdims=True))
        if not first:
            known = before[1][0, :, lanes]
            high = jnp.maximum(high, known)
            factors.append(jnp.exp2((known - high) * SCALE_LOG2))
        if not last:
            after[1][0, :, lanes] = high
        weights = jnp.exp2((s - jnp.concatenate([high] * count, 1)) * SCALE_LOG2)
        total = spread(jnp.sum(weights, axis=-1, keepdims=True))
        if not first:
            total += before[2][0, :, lanes] * factors[h]
        if not last:
            after[2][0, :, lanes] = total
        totals.append(total)
        rounded.append(weights.astype(jnp.bfloat16))
    for h in range(GROUP):
        lanes = slice(h * HD, (h + 1) * HD)
        mixed = jnp.dot(rounded[h], values, preferred_element_type=jnp.float32)
        if not first:
            mixed += before[0][0, :, lanes] * factors[h]
        if last:
            after[0][0, :, lanes] = (mixed / totals[h]).astype(jnp.bfloat16)
        else:
            after[0][0, :, lanes] = mixed


def attention(queries, where, order, table, head, pieces, slots, n_chip, state=(), last=True):
    blocks, _, columns = queries.shape
    width = GROUP * HD
    rows = 2 * len(pieces) * QB
    whole = pl.BlockSpec(memory_space=pltpu.VMEM)
    tile = pl.BlockSpec((1, QB, width), lambda b, *_: (b, 0, 0))
    shape = (blocks, QB, width)
    state_shape = jax.ShapeDtypeStruct(shape, jnp.float32)
    done_shape = jax.ShapeDtypeStruct(shape, jnp.bfloat16)
    return pl.pallas_call(
        functools.partial(attention_kernel, n_chip, slots, not state, last),
        out_shape=done_shape if last else (state_shape,) * 3,
        grid_spec=pltpu.PrefetchScalarGridSpec(
            num_scalar_prefetch=3,
            grid=(blocks,),
            in_specs=[pl.BlockSpec((1, QB, width), lambda b, *_: (b, 0, head))]
            + [whole] * len(pieces)
            + [tile] * len(state),
            out_specs=tile if last else (tile,) * 3,
        ),
        compiler_params=pltpu.CompilerParams(vmem_limit_bytes=VMEM_LIMIT),
        cost_estimate=pl.CostEstimate(flops=1, bytes_accessed=1, transcendentals=0),
    )(where, order, table, queries, *pieces, *state)


def row_block(n_outer, which, kv, g):
    if n_outer:
        return g * n_outer + kv + which * (KVH // 2)
    return which * (H // 2) + kv * GROUP + g


def lay_out_kernel(*refs):
    rows = refs[-1]
    width = GROUP * HD
    for at, ref in enumerate(refs[:-1]):
        columns = slice(at // 2 * width, (at // 2 + 1) * width)
        for block in range(2):
            first = (2 * block + at % 2) * QB
            rows[first : first + QB, columns] = ref[block]


def lay_out(parts):
    half = pl.BlockSpec((2, QB, GROUP * HD), lambda i: (0, 0, 0))
    shape = (4 * QB, len(parts) // 2 * GROUP * HD)
    return pl.pallas_call(
        lay_out_kernel,
        out_shape=jax.ShapeDtypeStruct(shape, jnp.bfloat16),
        grid=(1,),
        in_specs=[half] * len(parts),
        out_specs=pl.BlockSpec(shape, lambda i: (0, 0)),
        compiler_params=pltpu.CompilerParams(vmem_limit_bytes=VMEM_LIMIT),
    )(*parts)


def project_kernel(n_outer, groups, steps, where_ref, rows_ref, w_ref, *refs):
    o_ref, wbuf, sems = refs[-3:]
    side = where_ref[1]
    step = pl.program_id(0)
    tile = wbuf.shape[-1]
    tiles = w_ref.shape[-1] // tile
    slots = wbuf.shape[0]

    def fetch(later):
        columns = slice(later % tiles * tile, (later % tiles + 1) * tile)
        for at, (other, kv) in enumerate(groups):
            for g in range(GROUP):
                block = row_block(n_outer, 1 - side if other else side, kv, g)
                to = (at * GROUP + g) * HD
                pltpu.make_async_copy(
                    w_ref.at[later // tiles, pl.ds(pl.multiple_of(block * HD, HD), HD), columns],
                    wbuf.at[later % slots, to : to + HD, :],
                    sems.at[later % slots],
                ).start()

    @pl.when(step == 0)
    def _():
        for later in range(slots - 1):
            fetch(later)

    for later in range(slots - 1, steps):

        @pl.when(step == later - slots + 1)
        def _():
            fetch(later)

    slot = lax.rem(step, slots)
    pltpu.make_async_copy(wbuf.at[slot], wbuf.at[slot], sems.at[slot]).wait()
    total = jnp.dot(rows_ref[...], wbuf[slot], preferred_element_type=jnp.float32)
    if len(refs) > 3:
        total += refs[0][:, pl.ds(pl.multiple_of(step * tile, tile), tile)]
    o_ref[...] = total.astype(o_ref.dtype)


def project(n_outer, where, rows, groups, weights, before=None, tile=PROJECT_TILE):
    parts, _, columns = weights.shape
    steps = parts * columns // tile
    length, depth = rows.shape
    slots = 2 if before is None else min(steps, 4)
    block = pl.BlockSpec((length, tile), lambda s, *_: (0, s))
    dtype = jnp.float32 if before is None else jnp.bfloat16
    return pl.pallas_call(
        functools.partial(project_kernel, n_outer, groups, steps),
        out_shape=jax.ShapeDtypeStruct((length, parts * columns), dtype),
        grid_spec=pltpu.PrefetchScalarGridSpec(
            num_scalar_prefetch=1,
            grid=(steps,),
            in_specs=[
                pl.BlockSpec((length, depth), lambda s, *_: (0, 0)),
                pl.BlockSpec(memory_space=pltpu.HBM),
            ]
            + [pl.BlockSpec(memory_space=pltpu.VMEM)] * (before is not None),
            out_specs=block,
            scratch_shapes=[
                pltpu.VMEM((slots, depth, tile), jnp.bfloat16),
                pltpu.SemaphoreType.DMA((slots,)),
            ],
        ),
        compiler_params=pltpu.CompilerParams(vmem_limit_bytes=VMEM_LIMIT),
        cost_estimate=pl.CostEstimate(flops=1, bytes_accessed=1, transcendentals=0),
    )(where, rows, weights, *([] if before is None else [before]))


LINE = "outer"
PLANE = ("groups", "side", "core")
SEQ = ("outer", "side", "core")


def body(n_groups, n_outer, queries, keys, values, block_table, out_weight):
    n_chip = n_outer * 2
    order_rows = arrivals(n_outer)

    def index(outer, side, core):
        return (outer * 2 + side) * 2 + core

    spots = [(o, s, c) for o in range(n_outer) for s in range(2) for c in range(2)]
    group = lax.axis_index("groups")
    outer, side, core = (lax.axis_index(name) for name in SEQ)
    where = jnp.stack([outer, side, core, side]).astype(jnp.int32)
    where_across = jnp.stack([outer, side, core, 1 - side]).astype(jnp.int32)
    order = jnp.asarray(
        np.array([[p + d for d in row] for p, row in enumerate(order_rows)], np.int32)
    )

    def swap_core(array):
        return lax.ppermute(
            array, SEQ, [(index(o, s, c), index(o, s, 1 - c)) for o, s, c in spots]
        )

    def swap_side(array):
        return lax.ppermute(
            array, SEQ, [(index(o, s, c), index(o, 1 - s, c)) for o, s, c in spots]
        )

    def move(array, hop, way):
        return lax.ppermute(
            array,
            SEQ,
            [
                (index(o, s, c), index(o + way, s, c))
                for o, s, c in spots
                if 0 <= o + way < n_outer and 0 <= o - (hop - 1) * way < n_outer
            ],
        )

    def after(array, *others):
        return lax.optimization_barrier((array, *others))[0]

    def line(array, gates={}, got={}):
        got = {0: array, **got}
        for hop in range(1, n_outer):
            for way in (1, -1):
                if -way * hop in got:
                    continue
                sent = got[-way * (hop - 1)]
                if hop in gates:
                    sent = after(sent, *gates[hop])
                got[-way * hop] = move(sent, hop, way)
        return got

    def pick(got, k):
        wanted = [row[k] for row in order_rows]
        result = got[wanted[0]]
        for offset in sorted(set(wanted[1:])):
            mask = functools.reduce(
                jnp.logical_or, [outer == p for p in range(n_outer) if wanted[p] == offset]
            )
            if offset != wanted[0]:
                result = jnp.where(mask, got[offset], result)
        return result

    def half_of(array, which):
        width = array.shape[-1] // 2
        return lax.dynamic_slice_in_dim(array, which * width, width, array.ndim - 1)

    part = out_weight.shape[1] // n_groups
    columns = lax.dynamic_slice_in_dim(out_weight, group * part, part, 1)
    gathered = lax.all_gather(columns, LINE, axis=0, tiled=True)

    mine = jnp.concatenate([half_of(keys, side), half_of(values, side)], 0)
    theirs = jnp.concatenate([half_of(keys, 1 - side), half_of(values, 1 - side)], 0)
    theirs = swap_side(theirs)

    query_blocks = queries.reshape(2, 2, QB, H * HD)
    far_queries = swap_core(query_blocks[:, 1])
    far_table = swap_core(block_table)
    table = jnp.concatenate([block_table[0::2], far_table[1::2]], 0)
    near_queries = query_blocks[:, 0]

    def my_blocks(which):
        return jnp.concatenate([half_of(near_queries, which), half_of(far_queries, which)], 0)

    across_queries = swap_side(my_blocks(1 - side))
    across_table = swap_side(table)

    chains = [
        jnp.concatenate([half[:, h * HD : (h + 1) * HD] for half in (mine, theirs)], 0)
        for h in range(KVH // 2)
    ]
    gathered = after(gathered, across_queries, across_table, *chains)
    chains = [after(chain, gathered) for chain in chains]
    gathered = lax.all_gather(gathered, PLANE, axis=0, tiled=True)
    held = out_weight.shape[0]
    order_of_rows = n_outer
    if held != HD:
        gathered = gathered.reshape(n_groups, 2, 2, n_outer, held, part)
        gathered = jnp.transpose(gathered, (0, 3, 1, 2, 4, 5))
        order_of_rows = 0
    gathered = gathered.reshape(n_groups, H * HD, part)

    asks = (
        (across_queries, where_across, order, across_table),
        (my_blocks(side), where, order, table),
    )
    last = n_outer - 1
    lines = [line(chain) for chain in chains]
    states = []
    for head, got in enumerate(lines):
        near = [got[0]]
        for k in range(1, last):
            tied = {d: after(got[d], near[-1]) for d in sorted({row[k] for row in order_rows})}
            near.append(pick(tied, k))
        states.append(
            [attention(*ask, head, near, tuple(range(last)), n_chip, last=False) for ask in asks]
        )
    tie = [state[2] for pair in states for state in pair]
    late, across = [], []
    for head, got in enumerate(lines):
        piece = pick({d: after(got[d], *tie) for d in sorted({row[last] for row in order_rows})}, last)
        late.append([piece])
        out = attention(*asks[0], head, late[head], (last,), n_chip, states[head][0])
        tie = [out]
        if head + 1 == KVH // 2:
            out = jnp.concatenate([out[:2], swap_core(out[2:])], 0)
        across.append(swap_side(out))
    def even_and_odd(array):
        return [array, swap_core(array[2:])]

    parts = []
    for head in range(KVH // 2):
        state = [after(array, *tie) for array in states[head][1]]
        near = attention(*asks[1], head, late[head], (last,), n_chip, state)
        parts += [near, swap_core(near[2:])]
    for array in across[:-1]:
        parts += even_and_odd(array)
    groups = [(other, kv) for other in (0, 1) for kv in range(KVH // 2)]
    sums = project(order_of_rows, where, lay_out(parts), groups[:-1], gathered)
    arrived = after(across[-1], sums)
    rows = lay_out([arrived[:2], arrived[2:]])
    return project(order_of_rows, where, rows, groups[-1:], gathered, sums)


def solution(mesh):
    n_groups, n_seq = mesh.shape["groups"], mesh.shape["seq"]
    n_outer = n_seq // 4
    split = Mesh(mesh.devices.reshape(n_groups, n_outer, 2, 2), ("groups", *SEQ))
    rows = P(("groups", *SEQ), None)
    in_specs = (rows, rows, rows, rows, P(SEQ, None))
    run = functools.partial(body, n_groups, n_outer)
    return jax.shard_map(run, mesh=split, in_specs=in_specs, out_specs=rows, check_vma=False)
```

```python
import functools

import jax
import jax.numpy as jnp
import numpy as np
from jax import lax
from jax.experimental import pallas as pl
from jax.experimental.pallas import tpu as pltpu
from jax.sharding import Mesh
from jax.sharding import PartitionSpec as P

H = 16
KVH = 4
HD = 128
QB = 128
ENTRIES = 8
GROUP = H // KVH
SCALE_LOG2 = HD ** (-0.5) * 1.4426950408889634
NT = (((1,), (1,)), ((), ()))
VMEM_LIMIT = 40 * 1024 * 1024
PROJECT_TILE = 1024


def arrivals(n_outer):
    rows = []
    for place in range(n_outer):
        row = [0]
        for hop in range(1, n_outer):
            if place - hop >= 0:
                row.append(-hop)
            if place + hop < n_outer:
                row.append(hop)
        rows.append(row)
    return rows


def attention_kernel(n_chip, slots, first, last, where_ref, order_ref, table_ref, q_ref, *refs):
    pieces, refs = refs[: len(slots)], refs[len(slots) :]
    before, after = ((), refs) if first else (refs[:3], refs[3:])
    count = 2 * len(slots)
    step = pl.program_id(0)
    per_entry = n_chip // ENTRIES
    outer, side, core, asking = where_ref[0], where_ref[1], where_ref[2], where_ref[3]
    turn = jnp.where(step < 2, 0, core) + 2 * n_chip - (outer * 2 + asking)

    starts, usable = [], []
    for at in range(count):
        source_side = side if at < len(slots) else 1 - side
        source = order_ref[outer, slots[at % len(slots)]] * 2 + source_side
        ahead = lax.rem(source + turn, n_chip)
        row = table_ref[step, ahead // per_entry] & 3
        base = 0 if at < len(slots) else 8
        starts.append(pl.multiple_of((base + row) * QB, QB))
        usable.append(lax.rem(ahead, per_entry) == 0)

    def gather(base):
        return jnp.concatenate(
            [pieces[at % len(slots)][pl.ds(start + base, QB), :] for at, start in enumerate(starts)],
            0,
        )

    keys, values = gather(0), gather(4 * QB)

    def spread(column):
        return jnp.broadcast_to(column, (QB, HD))

    scores = []
    for h in range(GROUP):
        s = lax.dot_general(
            q_ref[0, :, h * HD : (h + 1) * HD], keys, NT, preferred_element_type=jnp.float32
        )
        if per_entry > 1:
            s = jnp.concatenate(
                [
                    jnp.where(ok, s[:, at * QB : (at + 1) * QB], -1e30)
                    for at, ok in enumerate(usable)
                ],
                1,
            )
        scores.append(s)
    rounded, totals, factors = [], [], []
    for h, s in enumerate(scores):
        lanes = slice(h * HD, (h + 1) * HD)
        high = spread(jnp.max(s, axis=-1, keepdims=True))
        if not first:
            known = before[1][0, :, lanes]
            high = jnp.maximum(high, known)
            factors.append(jnp.exp2((known - high) * SCALE_LOG2))
        if not last:
            after[1][0, :, lanes] = high
        weights = jnp.exp2((s - jnp.concatenate([high] * count, 1)) * SCALE_LOG2)
        total = spread(jnp.sum(weights, axis=-1, keepdims=True))
        if not first:
            total += before[2][0, :, lanes] * factors[h]
        if not last:
            after[2][0, :, lanes] = total
        totals.append(total)
        rounded.append(weights.astype(jnp.bfloat16))
    for h in range(GROUP):
        lanes = slice(h * HD, (h + 1) * HD)
        mixed = jnp.dot(rounded[h], values, preferred_element_type=jnp.float32)
        if not first:
            mixed += before[0][0, :, lanes] * factors[h]
        if last:
            after[0][0, :, lanes] = (mixed / totals[h]).astype(jnp.bfloat16)
        else:
            after[0][0, :, lanes] = mixed


def attention(queries, where, order, table, head, pieces, slots, n_chip, state=(), last=True):
    blocks, _, columns = queries.shape
    width = GROUP * HD
    rows = 2 * len(pieces) * QB
    whole = pl.BlockSpec(memory_space=pltpu.VMEM)
    tile = pl.BlockSpec((1, QB, width), lambda b, *_: (b, 0, 0))
    shape = (blocks, QB, width)
    state_shape = jax.ShapeDtypeStruct(shape, jnp.float32)
    done_shape = jax.ShapeDtypeStruct(shape, jnp.bfloat16)
    return pl.pallas_call(
        functools.partial(attention_kernel, n_chip, slots, not state, last),
        out_shape=done_shape if last else (state_shape,) * 3,
        grid_spec=pltpu.PrefetchScalarGridSpec(
            num_scalar_prefetch=3,
            grid=(blocks,),
            in_specs=[pl.BlockSpec((1, QB, width), lambda b, *_: (b, 0, head))]
            + [whole] * len(pieces)
            + [tile] * len(state),
            out_specs=tile if last else (tile,) * 3,
        ),
        compiler_params=pltpu.CompilerParams(vmem_limit_bytes=VMEM_LIMIT),
        cost_estimate=pl.CostEstimate(flops=1, bytes_accessed=1, transcendentals=0),
    )(where, order, table, queries, *pieces, *state)


def row_block(n_outer, which, kv, g):
    if n_outer:
        return g * n_outer + kv + which * (KVH // 2)
    return which * (H // 2) + kv * GROUP + g


def lay_out_kernel(*refs):
    rows = refs[-1]
    width = GROUP * HD
    for at, ref in enumerate(refs[:-1]):
        columns = slice(at // 2 * width, (at // 2 + 1) * width)
        for block in range(2):
            first = (2 * block + at % 2) * QB
            rows[first : first + QB, columns] = ref[block]


def lay_out(parts):
    half = pl.BlockSpec((2, QB, GROUP * HD), lambda i: (0, 0, 0))
    shape = (4 * QB, len(parts) // 2 * GROUP * HD)
    return pl.pallas_call(
        lay_out_kernel,
        out_shape=jax.ShapeDtypeStruct(shape, jnp.bfloat16),
        grid=(1,),
        in_specs=[half] * len(parts),
        out_specs=pl.BlockSpec(shape, lambda i: (0, 0)),
        compiler_params=pltpu.CompilerParams(vmem_limit_bytes=VMEM_LIMIT),
    )(*parts)


def project_kernel(n_outer, groups, steps, where_ref, rows_ref, w_ref, *refs):
    o_ref, wbuf, sems = refs[-3:]
    side = where_ref[1]
    step = pl.program_id(0)
    tile = wbuf.shape[-1]
    tiles = w_ref.shape[-1] // tile
    slots = wbuf.shape[0]

    def fetch(later):
        columns = slice(later % tiles * tile, (later % tiles + 1) * tile)
        for at, (other, kv) in enumerate(groups):
            for g in range(GROUP):
                block = row_block(n_outer, 1 - side if other else side, kv, g)
                to = (at * GROUP + g) * HD
                pltpu.make_async_copy(
                    w_ref.at[later // tiles, pl.ds(pl.multiple_of(block * HD, HD), HD), columns],
                    wbuf.at[later % slots, to : to + HD, :],
                    sems.at[later % slots],
                ).start()

    @pl.when(step == 0)
    def _():
        for later in range(slots - 1):
            fetch(later)

    for later in range(slots - 1, steps):

        @pl.when(step == later - slots + 1)
        def _():
            fetch(later)

    slot = lax.rem(step, slots)
    pltpu.make_async_copy(wbuf.at[slot], wbuf.at[slot], sems.at[slot]).wait()
    total = jnp.dot(rows_ref[...], wbuf[slot], preferred_element_type=jnp.float32)
    if len(refs) > 3:
        total += refs[0][:, pl.ds(pl.multiple_of(step * tile, tile), tile)]
    o_ref[...] = total.astype(o_ref.dtype)


def project(n_outer, where, rows, groups, weights, before=None, tile=PROJECT_TILE):
    parts, _, columns = weights.shape
    steps = parts * columns // tile
    length, depth = rows.shape
    slots = 2 if before is None else min(steps, 4)
    block = pl.BlockSpec((length, tile), lambda s, *_: (0, s))
    dtype = jnp.float32 if before is None else jnp.bfloat16
    return pl.pallas_call(
        functools.partial(project_kernel, n_outer, groups, steps),
        out_shape=jax.ShapeDtypeStruct((length, parts * columns), dtype),
        grid_spec=pltpu.PrefetchScalarGridSpec(
            num_scalar_prefetch=1,
            grid=(steps,),
            in_specs=[
                pl.BlockSpec((length, depth), lambda s, *_: (0, 0)),
                pl.BlockSpec(memory_space=pltpu.HBM),
            ]
            + [pl.BlockSpec(memory_space=pltpu.VMEM)] * (before is not None),
            out_specs=block,
            scratch_shapes=[
                pltpu.VMEM((slots, depth, tile), jnp.bfloat16),
                pltpu.SemaphoreType.DMA((slots,)),
            ],
        ),
        compiler_params=pltpu.CompilerParams(vmem_limit_bytes=VMEM_LIMIT),
        cost_estimate=pl.CostEstimate(flops=1, bytes_accessed=1, transcendentals=0),
    )(where, rows, weights, *([] if before is None else [before]))


LINE = "outer"
PLANE = ("groups", "side", "core")
SEQ = ("outer", "side", "core")


def body(n_groups, n_outer, queries, keys, values, block_table, out_weight):
    n_chip = n_outer * 2
    order_rows = arrivals(n_outer)

    def index(outer, side, core):
        return (outer * 2 + side) * 2 + core

    spots = [(o, s, c) for o in range(n_outer) for s in range(2) for c in range(2)]
    group = lax.axis_index("groups")
    outer, side, core = (lax.axis_index(name) for name in SEQ)
    where = jnp.stack([outer, side, core, side]).astype(jnp.int32)
    where_across = jnp.stack([outer, side, core, 1 - side]).astype(jnp.int32)
    order = jnp.asarray(
        np.array([[p + d for d in row] for p, row in enumerate(order_rows)], np.int32)
    )

    def swap_core(array):
        return lax.ppermute(
            array, SEQ, [(index(o, s, c), index(o, s, 1 - c)) for o, s, c in spots]
        )

    def swap_side(array):
        return lax.ppermute(
            array, SEQ, [(index(o, s, c), index(o, 1 - s, c)) for o, s, c in spots]
        )

    def move(array, hop, way):
        return lax.ppermute(
            array,
            SEQ,
            [
                (index(o, s, c), index(o + way, s, c))
                for o, s, c in spots
                if 0 <= o + way < n_outer and 0 <= o - (hop - 1) * way < n_outer
            ],
        )

    def after(array, *others):
        return lax.optimization_barrier((array, *others))[0]

    def line(array, gates={}, got={}):
        got = {0: array, **got}
        for hop in range(1, n_outer):
            for way in (1, -1):
                if -way * hop in got:
                    continue
                sent = got[-way * (hop - 1)]
                if hop in gates:
                    sent = after(sent, *gates[hop])
                got[-way * hop] = move(sent, hop, way)
        return got

    def pick(got, k):
        wanted = [row[k] for row in order_rows]
        result = got[wanted[0]]
        for offset in sorted(set(wanted[1:])):
            mask = functools.reduce(
                jnp.logical_or, [outer == p for p in range(n_outer) if wanted[p] == offset]
            )
            if offset != wanted[0]:
                result = jnp.where(mask, got[offset], result)
        return result

    def half_of(array, which):
        width = array.shape[-1] // 2
        return lax.dynamic_slice_in_dim(array, which * width, width, array.ndim - 1)

    part = out_weight.shape[1] // n_groups
    columns = lax.dynamic_slice_in_dim(out_weight, group * part, part, 1)
    gathered = lax.all_gather(columns, LINE, axis=0, tiled=True)

    mine = jnp.concatenate([half_of(keys, side), half_of(values, side)], 0)
    theirs = jnp.concatenate([half_of(keys, 1 - side), half_of(values, 1 - side)], 0)
    theirs = swap_side(theirs)

    query_blocks = queries.reshape(2, 2, QB, H * HD)
    far_queries = swap_core(query_blocks[:, 1])
    far_table = swap_core(block_table)
    table = jnp.concatenate([block_table[0::2], far_table[1::2]], 0)
    near_queries = query_blocks[:, 0]

    def my_blocks(which):
        return jnp.concatenate([half_of(near_queries, which), half_of(far_queries, which)], 0)

    across_queries = swap_side(my_blocks(1 - side))
    across_table = swap_side(table)

    chains = [
        jnp.concatenate([half[:, h * HD : (h + 1) * HD] for half in (mine, theirs)], 0)
        for h in range(KVH // 2)
    ]
    gathered = after(gathered, across_queries, across_table, *chains)
    chains = [after(chain, gathered) for chain in chains]
    gathered = lax.all_gather(gathered, PLANE, axis=0, tiled=True)
    held = out_weight.shape[0]
    order_of_rows = n_outer
    if held != HD:
        gathered = gathered.reshape(n_groups, 2, 2, n_outer, held, part)
        gathered = jnp.transpose(gathered, (0, 3, 1, 2, 4, 5))
        order_of_rows = 0
    gathered = gathered.reshape(n_groups, H * HD, part)

    asks = (
        (across_queries, where_across, order, across_table),
        (my_blocks(side), where, order, table),
    )
    last = n_outer - 1
    lines = [line(chain) for chain in chains]
    states = []
    for head, got in enumerate(lines):
        near = [got[0]]
        for k in range(1, last):
            tied = {d: after(got[d], near[-1]) for d in sorted({row[k] for row in order_rows})}
            near.append(pick(tied, k))
        states.append(
            [attention(*ask, head, near, tuple(range(last)), n_chip, last=False) for ask in asks]
        )
    tie = [state[2] for pair in states for state in pair]
    late, across = [], []
    for head, got in enumerate(lines):
        piece = pick({d: after(got[d], *tie) for d in sorted({row[last] for row in order_rows})}, last)
        late.append([piece])
        out = attention(*asks[0], head, late[head], (last,), n_chip, states[head][0])
        tie = [out]
        out = jnp.concatenate([out[:2], swap_core(out[2:])], 0)
        across.append(swap_side(out))
    parts = []
    for head in range(KVH // 2):
        state = [after(array, *tie) for array in states[head][1]]
        near = attention(*asks[1], head, late[head], (last,), n_chip, state)
        parts += [near, swap_core(near[2:])]
    own = [(0, kv) for kv in range(KVH // 2)]
    other = [(1, kv) for kv in range(KVH // 2)]
    sums = project(order_of_rows, where, lay_out(parts), own, gathered)
    arrived = [after(array, sums) for array in across]
    rows = lay_out([blocks for array in arrived for blocks in (array[:2], array[2:])])
    return project(order_of_rows, where, rows, other, gathered, sums)


def solution(mesh):
    n_groups, n_seq = mesh.shape["groups"], mesh.shape["seq"]
    n_outer = n_seq // 4
    split = Mesh(mesh.devices.reshape(n_groups, n_outer, 2, 2), ("groups", *SEQ))
    rows = P(("groups", *SEQ), None)
    in_specs = (rows, rows, rows, rows, P(SEQ, None))
    run = functools.partial(body, n_groups, n_outer)
    return jax.shard_map(run, mesh=split, in_specs=in_specs, out_specs=rows, check_vma=False)
```

```python
import functools

import jax
import jax.numpy as jnp
import numpy as np
from jax import lax
from jax.experimental import pallas as pl
from jax.experimental.pallas import tpu as pltpu
from jax.sharding import Mesh
from jax.sharding import PartitionSpec as P

H = 16
KVH = 4
HD = 128
QB = 128
ENTRIES = 8
GROUP = H // KVH
SCALE_LOG2 = HD ** (-0.5) * 1.4426950408889634
NT = (((1,), (1,)), ((), ()))
VMEM_LIMIT = 40 * 1024 * 1024
PROJECT_TILE = 1024


def arrivals(n_outer):
    rows = []
    for place in range(n_outer):
        row = [0]
        for hop in range(1, n_outer):
            if place - hop >= 0:
                row.append(-hop)
            if place + hop < n_outer:
                row.append(hop)
        rows.append(row)
    return rows


def attention_kernel(n_chip, slots, first, last, where_ref, order_ref, table_ref, q_ref, *refs):
    pieces, refs = refs[: len(slots)], refs[len(slots) :]
    before, after = ((), refs) if first else (refs[:3], refs[3:])
    count = 2 * len(slots)
    step = pl.program_id(0)
    per_entry = n_chip // ENTRIES
    outer, side, core, asking = where_ref[0], where_ref[1], where_ref[2], where_ref[3]
    turn = jnp.where(step < 2, 0, core) + 2 * n_chip - (outer * 2 + asking)

    starts, usable = [], []
    for at in range(count):
        source_side = side if at < len(slots) else 1 - side
        source = order_ref[outer, slots[at % len(slots)]] * 2 + source_side
        ahead = lax.rem(source + turn, n_chip)
        row = table_ref[step, ahead // per_entry] & 3
        base = 0 if at < len(slots) else 8
        starts.append(pl.multiple_of((base + row) * QB, QB))
        usable.append(lax.rem(ahead, per_entry) == 0)

    def gather(base):
        return jnp.concatenate(
            [pieces[at % len(slots)][pl.ds(start + base, QB), :] for at, start in enumerate(starts)],
            0,
        )

    keys, values = gather(0), gather(4 * QB)

    def spread(column):
        return jnp.broadcast_to(column, (QB, HD))

    scores = []
    for h in range(GROUP):
        s = lax.dot_general(
            q_ref[0, :, h * HD : (h + 1) * HD], keys, NT, preferred_element_type=jnp.float32
        )
        if per_entry > 1:
            s = jnp.concatenate(
                [
                    jnp.where(ok, s[:, at * QB : (at + 1) * QB], -1e30)
                    for at, ok in enumerate(usable)
                ],
                1,
            )
        scores.append(s)
    rounded, totals, factors = [], [], []
    for h, s in enumerate(scores):
        lanes = slice(h * HD, (h + 1) * HD)
        high = spread(jnp.max(s, axis=-1, keepdims=True))
        if not first:
            known = before[1][0, :, lanes]
            high = jnp.maximum(high, known)
            factors.append(jnp.exp2((known - high) * SCALE_LOG2))
        if not last:
            after[1][0, :, lanes] = high
        weights = jnp.exp2((s - jnp.concatenate([high] * count, 1)) * SCALE_LOG2)
        total = spread(jnp.sum(weights, axis=-1, keepdims=True))
        if not first:
            total += before[2][0, :, lanes] * factors[h]
        if not last:
            after[2][0, :, lanes] = total
        totals.append(total)
        rounded.append(weights.astype(jnp.bfloat16))
    for h in range(GROUP):
        lanes = slice(h * HD, (h + 1) * HD)
        mixed = jnp.dot(rounded[h], values, preferred_element_type=jnp.float32)
        if not first:
            mixed += before[0][0, :, lanes] * factors[h]
        if last:
            after[0][0, :, lanes] = (mixed / totals[h]).astype(jnp.bfloat16)
        else:
            after[0][0, :, lanes] = mixed


def attention(queries, where, order, table, head, pieces, slots, n_chip, state=(), last=True):
    blocks, _, columns = queries.shape
    width = GROUP * HD
    rows = 2 * len(pieces) * QB
    whole = pl.BlockSpec(memory_space=pltpu.VMEM)
    tile = pl.BlockSpec((1, QB, width), lambda b, *_: (b, 0, 0))
    shape = (blocks, QB, width)
    state_shape = jax.ShapeDtypeStruct(shape, jnp.float32)
    done_shape = jax.ShapeDtypeStruct(shape, jnp.bfloat16)
    return pl.pallas_call(
        functools.partial(attention_kernel, n_chip, slots, not state, last),
        out_shape=done_shape if last else (state_shape,) * 3,
        grid_spec=pltpu.PrefetchScalarGridSpec(
            num_scalar_prefetch=3,
            grid=(blocks,),
            in_specs=[pl.BlockSpec((1, QB, width), lambda b, *_: (b, 0, head))]
            + [whole] * len(pieces)
            + [tile] * len(state),
            out_specs=tile if last else (tile,) * 3,
        ),
        compiler_params=pltpu.CompilerParams(vmem_limit_bytes=VMEM_LIMIT),
        cost_estimate=pl.CostEstimate(flops=1, bytes_accessed=1, transcendentals=0),
    )(where, order, table, queries, *pieces, *state)


def row_block(n_outer, which, kv, g):
    if n_outer:
        return g * n_outer + kv + which * (KVH // 2)
    return which * (H // 2) + kv * GROUP + g


def lay_out_kernel(*refs):
    rows = refs[-1]
    width = GROUP * HD
    for at, ref in enumerate(refs[:-1]):
        columns = slice(at // 2 * width, (at // 2 + 1) * width)
        for block in range(2):
            first = (2 * block + at % 2) * QB
            rows[first : first + QB, columns] = ref[block]


def lay_out(parts):
    half = pl.BlockSpec((2, QB, GROUP * HD), lambda i: (0, 0, 0))
    shape = (4 * QB, len(parts) // 2 * GROUP * HD)
    return pl.pallas_call(
        lay_out_kernel,
        out_shape=jax.ShapeDtypeStruct(shape, jnp.bfloat16),
        grid=(1,),
        in_specs=[half] * len(parts),
        out_specs=pl.BlockSpec(shape, lambda i: (0, 0)),
        compiler_params=pltpu.CompilerParams(vmem_limit_bytes=VMEM_LIMIT),
    )(*parts)


def project_kernel(n_outer, groups, steps, where_ref, rows_ref, w_ref, *refs):
    o_ref, wbuf, sems = refs[-3:]
    side = where_ref[1]
    step = pl.program_id(0)
    tile = wbuf.shape[-1]
    tiles = w_ref.shape[-1] // tile
    slots = wbuf.shape[0]

    def fetch(later):
        columns = slice(later % tiles * tile, (later % tiles + 1) * tile)
        for at, (other, kv) in enumerate(groups):
            for g in range(GROUP):
                block = row_block(n_outer, 1 - side if other else side, kv, g)
                to = (at * GROUP + g) * HD
                pltpu.make_async_copy(
                    w_ref.at[later // tiles, pl.ds(pl.multiple_of(block * HD, HD), HD), columns],
                    wbuf.at[later % slots, to : to + HD, :],
                    sems.at[later % slots],
                ).start()

    @pl.when(step == 0)
    def _():
        for later in range(slots - 1):
            fetch(later)

    for later in range(slots - 1, steps):

        @pl.when(step == later - slots + 1)
        def _():
            fetch(later)

    slot = lax.rem(step, slots)
    pltpu.make_async_copy(wbuf.at[slot], wbuf.at[slot], sems.at[slot]).wait()
    total = jnp.dot(rows_ref[...], wbuf[slot], preferred_element_type=jnp.float32)
    if len(refs) > 3:
        total += refs[0][:, pl.ds(pl.multiple_of(step * tile, tile), tile)]
    o_ref[...] = total.astype(o_ref.dtype)


def project(n_outer, where, rows, groups, weights, before=None, tile=PROJECT_TILE):
    parts, _, columns = weights.shape
    steps = parts * columns // tile
    length, depth = rows.shape
    slots = 2 if before is None else min(steps, 4)
    block = pl.BlockSpec((length, tile), lambda s, *_: (0, s))
    dtype = jnp.float32 if before is None else jnp.bfloat16
    return pl.pallas_call(
        functools.partial(project_kernel, n_outer, groups, steps),
        out_shape=jax.ShapeDtypeStruct((length, parts * columns), dtype),
        grid_spec=pltpu.PrefetchScalarGridSpec(
            num_scalar_prefetch=1,
            grid=(steps,),
            in_specs=[
                pl.BlockSpec((length, depth), lambda s, *_: (0, 0)),
                pl.BlockSpec(memory_space=pltpu.HBM),
            ]
            + [pl.BlockSpec(memory_space=pltpu.VMEM)] * (before is not None),
            out_specs=block,
            scratch_shapes=[
                pltpu.VMEM((slots, depth, tile), jnp.bfloat16),
                pltpu.SemaphoreType.DMA((slots,)),
            ],
        ),
        compiler_params=pltpu.CompilerParams(vmem_limit_bytes=VMEM_LIMIT),
        cost_estimate=pl.CostEstimate(flops=1, bytes_accessed=1, transcendentals=0),
    )(where, rows, weights, *([] if before is None else [before]))


LINE = "outer"
PLANE = ("groups", "side", "core")
SEQ = ("outer", "side", "core")


def body(n_groups, n_outer, queries, keys, values, block_table, out_weight):
    n_chip = n_outer * 2
    order_rows = arrivals(n_outer)

    def index(outer, side, core):
        return (outer * 2 + side) * 2 + core

    spots = [(o, s, c) for o in range(n_outer) for s in range(2) for c in range(2)]
    group = lax.axis_index("groups")
    outer, side, core = (lax.axis_index(name) for name in SEQ)
    where = jnp.stack([outer, side, core, side]).astype(jnp.int32)
    where_across = jnp.stack([outer, side, core, 1 - side]).astype(jnp.int32)
    order = jnp.asarray(
        np.array([[p + d for d in row] for p, row in enumerate(order_rows)], np.int32)
    )

    def swap_core(array):
        return lax.ppermute(
            array, SEQ, [(index(o, s, c), index(o, s, 1 - c)) for o, s, c in spots]
        )

    def swap_side(array):
        return lax.ppermute(
            array, SEQ, [(index(o, s, c), index(o, 1 - s, c)) for o, s, c in spots]
        )

    def move(array, hop, way):
        return lax.ppermute(
            array,
            SEQ,
            [
                (index(o, s, c), index(o + way, s, c))
                for o, s, c in spots
                if 0 <= o + way < n_outer and 0 <= o - (hop - 1) * way < n_outer
            ],
        )

    def after(array, *others):
        return lax.optimization_barrier((array, *others))[0]

    def line(array, gates={}, got={}):
        got = {0: array, **got}
        for hop in range(1, n_outer):
            for way in (1, -1):
                if -way * hop in got:
                    continue
                sent = got[-way * (hop - 1)]
                if hop in gates:
                    sent = after(sent, *gates[hop])
                got[-way * hop] = move(sent, hop, way)
        return got

    def pick(got, k):
        wanted = [row[k] for row in order_rows]
        result = got[wanted[0]]
        for offset in sorted(set(wanted[1:])):
            mask = functools.reduce(
                jnp.logical_or, [outer == p for p in range(n_outer) if wanted[p] == offset]
            )
            if offset != wanted[0]:
                result = jnp.where(mask, got[offset], result)
        return result

    def half_of(array, which):
        width = array.shape[-1] // 2
        return lax.dynamic_slice_in_dim(array, which * width, width, array.ndim - 1)

    part = out_weight.shape[1] // n_groups
    columns = lax.dynamic_slice_in_dim(out_weight, group * part, part, 1)
    gathered = lax.all_gather(columns, LINE, axis=0, tiled=True)

    mine = jnp.concatenate([half_of(keys, side), half_of(values, side)], 0)
    theirs = jnp.concatenate([half_of(keys, 1 - side), half_of(values, 1 - side)], 0)
    theirs = swap_side(theirs)

    query_blocks = queries.reshape(2, 2, QB, H * HD)
    far_queries = swap_core(query_blocks[:, 1])
    far_table = swap_core(block_table)
    table = jnp.concatenate([block_table[0::2], far_table[1::2]], 0)
    near_queries = query_blocks[:, 0]

    def my_blocks(which):
        return jnp.concatenate([half_of(near_queries, which), half_of(far_queries, which)], 0)

    across_queries = swap_side(my_blocks(1 - side))
    across_table = swap_side(table)

    chains = [
        jnp.concatenate([half[:, h * HD : (h + 1) * HD] for half in (mine, theirs)], 0)
        for h in range(KVH // 2)
    ]
    gathered = after(gathered, across_queries, across_table, *chains)
    chains = [after(chain, gathered) for chain in chains]
    gathered = lax.all_gather(gathered, PLANE, axis=0, tiled=True)
    held = out_weight.shape[0]
    order_of_rows = n_outer
    if held != HD:
        gathered = gathered.reshape(n_groups, 2, 2, n_outer, held, part)
        gathered = jnp.transpose(gathered, (0, 3, 1, 2, 4, 5))
        order_of_rows = 0
    gathered = gathered.reshape(n_groups, H * HD, part)

    asks = (
        (across_queries, where_across, order, across_table),
        (my_blocks(side), where, order, table),
    )
    last = n_outer - 1
    lines = [line(chain) for chain in chains]
    states = []
    for head, got in enumerate(lines):
        near = [got[0]]
        for k in range(1, last):
            tied = {d: after(got[d], near[-1]) for d in sorted({row[k] for row in order_rows})}
            near.append(pick(tied, k))
        states.append(
            [attention(*ask, head, near, tuple(range(last)), n_chip, last=False) for ask in asks]
        )
    tie = [state[2] for pair in states for state in pair]
    late, across = [], []
    for head, got in enumerate(lines):
        piece = pick({d: after(got[d], *tie) for d in sorted({row[last] for row in order_rows})}, last)
        late.append([piece])
        out = attention(*asks[0], head, late[head], (last,), n_chip, states[head][0])
        tie = [out]
        out = jnp.concatenate([out[:2], swap_core(out[2:])], 0)
        across.append(swap_side(out))
    def even_and_odd(array):
        return [array[:2], array[2:]]

    parts = []
    for head in range(KVH // 2):
        state = [after(array, *tie) for array in states[head][1]]
        near = attention(*asks[1], head, late[head], (last,), n_chip, state)
        parts += [near, swap_core(near[2:])]
    for array in across[:-1]:
        parts += even_and_odd(array)
    groups = [(other, kv) for other in (0, 1) for kv in range(KVH // 2)]
    sums = project(order_of_rows, where, lay_out(parts), groups[:-1], gathered)
    arrived = after(across[-1], sums)
    rows = lay_out([arrived[:2], arrived[2:]])
    return project(order_of_rows, where, rows, groups[-1:], gathered, sums)


def solution(mesh):
    n_groups, n_seq = mesh.shape["groups"], mesh.shape["seq"]
    n_outer = n_seq // 4
    split = Mesh(mesh.devices.reshape(n_groups, n_outer, 2, 2), ("groups", *SEQ))
    rows = P(("groups", *SEQ), None)
    in_specs = (rows, rows, rows, rows, P(SEQ, None))
    run = functools.partial(body, n_groups, n_outer)
    return jax.shard_map(run, mesh=split, in_specs=in_specs, out_specs=rows, check_vma=False)
```
